32 devices in a mesh: frame: 16 (over z, y, core), state: 2 (over x).
Axes of the slice: x: 2, y: 2, z: 4, core: 2. Of those that a mesh axis runs over, the one named last changes fastest.
Arguments:
- object_slices: float32 [2, 2, 4096, 512], P(None, None, 'frame'), may hold values from -4 to 4
- probe: float32 [2, 2, 256, 256], P('state'), may hold values from -4 to 4
- amplitude: float32 [16, 256, 256], P('frame'), may hold values from 0.5 to 4
- positions: int32 [16, 2], P('frame'), may hold values from 0 to 256, as said below
- propagator: float32 [256, 256], replicated, may hold values from -3.140625 to 3.140625
Outputs:
- gradient: float32 [2, 2, 4096, 512], P(None, None, ('frame', 'state'))
The draws below stay inside these ranges and needn't reach their ends.
Inputs may be any that keep to these rules, and one draw needn't show every extreme that they name: positions[f, 0] is the row offset of frame f's patch within the rows owned by its owner f, from 0 to 255; positions[f, 1] is its column offset, from 0 to 256.
All inputs are finite; a program needn't handle non-finite values.
Results may differ from the reference program's by a relative error of at most 0.0001.
Values sent between devices are 32-bit elements; how exact they have to be, the bound alone decides.
No kernel may reach another device: no remote copies, remote signals or barrier semaphores. Data moves between devices by JAX's collectives and lax.ppermute only.
A program may use at most 64 MiB of HBM per device.

```python
import math
import jax
import jax.numpy as jnp
from jax import lax

P_SIZE = 256
F_DEV = 1
TILE = 256
OBJ_COLS = 512
STATES = 2
FRAMES = 16
OBJ_ROWS = 4096


def draw_positions(key, part):
    row_key = jax.random.fold_in(key, 11)
    col_key = jax.random.fold_in(key, 23)
    rows_drawn = jax.random.randint(row_key, (FRAMES, 1), 0, TILE, dtype=jnp.int32)
    cols_drawn = jax.random.randint(col_key, (FRAMES, 1), 0, OBJ_COLS - P_SIZE + 1, dtype=jnp.int32)
    return jnp.concatenate([rows_drawn, cols_drawn], axis=1)


def shard_levels(stream_key, dims, shards, low, top_value):
    gain = 1.0
    for dim, blocks in shards:
        draws = jax.random.uniform(jax.random.fold_in(jax.random.fold_in(stream_key, 6), dim), (blocks,), jnp.float32, low / len(shards), top_value / len(shards))
        gain = gain * jnp.repeat(jnp.exp(draws), dims[dim] // blocks).reshape((-1,) + (1,) * (len(dims) - 1 - dim))
    return gain


def normal_values(stream_key, extent, spread, reach, shards=(), held_as=jnp.bfloat16):
    result = jax.random.normal(stream_key, extent, jnp.float32) * spread
    if len(shards) > 0:
        result = shard_levels(stream_key, extent, shards, -0.22, 0.18) * result
    return jnp.clip(result, min=-reach, max=reach).astype(held_as)


def setup_inputs(seed: int = 0) -> dict:
    key_of = jax.random.split(jax.random.key(seed), 6)
    return {
        "object_slices": normal_values(key_of[0], (2, 2, OBJ_ROWS, OBJ_COLS), 0.7, 4.0, ((2, 16),), jnp.float32),
        "probe": normal_values(key_of[1], (STATES, 2, P_SIZE, P_SIZE), 0.5, 4.0, ((0, 2),), jnp.float32),
        "amplitude": jnp.clip(jnp.exp(math.log(4.0) - 2.0794415 * jax.random.uniform(key_of[2], (FRAMES, P_SIZE, P_SIZE), jnp.float32) ** shard_levels(key_of[2], (FRAMES, P_SIZE, P_SIZE), ((0, 16),), -0.2, 0.2)), 0.5, 4.0),
        "positions": draw_positions(jax.random.fold_in(key_of[5], 71), 0),
        "propagator": jnp.clip(jax.random.uniform(key_of[4], (P_SIZE, P_SIZE), jnp.float32, -3.140625, 3.140625), -3.140625, 3.140625),
    }


def reference(object_slices, probe, amplitude, positions, propagator):
    rows_all = object_slices.shape[2]
    pixels = amplitude.shape[1]
    padded = jnp.concatenate([object_slices, object_slices[:, :, :pixels]], axis=2)
    field = padded[:, 0] + 1j * padded[:, 1]
    kernel = jnp.cos(propagator) + 1j * jnp.sin(propagator)
    modes = probe[:, 0] + 1j * probe[:, 1]
    owners = jnp.arange(FRAMES, dtype=jnp.int32) // F_DEV * TILE
    row_starts = (owners + positions[:, 0]).astype(jnp.int32)
    col_starts = positions[:, 1].astype(jnp.int32)

    def forward(values):
        return jnp.fft.fft2(values, axes=(-2, -1), norm='ortho')

    def inverse(values):
        return jnp.fft.ifft2(values, axes=(-2, -1), norm='ortho')

    def step(summed, inputs):
        row_at, col_at, measured = inputs
        zero_at = jnp.zeros((), jnp.int32)
        corner = (zero_at, row_at, col_at)
        patch = lax.dynamic_slice(field, corner, (2, pixels, pixels))
        wave = modes * patch[0]
        inner = inverse(kernel * forward(wave))
        far = forward(patch[1] * inner)
        intensity = lax.optimization_barrier(jnp.sum(jnp.real(far) ** 2 + jnp.imag(far) ** 2, axis=0))
        factor = 1.0 - measured / jnp.sqrt(intensity + 1.0)
        back = inverse(factor * far)
        second = lax.optimization_barrier(jnp.sum(jnp.conj(inner) * back, axis=0))
        chi = jnp.conj(patch[1]) * back
        front = inverse(jnp.conj(kernel) * forward(chi))
        first = lax.optimization_barrier(jnp.sum(jnp.conj(modes) * front, axis=0))
        present = lax.dynamic_slice(summed, corner, (2, pixels, pixels))
        summed = lax.dynamic_update_slice(summed, present + jnp.stack([first, second]), corner)
        return (summed, None)
    start = jnp.zeros(field.shape, field.dtype)
    summed, unused = lax.scan(step, start, (row_starts, col_starts, amplitude))
    folded = summed[:, :rows_all]
    folded = folded.at[:, :pixels].add(summed[:, rows_all:])
    return jnp.stack([jnp.real(folded), jnp.imag(folded)], axis=1)
```

```python
import functools
import math

import jax
import jax.numpy as jnp
import numpy as np
from jax import lax
from jax.experimental import pallas as pl
from jax.experimental.pallas import tpu as pltpu
from jax.sharding import PartitionSpec as P

F32 = jnp.float32
BF16 = jnp.bfloat16
VMEM = pl.BlockSpec(memory_space=pltpu.VMEM)
SMEM = pl.BlockSpec(memory_space=pltpu.SMEM)
LIMIT = 24 * 1024 * 1024


def shifted(value, axis, by):
    count = lax.axis_size(axis)
    return lax.ppermute(value, axis, [(i, (i + by) % count) for i in range(count)])


def call(body, outs, ins, scratch=(), flops=0, moved=0):
    return pl.pallas_call(
        body,
        out_shape=[jax.ShapeDtypeStruct(shape, F32) for shape in outs],
        in_specs=ins,
        out_specs=[VMEM] * len(outs),
        scratch_shapes=list(scratch),
        compiler_params=pltpu.CompilerParams(vmem_limit_bytes=LIMIT),
        cost_estimate=pl.CostEstimate(flops=flops, bytes_accessed=moved, transcendentals=0),
    )


def tables(length):
    half = length // 2
    n = np.arange(half)[:, None]
    forms = []
    for parity in (0, 1):
        k = 2 * np.arange(half)[None, :] + parity
        angle = -2.0 * math.pi * ((n * k) % length) / length
        re, im = np.cos(angle) / math.sqrt(length), np.sin(angle) / math.sqrt(length)
        right = np.block([[re, im], [-im, re]])
        forms += [right, right.T]
    stack = np.stack(forms).astype(np.float64)
    top = stack.astype(BF16)
    rest = (stack - top.astype(np.float64)).astype(BF16)
    return jnp.asarray(np.stack([top, rest]))


def halves(value):
    top = value.astype(BF16)
    return top, (value - top.astype(F32)).astype(BF16)


def dot(a, b):
    return lax.dot_general(a, b, (((1,), (0,)), ((), ())), preferred_element_type=F32)


def times_table(value, tab, which):
    top, rest = halves(value)
    return dot(top, tab[0, which]) + (dot(rest, tab[0, which]) + dot(top, tab[1, which]))


def table_times(value, tab, which):
    top, rest = halves(value)
    return dot(tab[0, which], top) + (dot(tab[0, which], rest) + dot(tab[1, which], top))


def columns_forward(re, im, tab):
    h = re.shape[1] // 2
    r0, r1, i0, i1 = re[:, :h], re[:, h:], im[:, :h], im[:, h:]
    even = times_table(jnp.concatenate([r0 + r1, i0 + i1], 1), tab, 0)
    odd = times_table(jnp.concatenate([r0 - r1, i0 - i1], 1), tab, 2)
    return (
        jnp.concatenate([even[:, :h], odd[:, :h]], 1),
        jnp.concatenate([even[:, h:], odd[:, h:]], 1),
    )


def columns_inverse(re, im, tab):
    h = re.shape[1] // 2
    even = times_table(jnp.concatenate([re[:, :h], im[:, :h]], 1), tab, 1)
    odd = times_table(jnp.concatenate([re[:, h:], im[:, h:]], 1), tab, 3)
    total, gap = even + odd, even - odd
    return (
        jnp.concatenate([total[:, :h], gap[:, :h]], 1),
        jnp.concatenate([total[:, h:], gap[:, h:]], 1),
    )


def rows_forward(re, im, tab):
    h = re.shape[0] // 2
    r0, r1, i0, i1 = re[:h], re[h:], im[:h], im[h:]
    even = table_times(jnp.concatenate([r0 + r1, i0 + i1], 0), tab, 1)
    odd = table_times(jnp.concatenate([r0 - r1, i0 - i1], 0), tab, 3)
    return (
        jnp.concatenate([even[:h], odd[:h]], 0),
        jnp.concatenate([even[h:], odd[h:]], 0),
    )


def rows_inverse(re, im, tab):
    h = re.shape[0] // 2
    even = table_times(jnp.concatenate([re[:h], im[:h]], 0), tab, 0)
    odd = table_times(jnp.concatenate([re[h:], im[h:]], 0), tab, 2)
    total, gap = even + odd, even - odd
    return (
        jnp.concatenate([total[:h], gap[:h]], 0),
        jnp.concatenate([total[h:], gap[h:]], 0),
    )


def forward(re, im, tab):
    return rows_forward(*columns_forward(re, im, tab), tab)


def inverse(re, im, tab):
    return columns_inverse(*rows_inverse(re, im, tab), tab)


def thirds(value):
    top = value.astype(BF16)
    left = value - top.astype(F32)
    mid = left.astype(BF16)
    return top, mid, (left - mid.astype(F32)).astype(BF16)


def by_parity(value):
    size = value.shape[0]
    h = size // 2
    picks = []
    for along in (0, 1):
        place = lax.broadcasted_iota(jnp.int32, (size, size), along)
        source = lax.broadcasted_iota(jnp.int32, (size, size), 1 - along)
        wanted = jnp.where(place < h, 2 * place, 2 * (place - h) + 1)
        picks.append(jnp.where(source == wanted, 1.0, 0.0).astype(BF16))
    top, mid, low = thirds(value)
    value = (dot(picks[0], top) + dot(picks[0], mid)) + dot(picks[0], low)
    top, mid, low = thirds(value)
    return (dot(top, picks[1]) + dot(mid, picks[1])) + dot(low, picks[1])


def prepare_body(prop_ref, amp_ref, wave_re, wave_im, amp_out):
    phase = by_parity(prop_ref[...])
    wave_re[...] = jnp.cos(phase)
    wave_im[...] = jnp.sin(phase)
    amp_out[...] = by_parity(amp_ref[0])


def turn_body(pos_ref, probe_ref, out_ref):
    size = probe_ref.shape[-1]
    row, col = pos_ref[0, 0], lax.rem(pos_ref[0, 1], size)
    for m in range(probe_ref.shape[0]):
        for c in range(2):
            out_ref[m, c] = pltpu.roll(pltpu.roll(probe_ref[m, c], row, 0), col, 1)


def patch_of(own_ref, halo_ref, row, col):
    size = halo_ref.shape[-1]
    r = lax.broadcasted_iota(jnp.int32, (size, size), 0)
    c = lax.broadcasted_iota(jnp.int32, (size, size), 1)
    parts = []
    for part in range(2):
        own = jnp.where(c < col, own_ref[0, part, :, size:], own_ref[0, part, :, :size])
        parts.append(jnp.where(r < row, halo_ref[part], own))
    return parts


def inner_body(kept, count, pos_ref, own_ref, halo_ref, probe_ref, kr_ref, ki_ref, tab, *refs):
    before = refs[:-2]
    out_ref, patch = refs[-2:]
    for ref in before:
        out_ref[:kept] = ref[...]
    re, im = patch_of(own_ref, halo_ref, pos_ref[0, 0], pos_ref[0, 1])
    patch[0] = re
    patch[1] = im

    def state(m, carry):
        pr, pi = probe_ref[m, 0], probe_ref[m, 1]
        ar, ai = patch[0], patch[1]
        wr, wi = forward(pr * ar - pi * ai, pr * ai + pi * ar, tab)
        kr, ki = kr_ref[...], ki_ref[...]
        ir, ii = inverse(kr * wr - ki * wi, kr * wi + ki * wr, tab)
        out_ref[kept + m, 0] = ir
        out_ref[kept + m, 1] = ii
        return carry

    lax.fori_loop(0, count, state, 0)


def middle_body(rows, pos_ref, own_ref, halo_ref, inner_ref, amp_ref, tab, term_ref, chi_ref, patch, far, power):
    states = inner_ref.shape[0]
    re, im = patch_of(own_ref, halo_ref, pos_ref[0, 0], pos_ref[0, 1])
    patch[0] = re
    patch[1] = im
    power[...] = jnp.zeros_like(power)

    def outward(m, carry):
        br, bi = patch[0], patch[1]
        ir, ii = inner_ref[m, 0], inner_ref[m, 1]
        fr, fi = forward(br * ir - bi * ii, br * ii + bi * ir, tab)
        far[m, 0] = fr
        far[m, 1] = fi
        power[...] += fr * fr + fi * fi
        return carry

    lax.fori_loop(0, states, outward, 0)
    power[...] = 1.0 - amp_ref[...] / jnp.sqrt(power[...] + 1.0)
    term_ref[...] = jnp.zeros_like(term_ref)
    start = pl.multiple_of(pos_ref[0, 2] * rows, rows)

    def homeward(m, carry):
        factor = power[...]
        kr, ki = inverse(factor * far[m, 0], factor * far[m, 1], tab)
        far[m, 0] = kr
        far[m, 1] = ki
        br, bi = patch[0], patch[1]
        chi_ref[m, 0] = br * kr + bi * ki
        chi_ref[m, 1] = br * ki - bi * kr
        take = pl.ds(start, rows)
        ir, ii = inner_ref[m, 0, take], inner_ref[m, 1, take]
        kr, ki = far[m, 0, take], far[m, 1, take]
        term_ref[0] += ir * kr + ii * ki
        term_ref[1] += ir * ki - ii * kr
        return carry

    lax.fori_loop(0, states, homeward, 0)


def last_body(rows, pos_ref, chi_ref, first_ref, rest_ref, kr_ref, ki_ref, tab, term_ref, front):
    term_ref[...] = jnp.zeros_like(term_ref)
    start = pl.multiple_of(pos_ref[0, 2] * rows, rows)
    take = pl.ds(start, rows)

    def state(m, carry):
        wr, wi = forward(chi_ref[m, 0], chi_ref[m, 1], tab)
        kr, ki = kr_ref[...], ki_ref[...]
        ur, ui = rows_inverse(kr * wr + ki * wi, kr * wi - ki * wr, tab)
        front[0] = ur
        front[1] = ui
        fr, fi = columns_inverse(front[0, take], front[1, take], tab)
        own = m == 0
        at = jnp.maximum(m - 1, 0)
        pr = jnp.where(own, first_ref[0, 0, take], rest_ref[at, 0, take])
        pi = jnp.where(own, first_ref[0, 1, take], rest_ref[at, 1, take])
        term_ref[0] += pr * fr + pi * fi
        term_ref[1] += pr * fi - pi * fr
        return carry

    lax.fori_loop(0, chi_ref.shape[0], state, 0)


def gather_body(rows, pos_ref, zero_ref, zero_in, one_ref, one_in, out_ref):
    size = zero_ref.shape[-1]
    start = pos_ref[0, 2] * rows
    r = lax.broadcasted_iota(jnp.int32, (rows, size), 0) + start
    c = lax.broadcasted_iota(jnp.int32, (rows, size), 1)
    here, there = r >= pos_ref[0, 0], r < pos_ref[0, 3]
    here_right, there_right = c < pos_ref[0, 1], c < pos_ref[0, 4]
    for s, (own, came) in enumerate(((zero_ref, zero_in), (one_ref, one_in))):
        for part in range(2):
            mine = jnp.where(here, own[part], 0.0)
            theirs = jnp.where(there, came[part], 0.0)
            out_ref[s, part, :, :size] = jnp.where(here_right, 0.0, mine) + jnp.where(there_right, 0.0, theirs)
            out_ref[s, part, :, size:] = jnp.where(here_right, mine, 0.0) + jnp.where(there_right, theirs, 0.0)


def on_device(object_slices, probe, amplitude, positions, propagator):
    states = lax.axis_size("state")
    size = amplitude.shape[1]
    rows = object_slices.shape[2] // states
    assert object_slices.shape[2:] == (size, 2 * size) and positions.shape[0] == 1
    before = shifted(positions, "frame", 1)
    others = [shifted(probe, "state", by) for by in range(1, states)]
    rest = others[0] if states == 2 else jnp.concatenate(others, 0)
    tab = tables(size)
    flops = 24 * size**3
    share = states - 1

    column = lax.broadcasted_iota(jnp.int32, (2, size, size), 2)
    halos = []
    for s in range(2):
        picked = jnp.where(column < before[0, 1], object_slices[s, :, :, size:], object_slices[s, :, :, :size])
        halos.append(shifted(picked, "frame", -1))
    index = lax.axis_index("state").astype(jnp.int32)
    where = jnp.concatenate([positions, index[None, None], before], 1)

    grid = (size, size)
    kr, ki, amp = call(prepare_body, [grid] * 3, [VMEM] * 2, flops=2 * size**3, moved=20 * size**2)(propagator, amplitude)
    (first,) = call(turn_body, [probe.shape], [SMEM, VMEM], moved=16 * size**2)(positions, probe)
    (rest,) = call(turn_body, [rest.shape], [SMEM, VMEM], moved=16 * size**2 * share)(positions, rest)

    def inner(kept, count, at, turned, *given):
        (result,) = call(
            functools.partial(inner_body, kept, count),
            [(kept + count, 2) + grid],
            [SMEM, VMEM, VMEM, VMEM, VMEM, VMEM, VMEM] + [VMEM] * len(given),
            [pltpu.VMEM((2,) + grid, F32)],
            flops=2 * flops * count,
            moved=16 * size**2 * count,
        )(where, object_slices[0:1], halos[0], turned, kr, ki, tab, *given)
        return result

    waves = inner(0, 1, 0, first)
    waves = inner(1, share, 1, rest, waves)
    term_one, chi = call(
        functools.partial(middle_body, rows),
        [(2, rows, size), (states, 2) + grid],
        [SMEM] + [VMEM] * 5,
        [pltpu.VMEM((2,) + grid, F32), pltpu.VMEM((states, 2) + grid, F32), pltpu.VMEM(grid, F32)],
        flops=2 * flops * states,
        moved=32 * size**2 * states,
    )(where, object_slices[1:2], halos[1], waves, amp, tab)
    came_one = shifted(term_one, "frame", 1)
    (term_zero,) = call(
        functools.partial(last_body, rows),
        [(2, rows, size)],
        [SMEM] + [VMEM] * 6,
        [pltpu.VMEM((2,) + grid, F32)],
        flops=2 * flops * states,
        moved=16 * size**2 * states,
    )(where, chi, first, rest, kr, ki, tab)
    came_zero = shifted(term_zero, "frame", 1)
    (gradient,) = call(
        functools.partial(gather_body, rows),
        [(2, 2, rows, 2 * size)],
        [SMEM] + [VMEM] * 4,
        moved=64 * rows * size,
    )(where, term_zero, came_zero, term_one, came_one)
    return gradient


def solution(mesh):
    return jax.shard_map(
        on_device,
        mesh=mesh,
        in_specs=(
            P(None, None, "frame", None),
            P("state", None, None, None),
            P("frame", None, None),
            P("frame", None),
            P(),
        ),
        out_specs=P(None, None, ("frame", "state"), None),
        check_vma=False,
    )
```

```python
import functools
import math

import jax
import jax.numpy as jnp
import numpy as np
from jax import lax
from jax.experimental import pallas as pl
from jax.experimental.pallas import tpu as pltpu
from jax.sharding import PartitionSpec as P


F32 = jnp.float32
BF16 = jnp.bfloat16
VMEM = pl.BlockSpec(memory_space=pltpu.VMEM)
SMEM = pl.BlockSpec(memory_space=pltpu.SMEM)
LIMIT = 24 * 1024 * 1024


def shifted(value, axis, by):
    count = lax.axis_size(axis)
    return lax.ppermute(value, axis, [(i, (i + by) % count) for i in range(count)])


def call(body, outs, ins, scratch=(), flops=0, moved=0):
    return pl.pallas_call(
        body,
        out_shape=[jax.ShapeDtypeStruct(shape, F32) for shape in outs],
        in_specs=ins,
        out_specs=[VMEM] * len(outs),
        scratch_shapes=list(scratch),
        compiler_params=pltpu.CompilerParams(vmem_limit_bytes=LIMIT),
        cost_estimate=pl.CostEstimate(flops=flops, bytes_accessed=moved, transcendentals=0),
    )


def tables(length):
    half = length // 2
    n = np.arange(half)[:, None]
    forms = []
    for parity in (0, 1):
        k = 2 * np.arange(half)[None, :] + parity
        angle = -2.0 * math.pi * ((n * k) % length) / length
        re, im = np.cos(angle) / math.sqrt(length), np.sin(angle) / math.sqrt(length)
        right = np.block([[re, im], [-im, re]])
        forms += [right, right.T]
    stack = np.stack(forms).astype(np.float64)
    top = stack.astype(BF16)
    rest = (stack - top.astype(np.float64)).astype(BF16)
    return jnp.asarray(np.stack([top, rest]))


def halves(value):
    top = value.astype(BF16)
    return top, (value - top.astype(F32)).astype(BF16)


def dot(a, b):
    return lax.dot_general(a, b, (((1,), (0,)), ((), ())), preferred_element_type=F32)


def times_table(value, tab, which):
    top, rest = halves(value)
    return dot(top, tab[0, which]) + (dot(rest, tab[0, which]) + dot(top, tab[1, which]))


def table_times(value, tab, which):
    top, rest = halves(value)
    return dot(tab[0, which], top) + (dot(tab[0, which], rest) + dot(tab[1, which], top))


def columns_forward(re, im, tab):
    h = re.shape[1] // 2
    r0, r1, i0, i1 = re[:, :h], re[:, h:], im[:, :h], im[:, h:]
    even = times_table(jnp.concatenate([r0 + r1, i0 + i1], 1), tab, 0)
    odd = times_table(jnp.concatenate([r0 - r1, i0 - i1], 1), tab, 2)
    return (
        jnp.concatenate([even[:, :h], odd[:, :h]], 1),
        jnp.concatenate([even[:, h:], odd[:, h:]], 1),
    )


def columns_inverse(re, im, tab):
    h = re.shape[1] // 2
    even = times_table(jnp.concatenate([re[:, :h], im[:, :h]], 1), tab, 1)
    odd = times_table(jnp.concatenate([re[:, h:], im[:, h:]], 1), tab, 3)
    total, gap = even + odd, even - odd
    return (
        jnp.concatenate([total[:, :h], gap[:, :h]], 1),
        jnp.concatenate([total[:, h:], gap[:, h:]], 1),
    )


def rows_forward(re, im, tab):
    h = re.shape[0] // 2
    r0, r1, i0, i1 = re[:h], re[h:], im[:h], im[h:]
    even = table_times(jnp.concatenate([r0 + r1, i0 + i1], 0), tab, 1)
    odd = table_times(jnp.concatenate([r0 - r1, i0 - i1], 0), tab, 3)
    return (
        jnp.concatenate([even[:h], odd[:h]], 0),
        jnp.concatenate([even[h:], odd[h:]], 0),
    )


def rows_inverse(re, im, tab):
    h = re.shape[0] // 2
    even = table_times(jnp.concatenate([re[:h], im[:h]], 0), tab, 0)
    odd = table_times(jnp.concatenate([re[h:], im[h:]], 0), tab, 2)
    total, gap = even + odd, even - odd
    return (
        jnp.concatenate([total[:h], gap[:h]], 0),
        jnp.concatenate([total[h:], gap[h:]], 0),
    )


def forward(waves, tab):
    waves = [columns_forward(*wave, tab) for wave in waves]
    return [rows_forward(*wave, tab) for wave in waves]


def inverse(waves, tab):
    waves = [rows_inverse(*wave, tab) for wave in waves]
    return [columns_inverse(*wave, tab) for wave in waves]


def times(a, b):
    return a[0] * b[0] - a[1] * b[1], a[0] * b[1] + a[1] * b[0]


def times_conj(a, b):
    return a[0] * b[0] + a[1] * b[1], a[0] * b[1] - a[1] * b[0]


def in_groups(states, body):
    group = 2 if states % 2 == 0 else 1
    if states == group:
        body([m for m in range(group)])
        return

    def step(g, carry):
        body([g * group + m for m in range(group)])
        return carry

    lax.fori_loop(0, states // group, step, 0)


def thirds(value):
    top = value.astype(BF16)
    left = value - top.astype(F32)
    mid = left.astype(BF16)
    return top, mid, (left - mid.astype(F32)).astype(BF16)


def by_parity(value):
    size = value.shape[0]
    h = size // 2
    picks = []
    for along in (0, 1):
        place = lax.broadcasted_iota(jnp.int32, (size, size), along)
        source = lax.broadcasted_iota(jnp.int32, (size, size), 1 - along)
        wanted = jnp.where(place < h, 2 * place, 2 * (place - h) + 1)
        picks.append(jnp.where(source == wanted, 1.0, 0.0).astype(BF16))
    top, mid, low = thirds(value)
    value = (dot(picks[0], top) + dot(picks[0], mid)) + dot(picks[0], low)
    top, mid, low = thirds(value)
    return (dot(top, picks[1]) + dot(mid, picks[1])) + dot(low, picks[1])


def prepare_body(prop_ref, amp_ref, wave_re, wave_im, amp_out):
    phase = by_parity(prop_ref[...])
    wave_re[...] = jnp.cos(phase)
    wave_im[...] = jnp.sin(phase)
    amp_out[...] = by_parity(amp_ref[0])


def turn_body(pos_ref, probe_ref, out_ref):
    size = probe_ref.shape[-1]
    row, col = pos_ref[0, 0], lax.rem(pos_ref[0, 1], size)
    for m in range(probe_ref.shape[0]):
        for c in range(2):
            out_ref[m, c] = pltpu.roll(pltpu.roll(probe_ref[m, c], row, 0), col, 1)


def wrapped(ref, s, part, col):
    size = ref.shape[-2]
    c = lax.broadcasted_iota(jnp.int32, (size, size), 1)
    return jnp.where(c < col, ref[s, part, :, size:], ref[s, part, :, :size])


def send_body(before_ref, object_ref, zero_ref, one_ref):
    for s, out in enumerate((zero_ref, one_ref)):
        for part in range(2):
            out[part] = wrapped(object_ref, s, part, before_ref[0, 1])


def patch_of(s, object_ref, halo_ref, pos_ref):
    size = halo_ref.shape[-1]
    r = lax.broadcasted_iota(jnp.int32, (size, size), 0)
    return [
        jnp.where(r < pos_ref[0, 0], halo_ref[part], wrapped(object_ref, s, part, pos_ref[0, 1]))
        for part in range(2)
    ]


def pair(ref, *at):
    return ref[(*at, 0)], ref[(*at, 1)]


def inner_body(pos_ref, object_ref, halo_ref, first_ref, rest_ref, kr_ref, ki_ref, tab, out_ref, patch, probes):
    states = out_ref.shape[0]
    patch[0], patch[1] = patch_of(0, object_ref, halo_ref, pos_ref)
    probes[:1] = first_ref[...]
    probes[1:] = rest_ref[...]

    def body(group):
        waves = forward([times(pair(probes, m), pair(patch)) for m in group], tab)
        waves = inverse([times((kr_ref[...], ki_ref[...]), wave) for wave in waves], tab)
        for m, wave in zip(group, waves):
            out_ref[m, 0], out_ref[m, 1] = wave

    in_groups(states, body)


def middle_body(rows, pos_ref, object_ref, halo_ref, inner_ref, amp_ref, tab, term_ref, chi_ref, patch, far, power):
    states = inner_ref.shape[0]
    patch[0], patch[1] = patch_of(1, object_ref, halo_ref, pos_ref)
    power[...] = jnp.zeros_like(power)

    def outward(group):
        waves = forward([times(pair(patch), pair(inner_ref, m)) for m in group], tab)
        total = power[...]
        for m, wave in zip(group, waves):
            far[m, 0], far[m, 1] = wave
            total += wave[0] * wave[0] + wave[1] * wave[1]
        power[...] = total

    in_groups(states, outward)
    power[...] = 1.0 - amp_ref[...] / jnp.sqrt(power[...] + 1.0)
    term_ref[...] = jnp.zeros_like(term_ref)
    take = pl.ds(pl.multiple_of(pos_ref[0, 2] * rows, rows), rows)

    def homeward(group):
        waves = inverse([(power[...] * far[m, 0], power[...] * far[m, 1]) for m in group], tab)
        for m, wave in zip(group, waves):
            far[m, 0], far[m, 1] = wave
            chi_ref[m, 0], chi_ref[m, 1] = times_conj(pair(patch), wave)
        for m in group:
            part = times_conj(
                (inner_ref[m, 0, take], inner_ref[m, 1, take]), (far[m, 0, take], far[m, 1, take])
            )
            term_ref[0] += part[0]
            term_ref[1] += part[1]

    in_groups(states, homeward)


def last_body(rows, pos_ref, chi_ref, first_ref, rest_ref, kr_ref, ki_ref, tab, term_ref, front, probes):
    states = chi_ref.shape[0]
    take = pl.ds(pl.multiple_of(pos_ref[0, 2] * rows, rows), rows)
    term_ref[...] = jnp.zeros_like(term_ref)
    probes[:1] = first_ref[:, :, take]
    probes[1:] = rest_ref[:, :, take]

    def body(group):
        waves = forward([pair(chi_ref, m) for m in group], tab)
        waves = [rows_inverse(*times_conj((kr_ref[...], ki_ref[...]), wave), tab) for wave in waves]
        for m, wave in zip(group, waves):
            front[m, 0], front[m, 1] = wave
        for m in group:
            wave = columns_inverse(front[m, 0, take], front[m, 1, take], tab)
            part = times_conj(pair(probes, m), wave)
            term_ref[0] += part[0]
            term_ref[1] += part[1]

    in_groups(states, body)


def gather_body(slice_id, rows, pos_ref, own_ref, came_ref, *refs):
    out_ref, held, sem = refs[-3:]
    size = own_ref.shape[-1]
    start = pos_ref[0, 2] * rows
    r = lax.broadcasted_iota(jnp.int32, (rows, size), 0) + start
    c = lax.broadcasted_iota(jnp.int32, (rows, size), 1)
    here, there = r >= pos_ref[0, 0], r < pos_ref[0, 3]
    here_right, there_right = c < pos_ref[0, 1], c < pos_ref[0, 4]
    copies = []
    for part in range(2):
        mine = jnp.where(here, own_ref[part], 0.0)
        theirs = jnp.where(there, came_ref[part], 0.0)
        held[part, :, :size] = jnp.where(here_right, 0.0, mine) + jnp.where(there_right, 0.0, theirs)
        held[part, :, size:] = jnp.where(here_right, mine, 0.0) + jnp.where(there_right, theirs, 0.0)
        copies.append(pltpu.make_async_copy(held.at[part], out_ref.at[slice_id, part], sem.at[part]))
        copies[-1].start()
    for copy in copies:
        copy.wait()


def gather(slice_id, rows, size, where, own, came, *given):
    return pl.pallas_call(
        functools.partial(gather_body, slice_id, rows),
        out_shape=jax.ShapeDtypeStruct((2, 2, rows, 2 * size), F32),
        in_specs=[SMEM, VMEM, VMEM] + [pl.BlockSpec(memory_space=pl.ANY)] * len(given),
        out_specs=pl.BlockSpec(memory_space=pl.ANY),
        scratch_shapes=[pltpu.VMEM((2, rows, 2 * size), F32), pltpu.SemaphoreType.DMA((2,))],
        input_output_aliases={3: 0} if given else {},
        compiler_params=pltpu.CompilerParams(vmem_limit_bytes=LIMIT),
        cost_estimate=pl.CostEstimate(flops=0, bytes_accessed=32 * rows * size, transcendentals=0),
    )(where, own, came, *given)


def on_device(object_slices, probe, amplitude, positions, propagator):
    states = lax.axis_size("state")
    size = amplitude.shape[1]
    rows = object_slices.shape[2] // states
    assert object_slices.shape[2:] == (size, 2 * size) and positions.shape[0] == 1
    return gradient_of(object_slices, probe, amplitude, positions, propagator, states, size, rows)


def gradient_of(object_slices, probe, amplitude, positions, propagator, states, size, rows):
    grid = (size, size)
    unit = size * size
    flops = 24 * size**3
    tab = tables(size)
    before = shifted(positions, "frame", 1)
    others = [shifted(probe, "state", by) for by in range(1, states)]
    kr, ki, amp = call(prepare_body, [grid] * 3, [VMEM] * 2, flops=2 * size**3, moved=20 * unit)(propagator, amplitude)
    (first,) = call(turn_body, [probe.shape], [SMEM, VMEM], moved=16 * unit)(positions, probe)
    before, kr, ki, amp, first = lax.optimization_barrier((before, kr, ki, amp, first))
    index = lax.axis_index("state").astype(jnp.int32)
    where = jnp.concatenate([positions, index[None, None], before], 1)

    picked = call(send_body, [(2,) + grid] * 2, [SMEM, VMEM], moved=16 * unit)(before, object_slices)
    halo_zero = shifted(picked[0], "frame", -1)
    halo_one = shifted(picked[1], "frame", -1)
    rest = others[0] if states == 2 else jnp.concatenate(others, 0)
    (rest,) = call(turn_body, [rest.shape], [SMEM, VMEM], moved=16 * unit * (states - 1))(positions, rest)

    (waves,) = call(
        inner_body,
        [(states, 2) + grid],
        [SMEM] + [VMEM] * 7,
        [pltpu.VMEM((2,) + grid, F32), pltpu.VMEM((states, 2) + grid, F32)],
        flops=2 * flops * states,
        moved=16 * unit * states,
    )(where, object_slices, halo_zero, first, rest, kr, ki, tab)
    term_one, chi = call(
        functools.partial(middle_body, rows),
        [(2, rows, size), (states, 2) + grid],
        [SMEM] + [VMEM] * 5,
        [pltpu.VMEM((2,) + grid, F32), pltpu.VMEM((states, 2) + grid, F32), pltpu.VMEM(grid, F32)],
        flops=2 * flops * states,
        moved=32 * unit * states,
    )(where, object_slices, halo_one, waves, amp, tab)
    came_one = shifted(term_one, "frame", 1)
    (term_zero,) = call(
        functools.partial(last_body, rows),
        [(2, rows, size)],
        [SMEM] + [VMEM] * 6,
        [pltpu.VMEM((states, 2) + grid, F32), pltpu.VMEM((states, 2, rows, size), F32)],
        flops=2 * flops * states,
        moved=16 * unit * states,
    )(where, chi, first, rest, kr, ki, tab)
    came_zero = shifted(term_zero, "frame", 1)
    gradient = gather(1, rows, size, where, term_one, came_one)
    return gather(0, rows, size, where, term_zero, came_zero, gradient)


def solution(mesh):
    return jax.shard_map(
        on_device,
        mesh=mesh,
        in_specs=(
            P(None, None, "frame", None),
            P("state", None, None, None),
            P("frame", None, None),
            P("frame", None),
            P(),
        ),
        out_specs=P(None, None, ("frame", "state"), None),
        check_vma=False,
    )
```

```python
import functools
import math

import jax
import jax.numpy as jnp
import numpy as np
from jax import lax
from jax.experimental import pallas as pl
from jax.experimental.pallas import tpu as pltpu
from jax.sharding import PartitionSpec as P


F32 = jnp.float32
BF16 = jnp.bfloat16
VMEM = pl.BlockSpec(memory_space=pltpu.VMEM)
HBM = pl.BlockSpec(memory_space=pltpu.MemorySpace.HBM)
SMEM = pl.BlockSpec(memory_space=pltpu.SMEM)
LIMIT = 24 * 1024 * 1024


def shifted(value, axis, by):
    count = lax.axis_size(axis)
    return lax.ppermute(value, axis, [(i, (i + by) % count) for i in range(count)])


def in_hbm(value):
    return pltpu.with_memory_space_constraint(value, pltpu.MemorySpace.HBM)


def call(body, outs, ins, scratch=(), flops=0, moved=0):
    return pl.pallas_call(
        body,
        out_shape=[jax.ShapeDtypeStruct(shape, F32) for shape in outs],
        in_specs=ins,
        out_specs=[VMEM] * len(outs),
        scratch_shapes=list(scratch),
        compiler_params=pltpu.CompilerParams(vmem_limit_bytes=LIMIT),
        cost_estimate=pl.CostEstimate(flops=flops, bytes_accessed=moved, transcendentals=0),
    )


def tables(length):
    half = length // 2
    n = np.arange(half)[:, None]
    forms = []
    for parity in (0, 1):
        k = 2 * np.arange(half)[None, :] + parity
        angle = -2.0 * math.pi * ((n * k) % length) / length
        re, im = np.cos(angle) / math.sqrt(length), np.sin(angle) / math.sqrt(length)
        right = np.block([[re, im], [-im, re]])
        forms += [right, right.T]
    stack = np.stack(forms).astype(np.float64)
    top = stack.astype(BF16)
    rest = (stack - top.astype(np.float64)).astype(BF16)
    return jnp.asarray(np.stack([top, rest]))


def halves(value):
    top = value.astype(BF16)
    return top, (value - top.astype(F32)).astype(BF16)


def dot(a, b):
    return lax.dot_general(a, b, (((1,), (0,)), ((), ())), preferred_element_type=F32)


def times_table(value, tab, which):
    top, rest = halves(value)
    return dot(top, tab[0, which]) + (dot(rest, tab[0, which]) + dot(top, tab[1, which]))


def table_times(value, tab, which):
    top, rest = halves(value)
    return dot(tab[0, which], top) + (dot(tab[0, which], rest) + dot(tab[1, which], top))


def columns_forward(re, im, tab):
    h = re.shape[1] // 2
    r0, r1, i0, i1 = re[:, :h], re[:, h:], im[:, :h], im[:, h:]
    even = times_table(jnp.concatenate([r0 + r1, i0 + i1], 1), tab, 0)
    odd = times_table(jnp.concatenate([r0 - r1, i0 - i1], 1), tab, 2)
    return (
        jnp.concatenate([even[:, :h], odd[:, :h]], 1),
        jnp.concatenate([even[:, h:], odd[:, h:]], 1),
    )


def columns_inverse(re, im, tab):
    h = re.shape[1] // 2
    even = times_table(jnp.concatenate([re[:, :h], im[:, :h]], 1), tab, 1)
    odd = times_table(jnp.concatenate([re[:, h:], im[:, h:]], 1), tab, 3)
    total, gap = even + odd, even - odd
    return (
        jnp.concatenate([total[:, :h], gap[:, :h]], 1),
        jnp.concatenate([total[:, h:], gap[:, h:]], 1),
    )


def rows_forward(re, im, tab):
    h = re.shape[0] // 2
    r0, r1, i0, i1 = re[:h], re[h:], im[:h], im[h:]
    even = table_times(jnp.concatenate([r0 + r1, i0 + i1], 0), tab, 1)
    odd = table_times(jnp.concatenate([r0 - r1, i0 - i1], 0), tab, 3)
    return (
        jnp.concatenate([even[:h], odd[:h]], 0),
        jnp.concatenate([even[h:], odd[h:]], 0),
    )


def rows_inverse(re, im, tab):
    h = re.shape[0] // 2
    even = table_times(jnp.concatenate([re[:h], im[:h]], 0), tab, 0)
    odd = table_times(jnp.concatenate([re[h:], im[h:]], 0), tab, 2)
    total, gap = even + odd, even - odd
    return (
        jnp.concatenate([total[:h], gap[:h]], 0),
        jnp.concatenate([total[h:], gap[h:]], 0),
    )


def forward(waves, tab):
    waves = [columns_forward(*wave, tab) for wave in waves]
    return [rows_forward(*wave, tab) for wave in waves]


def inverse(waves, tab):
    waves = [rows_inverse(*wave, tab) for wave in waves]
    return [columns_inverse(*wave, tab) for wave in waves]


def times(a, b):
    return a[0] * b[0] - a[1] * b[1], a[0] * b[1] + a[1] * b[0]


def times_conj(a, b):
    return a[0] * b[0] + a[1] * b[1], a[0] * b[1] - a[1] * b[0]


def in_groups(states, body):
    group = 2 if states % 2 == 0 else 1
    if states == group:
        body([m for m in range(group)])
        return

    def step(g, carry):
        body([g * group + m for m in range(group)])
        return carry

    lax.fori_loop(0, states // group, step, 0)


def thirds(value):
    top = value.astype(BF16)
    left = value - top.astype(F32)
    mid = left.astype(BF16)
    return top, mid, (left - mid.astype(F32)).astype(BF16)


def by_parity(value):
    size = value.shape[0]
    h = size // 2
    picks = []
    for along in (0, 1):
        place = lax.broadcasted_iota(jnp.int32, (size, size), along)
        source = lax.broadcasted_iota(jnp.int32, (size, size), 1 - along)
        wanted = jnp.where(place < h, 2 * place, 2 * (place - h) + 1)
        picks.append(jnp.where(source == wanted, 1.0, 0.0).astype(BF16))
    top, mid, low = thirds(value)
    value = (dot(picks[0], top) + dot(picks[0], mid)) + dot(picks[0], low)
    top, mid, low = thirds(value)
    return (dot(top, picks[1]) + dot(mid, picks[1])) + dot(low, picks[1])


def turned(value, row, col):
    return pltpu.roll(pltpu.roll(value, row, 0), col, 1)


def prepare_body(
    pos_hbm, probe_hbm, prop_hbm, amp_hbm, object_hbm, tab_hbm,
    wave_re, wave_im, amp_out, first_out, object_out, tab_out, pos_out,
    pos, probe, prop, amp, sem,
):
    moves = (
        (pos_hbm, pos), (probe_hbm, probe), (prop_hbm, prop), (amp_hbm, amp),
        (pos_hbm, pos_out), (object_hbm, object_out), (tab_hbm, tab_out),
    )
    copies = [pltpu.make_async_copy(src, dst, sem.at[i]) for i, (src, dst) in enumerate(moves)]
    for copy in copies:
        copy.start()
    copies[0].wait()
    copies[1].wait()
    size = prop.shape[0]
    row, col = pos[0, 0], lax.rem(pos[0, 1], size)
    for c in range(2):
        first_out[0, c] = turned(probe[0, c], row, col)
    copies[2].wait()
    phase = by_parity(prop[...])
    wave_re[...] = jnp.cos(phase)
    wave_im[...] = jnp.sin(phase)
    copies[3].wait()
    amp_out[...] = by_parity(amp[0])
    for copy in copies[4:]:
        copy.wait()


def turn_body(pos_ref, first_ref, probe_ref, out_ref):
    size = probe_ref.shape[-1]
    row, col = pos_ref[0, 0], lax.rem(pos_ref[0, 1], size)
    out_ref[:1] = first_ref[...]
    for m in range(probe_ref.shape[0]):
        for c in range(2):
            out_ref[1 + m, c] = turned(probe_ref[m, c], row, col)


def spread(ref, which, shape):
    return jnp.broadcast_to(ref[0:1, which : which + 1], shape)


def wrapped(ref, s, part, col_ref):
    size = ref.shape[-2]
    c = lax.broadcasted_iota(jnp.int32, (size, size), 1)
    return jnp.where(c < spread(col_ref, 1, c.shape), ref[s, part, :, size:], ref[s, part, :, :size])


def send_body(before_ref, object_ref, zero_ref, one_ref):
    for s, out in enumerate((zero_ref, one_ref)):
        for part in range(2):
            out[part] = wrapped(object_ref, s, part, before_ref)


def patch_of(s, object_ref, halo_ref, pos_ref):
    size = halo_ref.shape[-1]
    r = lax.broadcasted_iota(jnp.int32, (size, size), 0)
    return [
        jnp.where(r < spread(pos_ref, 0, r.shape), halo_ref[part], wrapped(object_ref, s, part, pos_ref))
        for part in range(2)
    ]


def pair(ref, *at):
    return ref[(*at, 0)], ref[(*at, 1)]


def inner_body(pos_ref, object_ref, halo_ref, probe_ref, kr_ref, ki_ref, tab, out_ref, patch):
    states = out_ref.shape[0]
    patch[0], patch[1] = patch_of(0, object_ref, halo_ref, pos_ref)

    def body(group):
        waves = forward([times(pair(probe_ref, m), pair(patch)) for m in group], tab)
        waves = inverse([times((kr_ref[...], ki_ref[...]), wave) for wave in waves], tab)
        for m, wave in zip(group, waves):
            out_ref[m, 0], out_ref[m, 1] = wave

    in_groups(states, body)


def middle_body(rows, pos_ref, object_ref, halo_ref, inner_ref, amp_ref, tab, term_ref, chi_ref, patch, far, power):
    states = inner_ref.shape[0]
    patch[0], patch[1] = patch_of(1, object_ref, halo_ref, pos_ref)
    power[...] = jnp.zeros_like(power)

    def outward(group):
        waves = forward([times(pair(patch), pair(inner_ref, m)) for m in group], tab)
        total = power[...]
        for m, wave in zip(group, waves):
            far[m, 0], far[m, 1] = wave
            total += wave[0] * wave[0] + wave[1] * wave[1]
        power[...] = total

    in_groups(states, outward)
    power[...] = 1.0 - amp_ref[...] / jnp.sqrt(power[...] + 1.0)
    term_ref[...] = jnp.zeros_like(term_ref)
    take = pl.ds(pl.multiple_of(lax.axis_index("state") * rows, rows), rows)

    def homeward(group):
        waves = inverse([(power[...] * far[m, 0], power[...] * far[m, 1]) for m in group], tab)
        for m, wave in zip(group, waves):
            far[m, 0], far[m, 1] = wave
            chi_ref[m, 0], chi_ref[m, 1] = times_conj(pair(patch), wave)
        for m in group:
            part = times_conj(
                (inner_ref[m, 0, take], inner_ref[m, 1, take]), (far[m, 0, take], far[m, 1, take])
            )
            term_ref[0] += part[0]
            term_ref[1] += part[1]

    in_groups(states, homeward)


def last_body(rows, chi_ref, probe_ref, kr_ref, ki_ref, tab, term_ref, front):
    states = chi_ref.shape[0]
    take = pl.ds(pl.multiple_of(lax.axis_index("state") * rows, rows), rows)
    term_ref[...] = jnp.zeros_like(term_ref)

    def body(group):
        waves = forward([pair(chi_ref, m) for m in group], tab)
        waves = [rows_inverse(*times_conj((kr_ref[...], ki_ref[...]), wave), tab) for wave in waves]
        for m, wave in zip(group, waves):
            front[m, 0], front[m, 1] = wave
        for m in group:
            wave = columns_inverse(front[m, 0, take], front[m, 1, take], tab)
            part = times_conj((probe_ref[m, 0, take], probe_ref[m, 1, take]), wave)
            term_ref[0] += part[0]
            term_ref[1] += part[1]

    in_groups(states, body)


def gather_body(slice_id, rows, pos_ref, before_ref, own_ref, came_ref, *refs):
    out_ref, held, sem = refs[-3:]
    size = own_ref.shape[-1]
    start = lax.axis_index("state") * rows
    r = lax.broadcasted_iota(jnp.int32, (rows, size), 0) + start
    c = lax.broadcasted_iota(jnp.int32, (rows, size), 1)
    here, there = r >= spread(pos_ref, 0, r.shape), r < spread(before_ref, 0, r.shape)
    here_right, there_right = c < spread(pos_ref, 1, c.shape), c < spread(before_ref, 1, c.shape)
    copies = []
    for part in range(2):
        mine = jnp.where(here, own_ref[part], 0.0)
        theirs = jnp.where(there, came_ref[part], 0.0)
        held[part, :, :size] = jnp.where(here_right, 0.0, mine) + jnp.where(there_right, 0.0, theirs)
        held[part, :, size:] = jnp.where(here_right, mine, 0.0) + jnp.where(there_right, theirs, 0.0)
        copies.append(pltpu.make_async_copy(held.at[part], out_ref.at[slice_id, part], sem.at[part]))
        copies[-1].start()
    for copy in copies:
        copy.wait()


def gather(slice_id, rows, size, pos, before, own, came, *given):
    return pl.pallas_call(
        functools.partial(gather_body, slice_id, rows),
        out_shape=jax.ShapeDtypeStruct((2, 2, rows, 2 * size), F32),
        in_specs=[VMEM] * 4 + [pl.BlockSpec(memory_space=pl.ANY)] * len(given),
        out_specs=pl.BlockSpec(memory_space=pl.ANY),
        scratch_shapes=[pltpu.VMEM((2, rows, 2 * size), F32), pltpu.SemaphoreType.DMA((2,))],
        input_output_aliases={4: 0} if given else {},
        compiler_params=pltpu.CompilerParams(vmem_limit_bytes=LIMIT),
        cost_estimate=pl.CostEstimate(flops=0, bytes_accessed=32 * rows * size, transcendentals=0),
    )(pos, before, own, came, *given)


def on_device(object_slices, probe, amplitude, positions, propagator):
    states = lax.axis_size("state")
    size = amplitude.shape[1]
    rows = object_slices.shape[2] // states
    assert object_slices.shape[2:] == (size, 2 * size) and positions.shape[0] == 1
    return gradient_of(object_slices, probe, amplitude, positions, propagator, states, size, rows)


def gradient_of(object_slices, probe, amplitude, positions, propagator, states, size, rows):
    grid = (size, size)
    unit = size * size
    flops = 24 * size**3
    tab = tables(size)
    before = shifted(positions, "frame", 1)
    others = [shifted(probe, "state", by) for by in range(1, states)]
    kr, ki, amp, first, held, tab, pos = pl.pallas_call(
        prepare_body,
        out_shape=[jax.ShapeDtypeStruct(grid, F32)] * 3
        + [jax.ShapeDtypeStruct(x.shape, x.dtype) for x in (probe, object_slices, tab, positions)],
        in_specs=[HBM] * 6,
        out_specs=[VMEM] * 7,
        scratch_shapes=[
            pltpu.SMEM(positions.shape, jnp.int32),
            pltpu.VMEM(probe.shape, F32),
            pltpu.VMEM(grid, F32),
            pltpu.VMEM(amplitude.shape, F32),
            pltpu.SemaphoreType.DMA((7,)),
        ],
        compiler_params=pltpu.CompilerParams(vmem_limit_bytes=LIMIT),
        cost_estimate=pl.CostEstimate(flops=2 * size**3, bytes_accessed=60 * unit, transcendentals=0),
    )(*(in_hbm(x) for x in (positions, probe, propagator, amplitude, object_slices, tab)))
    picked = call(send_body, [(2,) + grid] * 2, [VMEM, VMEM], moved=16 * unit)(before, held)
    halo_zero = shifted(picked[0], "frame", -1)
    halo_one = shifted(picked[1], "frame", -1)
    rest = others[0] if states == 2 else jnp.concatenate(others, 0)
    (probes,) = call(turn_body, [(states, 2) + grid], [SMEM, VMEM, VMEM], moved=16 * unit * (states - 1))(
        pos, first, rest
    )

    (waves,) = call(
        inner_body,
        [(states, 2) + grid],
        [VMEM] * 7,
        [pltpu.VMEM((2,) + grid, F32)],
        flops=2 * flops * states,
        moved=16 * unit * states,
    )(pos, held, halo_zero, probes, kr, ki, tab)
    term_one, chi = call(
        functools.partial(middle_body, rows),
        [(2, rows, size), (states, 2) + grid],
        [VMEM] * 6,
        [pltpu.VMEM((2,) + grid, F32), pltpu.VMEM((states, 2) + grid, F32), pltpu.VMEM(grid, F32)],
        flops=2 * flops * states,
        moved=32 * unit * states,
    )(pos, held, halo_one, waves, amp, tab)
    came_one = shifted(term_one, "frame", 1)
    (term_zero,) = call(
        functools.partial(last_body, rows),
        [(2, rows, size)],
        [VMEM] * 5,
        [pltpu.VMEM((states, 2) + grid, F32)],
        flops=2 * flops * states,
        moved=16 * unit * states,
    )(chi, probes, kr, ki, tab)
    came_zero = shifted(term_zero, "frame", 1)
    gradient = gather(1, rows, size, pos, before, term_one, came_one)
    return gather(0, rows, size, pos, before, term_zero, came_zero, gradient)


def solution(mesh):
    return jax.shard_map(
        on_device,
        mesh=mesh,
        in_specs=(
            P(None, None, "frame", None),
            P("state", None, None, None),
            P("frame", None, None),
            P("frame", None),
            P(),
        ),
        out_specs=P(None, None, ("frame", "state"), None),
        check_vma=False,
    )
```

```python
import functools
import math

import jax
import jax.numpy as jnp
import numpy as np
from jax import lax
from jax.experimental import pallas as pl
from jax.experimental.pallas import tpu as pltpu
from jax.sharding import PartitionSpec as P


F32 = jnp.float32
BF16 = jnp.bfloat16
VMEM = pl.BlockSpec(memory_space=pltpu.VMEM)
HBM = pl.BlockSpec(memory_space=pltpu.MemorySpace.HBM)
SMEM = pl.BlockSpec(memory_space=pltpu.SMEM)
LIMIT = 24 * 1024 * 1024


def shifted(value, axis, by):
    count = lax.axis_size(axis)
    return lax.ppermute(value, axis, [(i, (i + by) % count) for i in range(count)])


def in_hbm(value):
    return pltpu.with_memory_space_constraint(value, pltpu.MemorySpace.HBM)


def call(body, outs, ins, scratch=(), flops=0, moved=0):
    return pl.pallas_call(
        body,
        out_shape=[jax.ShapeDtypeStruct(shape, F32) for shape in outs],
        in_specs=ins,
        out_specs=[VMEM] * len(outs),
        scratch_shapes=list(scratch),
        compiler_params=pltpu.CompilerParams(vmem_limit_bytes=LIMIT),
        cost_estimate=pl.CostEstimate(flops=flops, bytes_accessed=moved, transcendentals=0),
    )


def tables(length):
    half = length // 2
    n = np.arange(half)[:, None]
    forms = []
    for parity in (0, 1):
        k = 2 * np.arange(half)[None, :] + parity
        angle = -2.0 * math.pi * ((n * k) % length) / length
        re, im = np.cos(angle) / math.sqrt(length), np.sin(angle) / math.sqrt(length)
        right = np.block([[re, im], [-im, re]])
        forms += [right, right.T]
    stack = np.stack(forms).astype(np.float64)
    top = stack.astype(BF16)
    rest = (stack - top.astype(np.float64)).astype(BF16)
    return jnp.asarray(np.stack([top, rest]))


def halves(value):
    top = value.astype(BF16)
    return top, (value - top.astype(F32)).astype(BF16)


def dot(a, b):
    return lax.dot_general(a, b, (((1,), (0,)), ((), ())), preferred_element_type=F32)


def times_table(value, tab, which):
    top, rest = halves(value)
    return dot(top, tab[0, which]) + (dot(rest, tab[0, which]) + dot(top, tab[1, which]))


def table_times(value, tab, which):
    top, rest = halves(value)
    return dot(tab[0, which], top) + (dot(tab[0, which], rest) + dot(tab[1, which], top))


def columns_forward(re, im, tab):
    h = re.shape[1] // 2
    r0, r1, i0, i1 = re[:, :h], re[:, h:], im[:, :h], im[:, h:]
    even = times_table(jnp.concatenate([r0 + r1, i0 + i1], 1), tab, 0)
    odd = times_table(jnp.concatenate([r0 - r1, i0 - i1], 1), tab, 2)
    return (
        jnp.concatenate([even[:, :h], odd[:, :h]], 1),
        jnp.concatenate([even[:, h:], odd[:, h:]], 1),
    )


def columns_inverse(re, im, tab):
    h = re.shape[1] // 2
    even = times_table(jnp.concatenate([re[:, :h], im[:, :h]], 1), tab, 1)
    odd = times_table(jnp.concatenate([re[:, h:], im[:, h:]], 1), tab, 3)
    total, gap = even + odd, even - odd
    return (
        jnp.concatenate([total[:, :h], gap[:, :h]], 1),
        jnp.concatenate([total[:, h:], gap[:, h:]], 1),
    )


def rows_forward(re, im, tab):
    h = re.shape[0] // 2
    r0, r1, i0, i1 = re[:h], re[h:], im[:h], im[h:]
    even = table_times(jnp.concatenate([r0 + r1, i0 + i1], 0), tab, 1)
    odd = table_times(jnp.concatenate([r0 - r1, i0 - i1], 0), tab, 3)
    return (
        jnp.concatenate([even[:h], odd[:h]], 0),
        jnp.concatenate([even[h:], odd[h:]], 0),
    )


def rows_inverse(re, im, tab):
    h = re.shape[0] // 2
    even = table_times(jnp.concatenate([re[:h], im[:h]], 0), tab, 0)
    odd = table_times(jnp.concatenate([re[h:], im[h:]], 0), tab, 2)
    total, gap = even + odd, even - odd
    return (
        jnp.concatenate([total[:h], gap[:h]], 0),
        jnp.concatenate([total[h:], gap[h:]], 0),
    )


def forward(waves, tab):
    waves = [columns_forward(*wave, tab) for wave in waves]
    return [rows_forward(*wave, tab) for wave in waves]


def inverse(waves, tab):
    waves = [rows_inverse(*wave, tab) for wave in waves]
    return [columns_inverse(*wave, tab) for wave in waves]


def times(a, b):
    return a[0] * b[0] - a[1] * b[1], a[0] * b[1] + a[1] * b[0]


def times_conj(a, b):
    return a[0] * b[0] + a[1] * b[1], a[0] * b[1] - a[1] * b[0]


def in_groups(states, body):
    group = 2 if states % 2 == 0 else 1
    if states == group:
        body([m for m in range(group)])
        return

    def step(g, carry):
        body([g * group + m for m in range(group)])
        return carry

    lax.fori_loop(0, states // group, step, 0)


def thirds(value):
    top = value.astype(BF16)
    left = value - top.astype(F32)
    mid = left.astype(BF16)
    return top, mid, (left - mid.astype(F32)).astype(BF16)


def by_parity(value):
    size = value.shape[0]
    h = size // 2
    picks = []
    for along in (0, 1):
        place = lax.broadcasted_iota(jnp.int32, (size, size), along)
        source = lax.broadcasted_iota(jnp.int32, (size, size), 1 - along)
        wanted = jnp.where(place < h, 2 * place, 2 * (place - h) + 1)
        picks.append(jnp.where(source == wanted, 1.0, 0.0).astype(BF16))
    top, mid, low = thirds(value)
    value = (dot(picks[0], top) + dot(picks[0], mid)) + dot(picks[0], low)
    top, mid, low = thirds(value)
    return (dot(top, picks[1]) + dot(mid, picks[1])) + dot(low, picks[1])


def turned(value, row, col):
    return pltpu.roll(pltpu.roll(value, row, 0), col, 1)


def run_copies(moves, sem):
    copies = [pltpu.make_async_copy(src, dst, sem.at[i]) for i, (src, dst) in enumerate(moves)]
    for copy in copies:
        copy.start()
    return copies


def load_body(pos_hbm, probe_hbm, object_hbm, pos_out, plane_out, object_out, sem):
    plane = lax.rem(lax.axis_index("frame"), 2)
    moves = ((probe_hbm.at[0, plane], plane_out), (pos_hbm, pos_out), (object_hbm, object_out))
    for copy in run_copies(moves, sem):
        copy.wait()


def prepare_body(
    pos_hbm, probe_hbm, prop_hbm, amp_hbm, tab_hbm,
    wave_re, wave_im, amp_out, first_out, tab_out,
    pos, probe, prop, amp, sem,
):
    copies = run_copies(
        ((pos_hbm, pos), (probe_hbm, probe), (prop_hbm, prop), (amp_hbm, amp), (tab_hbm, tab_out)), sem
    )
    copies[0].wait()
    copies[1].wait()
    size = prop.shape[0]
    row, col = pos[0, 0], lax.rem(pos[0, 1], size)
    for c in range(2):
        first_out[0, c] = turned(probe[0, c], row, col)
    copies[2].wait()
    phase = by_parity(prop[...])
    wave_re[...] = jnp.cos(phase)
    wave_im[...] = jnp.sin(phase)
    copies[3].wait()
    amp_out[...] = by_parity(amp[0])
    copies[4].wait()


def turn_body(pos_ref, first_ref, *refs):
    out_ref = refs[-1]
    size = out_ref.shape[-1]
    row, col = pos_ref[0, 0], lax.rem(pos_ref[0, 1], size)
    swap = lax.rem(lax.axis_index("frame"), 2) == 1
    out_ref[:1] = first_ref[...]
    for m, (came, given) in enumerate(zip(refs[:-1:2], refs[1:-1:2])):
        for c, planes in enumerate(((came, given), (given, came))):
            out_ref[1 + m, c] = turned(jnp.where(swap, planes[1][...], planes[0][...]), row, col)


def spread(ref, which, shape):
    return jnp.broadcast_to(ref[0:1, which : which + 1], shape)


def wrapped(ref, s, part, col_ref):
    size = ref.shape[-2]
    c = lax.broadcasted_iota(jnp.int32, (size, size), 1)
    return jnp.where(c < spread(col_ref, 1, c.shape), ref[s, part, :, size:], ref[s, part, :, :size])


def send_body(before_ref, object_ref, zero_ref, one_ref):
    for s, out in enumerate((zero_ref, one_ref)):
        for part in range(2):
            out[part] = wrapped(object_ref, s, part, before_ref)


def patch_of(s, object_ref, halo_ref, pos_ref):
    size = halo_ref.shape[-1]
    r = lax.broadcasted_iota(jnp.int32, (size, size), 0)
    return [
        jnp.where(r < spread(pos_ref, 0, r.shape), halo_ref[part], wrapped(object_ref, s, part, pos_ref))
        for part in range(2)
    ]


def pair(ref, *at):
    return ref[(*at, 0)], ref[(*at, 1)]


def inner_body(pos_ref, object_ref, halo_ref, probe_ref, kr_ref, ki_ref, tab, out_ref, patch):
    states = out_ref.shape[0]
    patch[0], patch[1] = patch_of(0, object_ref, halo_ref, pos_ref)

    def body(group):
        waves = forward([times(pair(probe_ref, m), pair(patch)) for m in group], tab)
        waves = inverse([times((kr_ref[...], ki_ref[...]), wave) for wave in waves], tab)
        for m, wave in zip(group, waves):
            out_ref[m, 0], out_ref[m, 1] = wave

    in_groups(states, body)


def middle_body(rows, pos_ref, object_ref, halo_ref, inner_ref, amp_ref, tab, term_ref, chi_ref, patch, far, power):
    states = inner_ref.shape[0]
    patch[0], patch[1] = patch_of(1, object_ref, halo_ref, pos_ref)
    power[...] = jnp.zeros_like(power)

    def outward(group):
        waves = forward([times(pair(patch), pair(inner_ref, m)) for m in group], tab)
        total = power[...]
        for m, wave in zip(group, waves):
            far[m, 0], far[m, 1] = wave
            total += wave[0] * wave[0] + wave[1] * wave[1]
        power[...] = total

    in_groups(states, outward)
    power[...] = 1.0 - amp_ref[...] / jnp.sqrt(power[...] + 1.0)
    term_ref[...] = jnp.zeros_like(term_ref)
    take = pl.ds(pl.multiple_of(lax.axis_index("state") * rows, rows), rows)

    def homeward(group):
        waves = inverse([(power[...] * far[m, 0], power[...] * far[m, 1]) for m in group], tab)
        for m, wave in zip(group, waves):
            far[m, 0], far[m, 1] = wave
            chi_ref[m, 0], chi_ref[m, 1] = times_conj(pair(patch), wave)
        for m in group:
            part = times_conj(
                (inner_ref[m, 0, take], inner_ref[m, 1, take]), (far[m, 0, take], far[m, 1, take])
            )
            term_ref[0] += part[0]
            term_ref[1] += part[1]

    in_groups(states, homeward)


def last_body(rows, chi_ref, probe_ref, kr_ref, ki_ref, tab, term_ref, front):
    states = chi_ref.shape[0]
    take = pl.ds(pl.multiple_of(lax.axis_index("state") * rows, rows), rows)
    term_ref[...] = jnp.zeros_like(term_ref)

    def body(group):
        waves = forward([pair(chi_ref, m) for m in group], tab)
        waves = [rows_inverse(*times_conj((kr_ref[...], ki_ref[...]), wave), tab) for wave in waves]
        for m, wave in zip(group, waves):
            front[m, 0], front[m, 1] = wave
        for m in group:
            wave = columns_inverse(front[m, 0, take], front[m, 1, take], tab)
            part = times_conj((probe_ref[m, 0, take], probe_ref[m, 1, take]), wave)
            term_ref[0] += part[0]
            term_ref[1] += part[1]

    in_groups(states, body)


def gather_body(slice_id, rows, pos_ref, before_ref, own_ref, came_ref, *refs):
    out_ref, held, sem = refs[-3:]
    size = own_ref.shape[-1]
    start = lax.axis_index("state") * rows
    r = lax.broadcasted_iota(jnp.int32, (rows, size), 0) + start
    c = lax.broadcasted_iota(jnp.int32, (rows, size), 1)
    here, there = r >= spread(pos_ref, 0, r.shape), r < spread(before_ref, 0, r.shape)
    here_right, there_right = c < spread(pos_ref, 1, c.shape), c < spread(before_ref, 1, c.shape)
    copies = []
    for part in range(2):
        mine = jnp.where(here, own_ref[part], 0.0)
        theirs = jnp.where(there, came_ref[part], 0.0)
        held[part, :, :size] = jnp.where(here_right, 0.0, mine) + jnp.where(there_right, 0.0, theirs)
        held[part, :, size:] = jnp.where(here_right, mine, 0.0) + jnp.where(there_right, theirs, 0.0)
        copies.append(pltpu.make_async_copy(held.at[part], out_ref.at[slice_id, part], sem.at[part]))
        copies[-1].start()
    for copy in copies:
        copy.wait()


def gather(slice_id, rows, size, pos, before, own, came, *given):
    return pl.pallas_call(
        functools.partial(gather_body, slice_id, rows),
        out_shape=jax.ShapeDtypeStruct((2, 2, rows, 2 * size), F32),
        in_specs=[VMEM] * 4 + [pl.BlockSpec(memory_space=pl.ANY)] * len(given),
        out_specs=pl.BlockSpec(memory_space=pl.ANY),
        scratch_shapes=[pltpu.VMEM((2, rows, 2 * size), F32), pltpu.SemaphoreType.DMA((2,))],
        input_output_aliases={4: 0} if given else {},
        compiler_params=pltpu.CompilerParams(vmem_limit_bytes=LIMIT),
        cost_estimate=pl.CostEstimate(flops=0, bytes_accessed=32 * rows * size, transcendentals=0),
    )(pos, before, own, came, *given)


def on_device(object_slices, probe, amplitude, positions, propagator):
    states = lax.axis_size("state")
    size = amplitude.shape[1]
    rows = object_slices.shape[2] // states
    assert object_slices.shape[2:] == (size, 2 * size) and positions.shape[0] == 1
    assert lax.axis_size("frame") % 2 == 0
    return gradient_of(object_slices, probe, amplitude, positions, propagator, states, size, rows)


def gradient_of(object_slices, probe, amplitude, positions, propagator, states, size, rows):
    grid = (size, size)
    unit = size * size
    flops = 24 * size**3
    tab = tables(size)
    before = shifted(positions, "frame", 1)
    given = [in_hbm(x) for x in (positions, probe, object_slices)]
    pos, plane, held = pl.pallas_call(
        load_body,
        out_shape=[
            jax.ShapeDtypeStruct(positions.shape, jnp.int32),
            jax.ShapeDtypeStruct(grid, F32),
            jax.ShapeDtypeStruct(object_slices.shape, F32),
        ],
        in_specs=[HBM] * 3,
        out_specs=[VMEM] * 3,
        scratch_shapes=[pltpu.SemaphoreType.DMA((3,))],
        compiler_params=pltpu.CompilerParams(vmem_limit_bytes=LIMIT),
        cost_estimate=pl.CostEstimate(flops=0, bytes_accessed=40 * unit, transcendentals=0),
    )(*given)
    planes = []
    for by in range(1, states):
        planes.append(shifted(plane, "state", by))
    picked = call(send_body, [(2,) + grid] * 2, [VMEM, VMEM], moved=16 * unit)(before, held)
    halo_zero = shifted(picked[0], "frame", -1)
    halo_one = shifted(picked[1], "frame", -1)
    kr, ki, amp, first, tab = pl.pallas_call(
        prepare_body,
        out_shape=[jax.ShapeDtypeStruct(grid, F32)] * 3
        + [jax.ShapeDtypeStruct(x.shape, x.dtype) for x in (probe, tab)],
        in_specs=[HBM] * 5,
        out_specs=[VMEM] * 5,
        scratch_shapes=[
            pltpu.SMEM(positions.shape, jnp.int32),
            pltpu.VMEM(probe.shape, F32),
            pltpu.VMEM(grid, F32),
            pltpu.VMEM(amplitude.shape, F32),
            pltpu.SemaphoreType.DMA((5,)),
        ],
        compiler_params=pltpu.CompilerParams(vmem_limit_bytes=LIMIT),
        cost_estimate=pl.CostEstimate(flops=2 * size**3, bytes_accessed=60 * unit, transcendentals=0),
    )(*given[:2], *(in_hbm(x) for x in (propagator, amplitude, tab)))
    frames = lax.axis_size("frame")
    pairs = []
    for came in planes:
        pairs += [came, lax.ppermute(came, "frame", [(i, i ^ 1) for i in range(frames)])]
    (probes,) = call(
        turn_body, [(states, 2) + grid], [SMEM] + [VMEM] * (1 + len(pairs)), moved=16 * unit * (states - 1)
    )(pos, first, *pairs)

    (waves,) = call(
        inner_body,
        [(states, 2) + grid],
        [VMEM] * 7,
        [pltpu.VMEM((2,) + grid, F32)],
        flops=2 * flops * states,
        moved=16 * unit * states,
    )(pos, held, halo_zero, probes, kr, ki, tab)
    term_one, chi = call(
        functools.partial(middle_body, rows),
        [(2, rows, size), (states, 2) + grid],
        [VMEM] * 6,
        [pltpu.VMEM((2,) + grid, F32), pltpu.VMEM((states, 2) + grid, F32), pltpu.VMEM(grid, F32)],
        flops=2 * flops * states,
        moved=32 * unit * states,
    )(pos, held, halo_one, waves, amp, tab)
    came_one = shifted(term_one, "frame", 1)
    (term_zero,) = call(
        functools.partial(last_body, rows),
        [(2, rows, size)],
        [VMEM] * 5,
        [pltpu.VMEM((states, 2) + grid, F32)],
        flops=2 * flops * states,
        moved=16 * unit * states,
    )(chi, probes, kr, ki, tab)
    came_zero = shifted(term_zero, "frame", 1)
    gradient = gather(1, rows, size, pos, before, term_one, came_one)
    return gather(0, rows, size, pos, before, term_zero, came_zero, gradient)


def solution(mesh):
    return jax.shard_map(
        on_device,
        mesh=mesh,
        in_specs=(
            P(None, None, "frame", None),
            P("state", None, None, None),
            P("frame", None, None),
            P("frame", None),
            P(),
        ),
        out_specs=P(None, None, ("frame", "state"), None),
        check_vma=False,
    )
```

```python
import functools
import math

import jax
import jax.numpy as jnp
import numpy as np
from jax import lax
from jax.experimental import pallas as pl
from jax.experimental.pallas import tpu as pltpu
from jax.sharding import PartitionSpec as P


F32 = jnp.float32
BF16 = jnp.bfloat16
VMEM = pl.BlockSpec(memory_space=pltpu.VMEM)
HBM = pl.BlockSpec(memory_space=pltpu.MemorySpace.HBM)
SMEM = pl.BlockSpec(memory_space=pltpu.SMEM)
LIMIT = 24 * 1024 * 1024


def shifted(value, axis, by):
    count = lax.axis_size(axis)
    return lax.ppermute(value, axis, [(i, (i + by) % count) for i in range(count)])


def in_hbm(value):
    return pltpu.with_memory_space_constraint(value, pltpu.MemorySpace.HBM)


def call(body, outs, ins, scratch=(), flops=0, moved=0):
    return pl.pallas_call(
        body,
        out_shape=[jax.ShapeDtypeStruct(shape, F32) for shape in outs],
        in_specs=ins,
        out_specs=[VMEM] * len(outs),
        scratch_shapes=list(scratch),
        compiler_params=pltpu.CompilerParams(vmem_limit_bytes=LIMIT),
        cost_estimate=pl.CostEstimate(flops=flops, bytes_accessed=moved, transcendentals=0),
    )


def tables(length):
    half = length // 2
    n = np.arange(half)[:, None]
    forms = []
    for parity in (0, 1):
        k = 2 * np.arange(half)[None, :] + parity
        angle = -2.0 * math.pi * ((n * k) % length) / length
        re, im = np.cos(angle) / math.sqrt(length), np.sin(angle) / math.sqrt(length)
        right = np.block([[re, im], [-im, re]])
        forms += [right, right.T]
    stack = np.stack(forms).astype(np.float64)
    top = stack.astype(BF16)
    rest = (stack - top.astype(np.float64)).astype(BF16)
    return jnp.asarray(np.stack([top, rest]))


def halves(value):
    top = value.astype(BF16)
    return top, (value - top.astype(F32)).astype(BF16)


def dot(a, b):
    return lax.dot_general(a, b, (((1,), (0,)), ((), ())), preferred_element_type=F32)


def times_table(value, tab, which):
    top, rest = halves(value)
    return dot(top, tab[0, which]) + (dot(rest, tab[0, which]) + dot(top, tab[1, which]))


def table_times(value, tab, which):
    top, rest = halves(value)
    return dot(tab[0, which], top) + (dot(tab[0, which], rest) + dot(tab[1, which], top))


def columns_forward(re, im, tab):
    h = re.shape[1] // 2
    r0, r1, i0, i1 = re[:, :h], re[:, h:], im[:, :h], im[:, h:]
    even = times_table(jnp.concatenate([r0 + r1, i0 + i1], 1), tab, 0)
    odd = times_table(jnp.concatenate([r0 - r1, i0 - i1], 1), tab, 2)
    return (
        jnp.concatenate([even[:, :h], odd[:, :h]], 1),
        jnp.concatenate([even[:, h:], odd[:, h:]], 1),
    )


def columns_inverse(re, im, tab):
    h = re.shape[1] // 2
    even = times_table(jnp.concatenate([re[:, :h], im[:, :h]], 1), tab, 1)
    odd = times_table(jnp.concatenate([re[:, h:], im[:, h:]], 1), tab, 3)
    total, gap = even + odd, even - odd
    return (
        jnp.concatenate([total[:, :h], gap[:, :h]], 1),
        jnp.concatenate([total[:, h:], gap[:, h:]], 1),
    )


def rows_forward(re, im, tab):
    h = re.shape[0] // 2
    r0, r1, i0, i1 = re[:h], re[h:], im[:h], im[h:]
    even = table_times(jnp.concatenate([r0 + r1, i0 + i1], 0), tab, 1)
    odd = table_times(jnp.concatenate([r0 - r1, i0 - i1], 0), tab, 3)
    return (
        jnp.concatenate([even[:h], odd[:h]], 0),
        jnp.concatenate([even[h:], odd[h:]], 0),
    )


def rows_inverse(re, im, tab):
    h = re.shape[0] // 2
    even = table_times(jnp.concatenate([re[:h], im[:h]], 0), tab, 0)
    odd = table_times(jnp.concatenate([re[h:], im[h:]], 0), tab, 2)
    total, gap = even + odd, even - odd
    return (
        jnp.concatenate([total[:h], gap[:h]], 0),
        jnp.concatenate([total[h:], gap[h:]], 0),
    )


def forward(waves, tab):
    waves = [columns_forward(*wave, tab) for wave in waves]
    return [rows_forward(*wave, tab) for wave in waves]


def inverse(waves, tab):
    waves = [rows_inverse(*wave, tab) for wave in waves]
    return [columns_inverse(*wave, tab) for wave in waves]


def times(a, b):
    return a[0] * b[0] - a[1] * b[1], a[0] * b[1] + a[1] * b[0]


def times_conj(a, b):
    return a[0] * b[0] + a[1] * b[1], a[0] * b[1] - a[1] * b[0]


def in_groups(states, body):
    group = 2 if states % 2 == 0 else 1
    if states == group:
        body([m for m in range(group)])
        return

    def step(g, carry):
        body([g * group + m for m in range(group)])
        return carry

    lax.fori_loop(0, states // group, step, 0)


def thirds(value):
    top = value.astype(BF16)
    left = value - top.astype(F32)
    mid = left.astype(BF16)
    return top, mid, (left - mid.astype(F32)).astype(BF16)


def by_parity(value):
    size = value.shape[0]
    h = size // 2
    picks = []
    for along in (0, 1):
        place = lax.broadcasted_iota(jnp.int32, (size, size), along)
        source = lax.broadcasted_iota(jnp.int32, (size, size), 1 - along)
        wanted = jnp.where(place < h, 2 * place, 2 * (place - h) + 1)
        picks.append(jnp.where(source == wanted, 1.0, 0.0).astype(BF16))
    top, mid, low = thirds(value)
    value = (dot(picks[0], top) + dot(picks[0], mid)) + dot(picks[0], low)
    top, mid, low = thirds(value)
    return (dot(top, picks[1]) + dot(mid, picks[1])) + dot(low, picks[1])


def turned(value, row, col):
    return pltpu.roll(pltpu.roll(value, row, 0), col, 1)


def run_copies(moves, sem):
    copies = [pltpu.make_async_copy(src, dst, sem.at[i]) for i, (src, dst) in enumerate(moves)]
    for copy in copies:
        copy.start()
    return copies


def load_body(pos_hbm, probe_hbm, object_hbm, pos_out, plane_out, object_out, sem):
    plane = lax.rem(lax.axis_index("frame"), 2)
    half = object_hbm.shape[2] // 2
    moves = [(pos_hbm, pos_out)]
    for s in range(2):
        for part in range(2):
            for at in (pl.ds(0, half), pl.ds(half, half)):
                moves.append((object_hbm.at[s, part, at], object_out.at[s, part, at]))
    moves.append((probe_hbm.at[0, plane], plane_out))
    for copy in run_copies(moves, sem):
        copy.wait()


def prepare_body(
    pos_hbm, probe_hbm, prop_hbm, amp_hbm, tab_hbm,
    wave_re, wave_im, amp_out, first_out, tab_out,
    pos, probe, prop, amp, sem,
):
    copies = run_copies(
        ((pos_hbm, pos), (probe_hbm, probe), (prop_hbm, prop), (amp_hbm, amp), (tab_hbm, tab_out)), sem
    )
    copies[0].wait()
    copies[1].wait()
    size = prop.shape[0]
    row, col = pos[0, 0], lax.rem(pos[0, 1], size)
    for c in range(2):
        first_out[0, c] = turned(probe[0, c], row, col)
    copies[2].wait()
    phase = by_parity(prop[...])
    wave_re[...] = jnp.cos(phase)
    wave_im[...] = jnp.sin(phase)
    copies[3].wait()
    amp_out[...] = by_parity(amp[0])
    copies[4].wait()


def turn_body(pos_ref, first_ref, *refs):
    out_ref = refs[-1]
    size = out_ref.shape[-1]
    row, col = pos_ref[0, 0], lax.rem(pos_ref[0, 1], size)
    swap = lax.rem(lax.axis_index("frame"), 2) == 1
    out_ref[:1] = first_ref[...]
    for m, (came, given) in enumerate(zip(refs[:-1:2], refs[1:-1:2])):
        for c, planes in enumerate(((came, given), (given, came))):
            out_ref[1 + m, c] = turned(jnp.where(swap, planes[1][...], planes[0][...]), row, col)


def spread(ref, which, shape):
    return jnp.broadcast_to(ref[0:1, which : which + 1], shape)


def wrapped(ref, s, part, col_ref):
    size = ref.shape[-2]
    c = lax.broadcasted_iota(jnp.int32, (size, size), 1)
    return jnp.where(c < spread(col_ref, 1, c.shape), ref[s, part, :, size:], ref[s, part, :, :size])


def send_body(before_ref, object_ref, zero_ref, one_ref):
    for s, out in enumerate((zero_ref, one_ref)):
        for part in range(2):
            out[part] = wrapped(object_ref, s, part, before_ref)


def patch_of(s, object_ref, halo_ref, pos_ref):
    size = halo_ref.shape[-1]
    r = lax.broadcasted_iota(jnp.int32, (size, size), 0)
    return [
        jnp.where(r < spread(pos_ref, 0, r.shape), halo_ref[part], wrapped(object_ref, s, part, pos_ref))
        for part in range(2)
    ]


def pair(ref, *at):
    return ref[(*at, 0)], ref[(*at, 1)]


def inner_body(pos_ref, object_ref, halo_ref, probe_ref, kr_ref, ki_ref, tab, out_ref, patch):
    states = out_ref.shape[0]
    patch[0], patch[1] = patch_of(0, object_ref, halo_ref, pos_ref)

    def body(group):
        waves = forward([times(pair(probe_ref, m), pair(patch)) for m in group], tab)
        waves = inverse([times((kr_ref[...], ki_ref[...]), wave) for wave in waves], tab)
        for m, wave in zip(group, waves):
            out_ref[m, 0], out_ref[m, 1] = wave

    in_groups(states, body)


def middle_body(rows, pos_ref, object_ref, halo_ref, inner_ref, amp_ref, tab, term_ref, chi_ref, patch, far, power):
    states = inner_ref.shape[0]
    patch[0], patch[1] = patch_of(1, object_ref, halo_ref, pos_ref)
    power[...] = jnp.zeros_like(power)

    def outward(group):
        waves = forward([times(pair(patch), pair(inner_ref, m)) for m in group], tab)
        total = power[...]
        for m, wave in zip(group, waves):
            far[m, 0], far[m, 1] = wave
            total += wave[0] * wave[0] + wave[1] * wave[1]
        power[...] = total

    in_groups(states, outward)
    power[...] = 1.0 - amp_ref[...] / jnp.sqrt(power[...] + 1.0)
    term_ref[...] = jnp.zeros_like(term_ref)
    take = pl.ds(pl.multiple_of(lax.axis_index("state") * rows, rows), rows)

    def homeward(group):
        waves = inverse([(power[...] * far[m, 0], power[...] * far[m, 1]) for m in group], tab)
        for m, wave in zip(group, waves):
            far[m, 0], far[m, 1] = wave
            chi_ref[m, 0], chi_ref[m, 1] = times_conj(pair(patch), wave)
        for m in group:
            part = times_conj(
                (inner_ref[m, 0, take], inner_ref[m, 1, take]), (far[m, 0, take], far[m, 1, take])
            )
            term_ref[0] += part[0]
            term_ref[1] += part[1]

    in_groups(states, homeward)


def last_body(rows, chi_ref, probe_ref, kr_ref, ki_ref, tab, term_ref, front):
    states = chi_ref.shape[0]
    take = pl.ds(pl.multiple_of(lax.axis_index("state") * rows, rows), rows)
    term_ref[...] = jnp.zeros_like(term_ref)

    def body(group):
        waves = forward([pair(chi_ref, m) for m in group], tab)
        waves = [rows_inverse(*times_conj((kr_ref[...], ki_ref[...]), wave), tab) for wave in waves]
        for m, wave in zip(group, waves):
            front[m, 0], front[m, 1] = wave
        for m in group:
            wave = columns_inverse(front[m, 0, take], front[m, 1, take], tab)
            part = times_conj((probe_ref[m, 0, take], probe_ref[m, 1, take]), wave)
            term_ref[0] += part[0]
            term_ref[1] += part[1]

    in_groups(states, body)


def gather_body(slice_id, rows, pos_ref, before_ref, own_ref, came_ref, *refs):
    out_ref, held, sem = refs[-3:]
    size = own_ref.shape[-1]
    start = lax.axis_index("state") * rows
    r = lax.broadcasted_iota(jnp.int32, (rows, size), 0) + start
    c = lax.broadcasted_iota(jnp.int32, (rows, size), 1)
    here, there = r >= spread(pos_ref, 0, r.shape), r < spread(before_ref, 0, r.shape)
    here_right, there_right = c < spread(pos_ref, 1, c.shape), c < spread(before_ref, 1, c.shape)
    copies = []
    for part in range(2):
        mine = jnp.where(here, own_ref[part], 0.0)
        theirs = jnp.where(there, came_ref[part], 0.0)
        held[part, :, :size] = jnp.where(here_right, 0.0, mine) + jnp.where(there_right, 0.0, theirs)
        held[part, :, size:] = jnp.where(here_right, mine, 0.0) + jnp.where(there_right, theirs, 0.0)
        copies.append(pltpu.make_async_copy(held.at[part], out_ref.at[slice_id, part], sem.at[part]))
        copies[-1].start()
    for copy in copies:
        copy.wait()


def gather(slice_id, rows, size, pos, before, own, came, *given):
    return pl.pallas_call(
        functools.partial(gather_body, slice_id, rows),
        out_shape=jax.ShapeDtypeStruct((2, 2, rows, 2 * size), F32),
        in_specs=[VMEM] * 4 + [pl.BlockSpec(memory_space=pl.ANY)] * len(given),
        out_specs=pl.BlockSpec(memory_space=pl.ANY),
        scratch_shapes=[pltpu.VMEM((2, rows, 2 * size), F32), pltpu.SemaphoreType.DMA((2,))],
        input_output_aliases={4: 0} if given else {},
        compiler_params=pltpu.CompilerParams(vmem_limit_bytes=LIMIT),
        cost_estimate=pl.CostEstimate(flops=0, bytes_accessed=32 * rows * size, transcendentals=0),
    )(pos, before, own, came, *given)


def on_device(object_slices, probe, amplitude, positions, propagator):
    states = lax.axis_size("state")
    size = amplitude.shape[1]
    rows = object_slices.shape[2] // states
    assert object_slices.shape[2:] == (size, 2 * size) and positions.shape[0] == 1
    assert lax.axis_size("frame") % 2 == 0
    return gradient_of(object_slices, probe, amplitude, positions, propagator, states, size, rows)


def gradient_of(object_slices, probe, amplitude, positions, propagator, states, size, rows):
    grid = (size, size)
    unit = size * size
    flops = 24 * size**3
    tab = tables(size)
    before = shifted(positions, "frame", 1)
    given = [in_hbm(x) for x in (positions, probe, object_slices)]
    pos, plane, held = pl.pallas_call(
        load_body,
        out_shape=[
            jax.ShapeDtypeStruct(positions.shape, jnp.int32),
            jax.ShapeDtypeStruct(grid, F32),
            jax.ShapeDtypeStruct(object_slices.shape, F32),
        ],
        in_specs=[HBM] * 3,
        out_specs=[VMEM] * 3,
        scratch_shapes=[pltpu.SemaphoreType.DMA((10,))],
        compiler_params=pltpu.CompilerParams(vmem_limit_bytes=LIMIT),
        cost_estimate=pl.CostEstimate(flops=0, bytes_accessed=40 * unit, transcendentals=0),
    )(*given)
    picked = call(send_body, [(2,) + grid] * 2, [VMEM, VMEM], moved=16 * unit)(before, held)
    halo_zero = shifted(picked[0], "frame", -1)
    halo_one = shifted(picked[1], "frame", -1)
    planes = []
    for by in range(1, states):
        planes.append(shifted(plane, "state", by))
    kr, ki, amp, first, tab = pl.pallas_call(
        prepare_body,
        out_shape=[jax.ShapeDtypeStruct(grid, F32)] * 3
        + [jax.ShapeDtypeStruct(x.shape, x.dtype) for x in (probe, tab)],
        in_specs=[HBM] * 5,
        out_specs=[VMEM] * 5,
        scratch_shapes=[
            pltpu.SMEM(positions.shape, jnp.int32),
            pltpu.VMEM(probe.shape, F32),
            pltpu.VMEM(grid, F32),
            pltpu.VMEM(amplitude.shape, F32),
            pltpu.SemaphoreType.DMA((5,)),
        ],
        compiler_params=pltpu.CompilerParams(vmem_limit_bytes=LIMIT),
        cost_estimate=pl.CostEstimate(flops=2 * size**3, bytes_accessed=60 * unit, transcendentals=0),
    )(*given[:2], *(in_hbm(x) for x in (propagator, amplitude, tab)))
    frames = lax.axis_size("frame")
    pairs = []
    for came in planes:
        pairs += [came, lax.ppermute(came, "frame", [(i, i ^ 1) for i in range(frames)])]
    (probes,) = call(
        turn_body, [(states, 2) + grid], [SMEM] + [VMEM] * (1 + len(pairs)), moved=16 * unit * (states - 1)
    )(pos, first, *pairs)

    (waves,) = call(
        inner_body,
        [(states, 2) + grid],
        [VMEM] * 7,
        [pltpu.VMEM((2,) + grid, F32)],
        flops=2 * flops * states,
        moved=16 * unit * states,
    )(pos, held, halo_zero, probes, kr, ki, tab)
    term_one, chi = call(
        functools.partial(middle_body, rows),
        [(2, rows, size), (states, 2) + grid],
        [VMEM] * 6,
        [pltpu.VMEM((2,) + grid, F32), pltpu.VMEM((states, 2) + grid, F32), pltpu.VMEM(grid, F32)],
        flops=2 * flops * states,
        moved=32 * unit * states,
    )(pos, held, halo_one, waves, amp, tab)
    came_one = shifted(term_one, "frame", 1)
    (term_zero,) = call(
        functools.partial(last_body, rows),
        [(2, rows, size)],
        [VMEM] * 5,
        [pltpu.VMEM((states, 2) + grid, F32)],
        flops=2 * flops * states,
        moved=16 * unit * states,
    )(chi, probes, kr, ki, tab)
    came_zero = shifted(term_zero, "frame", 1)
    gradient = gather(1, rows, size, pos, before, term_one, came_one)
    return gather(0, rows, size, pos, before, term_zero, came_zero, gradient)


def solution(mesh):
    return jax.shard_map(
        on_device,
        mesh=mesh,
        in_specs=(
            P(None, None, "frame", None),
            P("state", None, None, None),
            P("frame", None, None),
            P("frame", None),
            P(),
        ),
        out_specs=P(None, None, ("frame", "state"), None),
        check_vma=False,
    )
```

```python
import functools
import math

import jax
import jax.numpy as jnp
import numpy as np
from jax import lax
from jax.experimental import pallas as pl
from jax.experimental.pallas import tpu as pltpu
from jax.sharding import PartitionSpec as P


F32 = jnp.float32
BF16 = jnp.bfloat16
VMEM = pl.BlockSpec(memory_space=pltpu.VMEM)
HBM = pl.BlockSpec(memory_space=pltpu.MemorySpace.HBM)
SMEM = pl.BlockSpec(memory_space=pltpu.SMEM)
LIMIT = 24 * 1024 * 1024


def shifted(value, axis, by):
    count = lax.axis_size(axis)
    return lax.ppermute(value, axis, [(i, (i + by) % count) for i in range(count)])


def in_hbm(value):
    return pltpu.with_memory_space_constraint(value, pltpu.MemorySpace.HBM)


def call(body, outs, ins, scratch=(), flops=0, moved=0):
    return pl.pallas_call(
        body,
        out_shape=[jax.ShapeDtypeStruct(shape, F32) for shape in outs],
        in_specs=ins,
        out_specs=[VMEM] * len(outs),
        scratch_shapes=list(scratch),
        compiler_params=pltpu.CompilerParams(vmem_limit_bytes=LIMIT),
        cost_estimate=pl.CostEstimate(flops=flops, bytes_accessed=moved, transcendentals=0),
    )


def tables(length):
    half = length // 2
    n = np.arange(half)[:, None]
    forms = []
    for parity in (0, 1):
        k = 2 * np.arange(half)[None, :] + parity
        angle = -2.0 * math.pi * ((n * k) % length) / length
        re, im = np.cos(angle) / math.sqrt(length), np.sin(angle) / math.sqrt(length)
        right = np.block([[re, im], [-im, re]])
        forms += [right, right.T]
    stack = np.stack(forms).astype(np.float64)
    top = stack.astype(BF16)
    rest = (stack - top.astype(np.float64)).astype(BF16)
    return jnp.asarray(np.stack([top, rest]))


def halves(value):
    top = value.astype(BF16)
    return top, (value - top.astype(F32)).astype(BF16)


def dot(a, b):
    return lax.dot_general(a, b, (((1,), (0,)), ((), ())), preferred_element_type=F32)


def times_table(value, tab, which):
    top, rest = halves(value)
    return dot(top, tab[0, which]) + (dot(rest, tab[0, which]) + dot(top, tab[1, which]))


def table_times(value, tab, which):
    top, rest = halves(value)
    return dot(tab[0, which], top) + (dot(tab[0, which], rest) + dot(tab[1, which], top))


def columns_forward(re, im, tab):
    h = re.shape[1] // 2
    r0, r1, i0, i1 = re[:, :h], re[:, h:], im[:, :h], im[:, h:]
    even = times_table(jnp.concatenate([r0 + r1, i0 + i1], 1), tab, 0)
    odd = times_table(jnp.concatenate([r0 - r1, i0 - i1], 1), tab, 2)
    return (
        jnp.concatenate([even[:, :h], odd[:, :h]], 1),
        jnp.concatenate([even[:, h:], odd[:, h:]], 1),
    )


def columns_inverse(re, im, tab):
    h = re.shape[1] // 2
    even = times_table(jnp.concatenate([re[:, :h], im[:, :h]], 1), tab, 1)
    odd = times_table(jnp.concatenate([re[:, h:], im[:, h:]], 1), tab, 3)
    total, gap = even + odd, even - odd
    return (
        jnp.concatenate([total[:, :h], gap[:, :h]], 1),
        jnp.concatenate([total[:, h:], gap[:, h:]], 1),
    )


def rows_forward(re, im, tab):
    h = re.shape[0] // 2
    r0, r1, i0, i1 = re[:h], re[h:], im[:h], im[h:]
    even = table_times(jnp.concatenate([r0 + r1, i0 + i1], 0), tab, 1)
    odd = table_times(jnp.concatenate([r0 - r1, i0 - i1], 0), tab, 3)
    return (
        jnp.concatenate([even[:h], odd[:h]], 0),
        jnp.concatenate([even[h:], odd[h:]], 0),
    )


def rows_inverse(re, im, tab):
    h = re.shape[0] // 2
    even = table_times(jnp.concatenate([re[:h], im[:h]], 0), tab, 0)
    odd = table_times(jnp.concatenate([re[h:], im[h:]], 0), tab, 2)
    total, gap = even + odd, even - odd
    return (
        jnp.concatenate([total[:h], gap[:h]], 0),
        jnp.concatenate([total[h:], gap[h:]], 0),
    )


def forward(waves, tab):
    waves = [columns_forward(*wave, tab) for wave in waves]
    return [rows_forward(*wave, tab) for wave in waves]


def inverse(waves, tab):
    waves = [rows_inverse(*wave, tab) for wave in waves]
    return [columns_inverse(*wave, tab) for wave in waves]


def times(a, b):
    return a[0] * b[0] - a[1] * b[1], a[0] * b[1] + a[1] * b[0]


def times_conj(a, b):
    return a[0] * b[0] + a[1] * b[1], a[0] * b[1] - a[1] * b[0]


def in_groups(states, body):
    group = 2 if states % 2 == 0 else 1
    if states == group:
        body([m for m in range(group)])
        return

    def step(g, carry):
        body([g * group + m for m in range(group)])
        return carry

    lax.fori_loop(0, states // group, step, 0)


def thirds(value):
    top = value.astype(BF16)
    left = value - top.astype(F32)
    mid = left.astype(BF16)
    return top, mid, (left - mid.astype(F32)).astype(BF16)


def by_parity(value):
    size = value.shape[0]
    h = size // 2
    picks = []
    for along in (0, 1):
        place = lax.broadcasted_iota(jnp.int32, (size, size), along)
        source = lax.broadcasted_iota(jnp.int32, (size, size), 1 - along)
        wanted = jnp.where(place < h, 2 * place, 2 * (place - h) + 1)
        picks.append(jnp.where(source == wanted, 1.0, 0.0).astype(BF16))
    top, mid, low = thirds(value)
    value = (dot(picks[0], top) + dot(picks[0], mid)) + dot(picks[0], low)
    top, mid, low = thirds(value)
    return (dot(top, picks[1]) + dot(mid, picks[1])) + dot(low, picks[1])


def turned(value, row, col):
    return pltpu.roll(pltpu.roll(value, row, 0), col, 1)


def run_copies(moves, sem):
    copies = [pltpu.make_async_copy(src, dst, sem.at[i]) for i, (src, dst) in enumerate(moves)]
    for copy in copies:
        copy.start()
    return copies


def load_body(pos_hbm, probe_hbm, object_hbm, pos_out, plane_out, object_out, sem):
    which = lax.rem(lax.axis_index("frame"), 2)
    half = object_hbm.shape[2] // 2
    moves = [(probe_hbm.at[0, which], plane_out), (pos_hbm, pos_out)]
    for s in range(2):
        for part in range(2):
            for at in (pl.ds(0, half), pl.ds(half, half)):
                moves.append((object_hbm.at[s, part, at], object_out.at[s, part, at]))
    for copy in run_copies(moves, sem):
        copy.wait()


def turn_body(pos_ref, *refs):
    half = len(refs) // 2
    for came, out in zip(refs[:half], refs[half:]):
        out[...] = turned(came[...], pos_ref[0, 0], lax.rem(pos_ref[0, 1], came.shape[1]))


def prepare_body(
    pos_hbm, probe_hbm, prop_hbm, amp_hbm, tab_hbm,
    wave_re, wave_im, amp_out, first_out, tab_out,
    pos, probe, prop, amp, sem,
):
    copies = run_copies(
        ((pos_hbm, pos), (probe_hbm, probe), (prop_hbm, prop), (amp_hbm, amp), (tab_hbm, tab_out)), sem
    )
    copies[0].wait()
    copies[1].wait()
    size = prop.shape[0]
    row, col = pos[0, 0], lax.rem(pos[0, 1], size)
    for c in range(2):
        first_out[0, c] = turned(probe[0, c], row, col)
    copies[2].wait()
    phase = by_parity(prop[...])
    wave_re[...] = jnp.cos(phase)
    wave_im[...] = jnp.sin(phase)
    copies[3].wait()
    amp_out[...] = by_parity(amp[0])
    copies[4].wait()


def spread(ref, which, shape):
    return jnp.broadcast_to(ref[0:1, which : which + 1], shape)


def wrapped(ref, s, part, col_ref):
    size = ref.shape[-2]
    c = lax.broadcasted_iota(jnp.int32, (size, size), 1)
    return jnp.where(c < spread(col_ref, 1, c.shape), ref[s, part, :, size:], ref[s, part, :, :size])


def send_body(before_ref, object_ref, zero_ref, one_ref):
    for s, out in enumerate((zero_ref, one_ref)):
        for part in range(2):
            out[part] = wrapped(object_ref, s, part, before_ref)


def patch_of(s, object_ref, halo_ref, pos_ref):
    size = halo_ref.shape[-1]
    r = lax.broadcasted_iota(jnp.int32, (size, size), 0)
    return [
        jnp.where(r < spread(pos_ref, 0, r.shape), halo_ref[part], wrapped(object_ref, s, part, pos_ref))
        for part in range(2)
    ]


def pair(ref, *at):
    return ref[(*at, 0)], ref[(*at, 1)]


def inner_body(pos, pos_ref, object_ref, halo_ref, first_ref, kr_ref, ki_ref, tab, *refs):
    out_ref, probe_ref, patch = refs[-3:]
    states = out_ref.shape[0]
    patch[0], patch[1] = patch_of(0, object_ref, halo_ref, pos_ref)
    swap = lax.rem(lax.axis_index("frame"), 2) == 1
    probe_ref[:1] = first_ref[...]
    for m, (came, given) in enumerate(zip(refs[:-3:2], refs[1:-3:2])):
        other = turned(given[...], pos[0, 0], lax.rem(pos[0, 1], given.shape[1]))
        probe_ref[1 + m, 0] = jnp.where(swap, other, came[...])
        probe_ref[1 + m, 1] = jnp.where(swap, came[...], other)

    def body(group):
        waves = forward([times(pair(probe_ref, m), pair(patch)) for m in group], tab)
        waves = inverse([times((kr_ref[...], ki_ref[...]), wave) for wave in waves], tab)
        for m, wave in zip(group, waves):
            out_ref[m, 0], out_ref[m, 1] = wave

    in_groups(states, body)


def middle_body(rows, pos_ref, object_ref, halo_ref, inner_ref, amp_ref, tab, term_ref, chi_ref, patch, far, power):
    states = inner_ref.shape[0]
    patch[0], patch[1] = patch_of(1, object_ref, halo_ref, pos_ref)
    power[...] = jnp.zeros_like(power)

    def outward(group):
        waves = forward([times(pair(patch), pair(inner_ref, m)) for m in group], tab)
        total = power[...]
        for m, wave in zip(group, waves):
            far[m, 0], far[m, 1] = wave
            total += wave[0] * wave[0] + wave[1] * wave[1]
        power[...] = total

    in_groups(states, outward)
    power[...] = 1.0 - amp_ref[...] / jnp.sqrt(power[...] + 1.0)
    term_ref[...] = jnp.zeros_like(term_ref)
    take = pl.ds(pl.multiple_of(lax.axis_index("state") * rows, rows), rows)

    def homeward(group):
        waves = inverse([(power[...] * far[m, 0], power[...] * far[m, 1]) for m in group], tab)
        for m, wave in zip(group, waves):
            far[m, 0], far[m, 1] = wave
            chi_ref[m, 0], chi_ref[m, 1] = times_conj(pair(patch), wave)
        for m in group:
            part = times_conj(
                (inner_ref[m, 0, take], inner_ref[m, 1, take]), (far[m, 0, take], far[m, 1, take])
            )
            term_ref[0] += part[0]
            term_ref[1] += part[1]

    in_groups(states, homeward)


def last_body(rows, chi_ref, probe_ref, kr_ref, ki_ref, tab, term_ref, front):
    states = chi_ref.shape[0]
    take = pl.ds(pl.multiple_of(lax.axis_index("state") * rows, rows), rows)
    term_ref[...] = jnp.zeros_like(term_ref)

    def body(group):
        waves = forward([pair(chi_ref, m) for m in group], tab)
        waves = [rows_inverse(*times_conj((kr_ref[...], ki_ref[...]), wave), tab) for wave in waves]
        for m, wave in zip(group, waves):
            front[m, 0], front[m, 1] = wave
        for m in group:
            wave = columns_inverse(front[m, 0, take], front[m, 1, take], tab)
            part = times_conj((probe_ref[m, 0, take], probe_ref[m, 1, take]), wave)
            term_ref[0] += part[0]
            term_ref[1] += part[1]

    in_groups(states, body)


def gather_body(slice_id, rows, pos_ref, before_ref, own_ref, came_ref, *refs):
    out_ref, held, sem = refs[-3:]
    size = own_ref.shape[-1]
    start = lax.axis_index("state") * rows
    r = lax.broadcasted_iota(jnp.int32, (rows, size), 0) + start
    c = lax.broadcasted_iota(jnp.int32, (rows, size), 1)
    here, there = r >= spread(pos_ref, 0, r.shape), r < spread(before_ref, 0, r.shape)
    here_right, there_right = c < spread(pos_ref, 1, c.shape), c < spread(before_ref, 1, c.shape)
    copies = []
    for part in range(2):
        mine = jnp.where(here, own_ref[part], 0.0)
        theirs = jnp.where(there, came_ref[part], 0.0)
        held[part, :, :size] = jnp.where(here_right, 0.0, mine) + jnp.where(there_right, 0.0, theirs)
        held[part, :, size:] = jnp.where(here_right, mine, 0.0) + jnp.where(there_right, theirs, 0.0)
        copies.append(pltpu.make_async_copy(held.at[part], out_ref.at[slice_id, part], sem.at[part]))
        copies[-1].start()
    for copy in copies:
        copy.wait()


def gather(slice_id, rows, size, pos, before, own, came, *given):
    return pl.pallas_call(
        functools.partial(gather_body, slice_id, rows),
        out_shape=jax.ShapeDtypeStruct((2, 2, rows, 2 * size), F32),
        in_specs=[VMEM] * 4 + [pl.BlockSpec(memory_space=pl.ANY)] * len(given),
        out_specs=pl.BlockSpec(memory_space=pl.ANY),
        scratch_shapes=[pltpu.VMEM((2, rows, 2 * size), F32), pltpu.SemaphoreType.DMA((2,))],
        input_output_aliases={4: 0} if given else {},
        compiler_params=pltpu.CompilerParams(vmem_limit_bytes=LIMIT),
        cost_estimate=pl.CostEstimate(flops=0, bytes_accessed=32 * rows * size, transcendentals=0),
    )(pos, before, own, came, *given)


def on_device(object_slices, probe, amplitude, positions, propagator):
    states = lax.axis_size("state")
    size = amplitude.shape[1]
    rows = object_slices.shape[2] // states
    assert object_slices.shape[2:] == (size, 2 * size) and positions.shape[0] == 1
    assert lax.axis_size("frame") % 2 == 0
    return gradient_of(object_slices, probe, amplitude, positions, propagator, states, size, rows)


def gradient_of(object_slices, probe, amplitude, positions, propagator, states, size, rows):
    grid = (size, size)
    unit = size * size
    flops = 24 * size**3
    tab = tables(size)
    before = shifted(positions, "frame", 1)
    given = [in_hbm(x) for x in (positions, probe, object_slices)]
    pos, plane, held = pl.pallas_call(
        load_body,
        out_shape=[
            jax.ShapeDtypeStruct(positions.shape, jnp.int32),
            jax.ShapeDtypeStruct(grid, F32),
            jax.ShapeDtypeStruct(object_slices.shape, F32),
        ],
        in_specs=[HBM] * 3,
        out_specs=[VMEM] * 3,
        scratch_shapes=[pltpu.SemaphoreType.DMA((10,))],
        compiler_params=pltpu.CompilerParams(vmem_limit_bytes=LIMIT),
        cost_estimate=pl.CostEstimate(flops=0, bytes_accessed=40 * unit, transcendentals=0),
    )(*given)
    picked = call(send_body, [(2,) + grid] * 2, [VMEM, VMEM], moved=16 * unit)(before, held)
    halo_zero = shifted(picked[0], "frame", -1)
    halo_one = shifted(picked[1], "frame", -1)
    planes = []
    for by in range(1, states):
        planes.append(shifted(plane, "state", by))
    kr, ki, amp, first, tab = pl.pallas_call(
        prepare_body,
        out_shape=[jax.ShapeDtypeStruct(grid, F32)] * 3
        + [jax.ShapeDtypeStruct(x.shape, x.dtype) for x in (probe, tab)],
        in_specs=[HBM] * 5,
        out_specs=[VMEM] * 5,
        scratch_shapes=[
            pltpu.SMEM(positions.shape, jnp.int32),
            pltpu.VMEM(probe.shape, F32),
            pltpu.VMEM(grid, F32),
            pltpu.VMEM(amplitude.shape, F32),
            pltpu.SemaphoreType.DMA((5,)),
        ],
        compiler_params=pltpu.CompilerParams(vmem_limit_bytes=LIMIT),
        cost_estimate=pl.CostEstimate(flops=2 * size**3, bytes_accessed=60 * unit, transcendentals=0),
    )(*given[:2], *(in_hbm(x) for x in (propagator, amplitude, tab)))
    frames = lax.axis_size("frame")
    own = call(turn_body, [grid] * len(planes), [SMEM] + [VMEM] * len(planes), moved=16 * unit)(pos, *planes)
    pairs = []
    for came, kept in zip(planes, own):
        pairs += [kept, lax.ppermute(came, "frame", [(i, i ^ 1) for i in range(frames)])]
    waves, probes = call(
        inner_body,
        [(states, 2) + grid] * 2,
        [SMEM] + [VMEM] * (7 + len(pairs)),
        [pltpu.VMEM((2,) + grid, F32)],
        flops=2 * flops * states,
        moved=24 * unit * states,
    )(pos, pos, held, halo_zero, first, kr, ki, tab, *pairs)
    term_one, chi = call(
        functools.partial(middle_body, rows),
        [(2, rows, size), (states, 2) + grid],
        [VMEM] * 6,
        [pltpu.VMEM((2,) + grid, F32), pltpu.VMEM((states, 2) + grid, F32), pltpu.VMEM(grid, F32)],
        flops=2 * flops * states,
        moved=32 * unit * states,
    )(pos, held, halo_one, waves, amp, tab)
    came_one = shifted(term_one, "frame", 1)
    (term_zero,) = call(
        functools.partial(last_body, rows),
        [(2, rows, size)],
        [VMEM] * 5,
        [pltpu.VMEM((states, 2) + grid, F32)],
        flops=2 * flops * states,
        moved=16 * unit * states,
    )(chi, probes, kr, ki, tab)
    came_zero = shifted(term_zero, "frame", 1)
    gradient = gather(1, rows, size, pos, before, term_one, came_one)
    return gather(0, rows, size, pos, before, term_zero, came_zero, gradient)


def solution(mesh):
    return jax.shard_map(
        on_device,
        mesh=mesh,
        in_specs=(
            P(None, None, "frame", None),
            P("state", None, None, None),
            P("frame", None, None),
            P("frame", None),
            P(),
        ),
        out_specs=P(None, None, ("frame", "state"), None),
        check_vma=False,
    )
```

```python
import functools
import math

import jax
import jax.numpy as jnp
import numpy as np
from jax import lax
from jax.experimental import pallas as pl
from jax.experimental.pallas import tpu as pltpu
from jax.sharding import PartitionSpec as P


F32 = jnp.float32
BF16 = jnp.bfloat16
VMEM = pl.BlockSpec(memory_space=pltpu.VMEM)
HBM = pl.BlockSpec(memory_space=pltpu.MemorySpace.HBM)
SMEM = pl.BlockSpec(memory_space=pltpu.SMEM)
LIMIT = 24 * 1024 * 1024


def shifted(value, axis, by):
    count = lax.axis_size(axis)
    return lax.ppermute(value, axis, [(i, (i + by) % count) for i in range(count)])


def in_hbm(value):
    return pltpu.with_memory_space_constraint(value, pltpu.MemorySpace.HBM)


def call(body, outs, ins, scratch=(), flops=0, moved=0):
    return pl.pallas_call(
        body,
        out_shape=[jax.ShapeDtypeStruct(shape, F32) for shape in outs],
        in_specs=ins,
        out_specs=[VMEM] * len(outs),
        scratch_shapes=list(scratch),
        compiler_params=pltpu.CompilerParams(vmem_limit_bytes=LIMIT),
        cost_estimate=pl.CostEstimate(flops=flops, bytes_accessed=moved, transcendentals=0),
    )


def tables(length):
    half = length // 2
    n = np.arange(half)[:, None]
    forms = []
    for parity in (0, 1):
        k = 2 * np.arange(half)[None, :] + parity
        angle = -2.0 * math.pi * ((n * k) % length) / length
        re, im = np.cos(angle) / math.sqrt(length), np.sin(angle) / math.sqrt(length)
        right = np.block([[re, im], [-im, re]])
        forms += [right, right.T]
    stack = np.stack(forms).astype(np.float64)
    top = stack.astype(BF16)
    rest = (stack - top.astype(np.float64)).astype(BF16)
    return jnp.asarray(np.stack([top, rest]))


def halves(value):
    top = value.astype(BF16)
    return top, (value - top.astype(F32)).astype(BF16)


def dot(a, b):
    return lax.dot_general(a, b, (((1,), (0,)), ((), ())), preferred_element_type=F32)


def times_table(value, tab, which):
    top, rest = halves(value)
    return dot(top, tab[0, which]) + (dot(rest, tab[0, which]) + dot(top, tab[1, which]))


def table_times(value, tab, which):
    top, rest = halves(value)
    return dot(tab[0, which], top) + (dot(tab[0, which], rest) + dot(tab[1, which], top))


def columns_forward(re, im, tab):
    h = re.shape[1] // 2
    r0, r1, i0, i1 = re[:, :h], re[:, h:], im[:, :h], im[:, h:]
    even = times_table(jnp.concatenate([r0 + r1, i0 + i1], 1), tab, 0)
    odd = times_table(jnp.concatenate([r0 - r1, i0 - i1], 1), tab, 2)
    return (
        jnp.concatenate([even[:, :h], odd[:, :h]], 1),
        jnp.concatenate([even[:, h:], odd[:, h:]], 1),
    )


def columns_inverse(re, im, tab):
    h = re.shape[1] // 2
    even = times_table(jnp.concatenate([re[:, :h], im[:, :h]], 1), tab, 1)
    odd = times_table(jnp.concatenate([re[:, h:], im[:, h:]], 1), tab, 3)
    total, gap = even + odd, even - odd
    return (
        jnp.concatenate([total[:, :h], gap[:, :h]], 1),
        jnp.concatenate([total[:, h:], gap[:, h:]], 1),
    )


def rows_forward(re, im, tab):
    h = re.shape[0] // 2
    r0, r1, i0, i1 = re[:h], re[h:], im[:h], im[h:]
    even = table_times(jnp.concatenate([r0 + r1, i0 + i1], 0), tab, 1)
    odd = table_times(jnp.concatenate([r0 - r1, i0 - i1], 0), tab, 3)
    return (
        jnp.concatenate([even[:h], odd[:h]], 0),
        jnp.concatenate([even[h:], odd[h:]], 0),
    )


def rows_inverse(re, im, tab):
    h = re.shape[0] // 2
    even = table_times(jnp.concatenate([re[:h], im[:h]], 0), tab, 0)
    odd = table_times(jnp.concatenate([re[h:], im[h:]], 0), tab, 2)
    total, gap = even + odd, even - odd
    return (
        jnp.concatenate([total[:h], gap[:h]], 0),
        jnp.concatenate([total[h:], gap[h:]], 0),
    )


def forward(waves, tab):
    waves = [columns_forward(*wave, tab) for wave in waves]
    return [rows_forward(*wave, tab) for wave in waves]


def inverse(waves, tab):
    waves = [rows_inverse(*wave, tab) for wave in waves]
    return [columns_inverse(*wave, tab) for wave in waves]


def times(a, b):
    return a[0] * b[0] - a[1] * b[1], a[0] * b[1] + a[1] * b[0]


def times_conj(a, b):
    return a[0] * b[0] + a[1] * b[1], a[0] * b[1] - a[1] * b[0]


def in_groups(states, body):
    group = 2 if states % 2 == 0 else 1
    if states == group:
        body([m for m in range(group)])
        return

    def step(g, carry):
        body([g * group + m for m in range(group)])
        return carry

    lax.fori_loop(0, states // group, step, 0)


def thirds(value):
    top = value.astype(BF16)
    left = value - top.astype(F32)
    mid = left.astype(BF16)
    return top, mid, (left - mid.astype(F32)).astype(BF16)


def by_parity(value):
    size = value.shape[0]
    h = size // 2
    picks = []
    for along in (0, 1):
        place = lax.broadcasted_iota(jnp.int32, (size, size), along)
        source = lax.broadcasted_iota(jnp.int32, (size, size), 1 - along)
        wanted = jnp.where(place < h, 2 * place, 2 * (place - h) + 1)
        picks.append(jnp.where(source == wanted, 1.0, 0.0).astype(BF16))
    top, mid, low = thirds(value)
    value = (dot(picks[0], top) + dot(picks[0], mid)) + dot(picks[0], low)
    top, mid, low = thirds(value)
    return (dot(top, picks[1]) + dot(mid, picks[1])) + dot(low, picks[1])


def turned(value, row, col):
    return pltpu.roll(pltpu.roll(value, row, 0), col, 1)


def run_copies(moves, sem):
    copies = [pltpu.make_async_copy(src, dst, sem.at[i]) for i, (src, dst) in enumerate(moves)]
    for copy in copies:
        copy.start()
    return copies


def load_body(pos_hbm, probe_hbm, object_hbm, pos_out, plane_out, object_out, sem):
    which = lax.rem(lax.axis_index("frame"), 2)
    half = object_hbm.shape[2] // 2
    moves = [(probe_hbm.at[0, which], plane_out), (pos_hbm, pos_out)]
    for s in range(2):
        for part in range(2):
            for at in (pl.ds(0, half), pl.ds(half, half)):
                moves.append((object_hbm.at[s, part, at], object_out.at[s, part, at]))
    for copy in run_copies(moves, sem):
        copy.wait()


def turn_of(pos_ref, size):
    return jnp.sum(pos_ref[0:1, 0:1]), lax.rem(jnp.sum(pos_ref[0:1, 1:2]), size)


def turn_body(pos_ref, *refs):
    half = len(refs) // 2
    turn = turn_of(pos_ref, refs[0].shape[1])
    for came, out in zip(refs[:half], refs[half:]):
        out[...] = turned(came[...], *turn)


def prepare_body(
    pos_hbm, probe_hbm, prop_hbm, amp_hbm, tab_hbm,
    wave_re, wave_im, amp_out, first_out, tab_out,
    pos, probe, prop, amp, sem,
):
    copies = run_copies(
        ((pos_hbm, pos), (probe_hbm, probe), (prop_hbm, prop), (amp_hbm, amp), (tab_hbm, tab_out)), sem
    )
    copies[0].wait()
    copies[1].wait()
    size = prop.shape[0]
    row, col = pos[0, 0], lax.rem(pos[0, 1], size)
    for c in range(2):
        first_out[0, c] = turned(probe[0, c], row, col)
    copies[2].wait()
    phase = by_parity(prop[...])
    wave_re[...] = jnp.cos(phase)
    wave_im[...] = jnp.sin(phase)
    copies[3].wait()
    amp_out[...] = by_parity(amp[0])
    copies[4].wait()


def spread(ref, which, shape):
    return jnp.broadcast_to(ref[0:1, which : which + 1], shape)


def wrapped(ref, s, part, col_ref):
    size = ref.shape[-2]
    c = lax.broadcasted_iota(jnp.int32, (size, size), 1)
    return jnp.where(c < spread(col_ref, 1, c.shape), ref[s, part, :, size:], ref[s, part, :, :size])


def send_body(before_ref, object_ref, zero_ref, one_ref):
    for s, out in enumerate((zero_ref, one_ref)):
        for part in range(2):
            out[part] = wrapped(object_ref, s, part, before_ref)


def patch_of(s, object_ref, halo_ref, pos_ref):
    size = halo_ref.shape[-1]
    r = lax.broadcasted_iota(jnp.int32, (size, size), 0)
    return [
        jnp.where(r < spread(pos_ref, 0, r.shape), halo_ref[part], wrapped(object_ref, s, part, pos_ref))
        for part in range(2)
    ]


def pair(ref, *at):
    return ref[(*at, 0)], ref[(*at, 1)]


def inner_body(pos_ref, object_ref, halo_ref, first_ref, kr_ref, ki_ref, tab, *refs):
    out_ref, probe_ref, patch = refs[-3:]
    states = out_ref.shape[0]
    patch[0], patch[1] = patch_of(0, object_ref, halo_ref, pos_ref)
    swap = lax.rem(lax.axis_index("frame"), 2) == 1
    probe_ref[:1] = first_ref[...]
    for m, (came, given) in enumerate(zip(refs[:-3:2], refs[1:-3:2])):
        other = turned(given[...], *turn_of(pos_ref, given.shape[1]))
        probe_ref[1 + m, 0] = jnp.where(swap, other, came[...])
        probe_ref[1 + m, 1] = jnp.where(swap, came[...], other)

    def body(group):
        waves = forward([times(pair(probe_ref, m), pair(patch)) for m in group], tab)
        waves = inverse([times((kr_ref[...], ki_ref[...]), wave) for wave in waves], tab)
        for m, wave in zip(group, waves):
            out_ref[m, 0], out_ref[m, 1] = wave

    in_groups(states, body)


def middle_body(rows, pos_ref, object_ref, halo_ref, inner_ref, amp_ref, tab, term_ref, chi_ref, patch, far, power):
    states = inner_ref.shape[0]
    patch[0], patch[1] = patch_of(1, object_ref, halo_ref, pos_ref)
    power[...] = jnp.zeros_like(power)

    def outward(group):
        waves = forward([times(pair(patch), pair(inner_ref, m)) for m in group], tab)
        total = power[...]
        for m, wave in zip(group, waves):
            far[m, 0], far[m, 1] = wave
            total += wave[0] * wave[0] + wave[1] * wave[1]
        power[...] = total

    in_groups(states, outward)
    power[...] = 1.0 - amp_ref[...] * lax.rsqrt(power[...] + 1.0)
    term_ref[...] = jnp.zeros_like(term_ref)
    take = pl.ds(pl.multiple_of(lax.axis_index("state") * rows, rows), rows)

    def homeward(group):
        waves = inverse([(power[...] * far[m, 0], power[...] * far[m, 1]) for m in group], tab)
        for m, wave in zip(group, waves):
            far[m, 0], far[m, 1] = wave
            chi_ref[m, 0], chi_ref[m, 1] = times_conj(pair(patch), wave)
        for m in group:
            part = times_conj(
                (inner_ref[m, 0, take], inner_ref[m, 1, take]), (far[m, 0, take], far[m, 1, take])
            )
            term_ref[0] += part[0]
            term_ref[1] += part[1]

    in_groups(states, homeward)


def last_body(rows, chi_ref, probe_ref, kr_ref, ki_ref, tab, term_ref, front):
    states = chi_ref.shape[0]
    take = pl.ds(pl.multiple_of(lax.axis_index("state") * rows, rows), rows)
    term_ref[...] = jnp.zeros_like(term_ref)

    def body(group):
        waves = forward([pair(chi_ref, m) for m in group], tab)
        waves = [rows_inverse(*times_conj((kr_ref[...], ki_ref[...]), wave), tab) for wave in waves]
        for m, wave in zip(group, waves):
            front[m, 0], front[m, 1] = wave
        for m in group:
            wave = columns_inverse(front[m, 0, take], front[m, 1, take], tab)
            part = times_conj((probe_ref[m, 0, take], probe_ref[m, 1, take]), wave)
            term_ref[0] += part[0]
            term_ref[1] += part[1]

    in_groups(states, body)


def gather_body(slice_id, rows, pos_ref, before_ref, own_ref, came_ref, *refs):
    out_ref, held, sem = refs[-3:]
    size = own_ref.shape[-1]
    start = lax.axis_index("state") * rows
    r = lax.broadcasted_iota(jnp.int32, (rows, size), 0) + start
    c = lax.broadcasted_iota(jnp.int32, (rows, size), 1)
    here, there = r >= spread(pos_ref, 0, r.shape), r < spread(before_ref, 0, r.shape)
    here_right, there_right = c < spread(pos_ref, 1, c.shape), c < spread(before_ref, 1, c.shape)
    chunks = 4 if rows % 32 == 0 else 1
    step = rows // chunks
    copies = []
    for chunk in range(chunks):
        at = pl.ds(chunk * step, step)
        cut = slice(chunk * step, chunk * step + step)
        for part in range(2):
            mine = jnp.where(here[cut], own_ref[part, at], 0.0)
            theirs = jnp.where(there[cut], came_ref[part, at], 0.0)
            left, right = here_right[cut], there_right[cut]
            held[part, at, :size] = jnp.where(left, 0.0, mine) + jnp.where(right, 0.0, theirs)
            held[part, at, size:] = jnp.where(left, mine, 0.0) + jnp.where(right, theirs, 0.0)
            copies.append(
                pltpu.make_async_copy(held.at[part, at], out_ref.at[slice_id, part, at], sem.at[len(copies)])
            )
            copies[-1].start()
    for copy in copies:
        copy.wait()


def gather(slice_id, rows, size, pos, before, own, came, *given):
    return pl.pallas_call(
        functools.partial(gather_body, slice_id, rows),
        out_shape=jax.ShapeDtypeStruct((2, 2, rows, 2 * size), F32),
        in_specs=[VMEM] * 4 + [pl.BlockSpec(memory_space=pl.ANY)] * len(given),
        out_specs=pl.BlockSpec(memory_space=pl.ANY),
        scratch_shapes=[pltpu.VMEM((2, rows, 2 * size), F32), pltpu.SemaphoreType.DMA((8,))],
        input_output_aliases={4: 0} if given else {},
        compiler_params=pltpu.CompilerParams(vmem_limit_bytes=LIMIT),
        cost_estimate=pl.CostEstimate(flops=0, bytes_accessed=32 * rows * size, transcendentals=0),
    )(pos, before, own, came, *given)


def on_device(object_slices, probe, amplitude, positions, propagator):
    states = lax.axis_size("state")
    size = amplitude.shape[1]
    rows = object_slices.shape[2] // states
    assert object_slices.shape[2:] == (size, 2 * size) and positions.shape[0] == 1
    assert lax.axis_size("frame") % 2 == 0
    return gradient_of(object_slices, probe, amplitude, positions, propagator, states, size, rows)


def gradient_of(object_slices, probe, amplitude, positions, propagator, states, size, rows):
    grid = (size, size)
    unit = size * size
    flops = 24 * size**3
    tab = tables(size)
    before = shifted(positions, "frame", 1)
    given = [in_hbm(x) for x in (positions, probe, object_slices)]
    pos, plane, held = pl.pallas_call(
        load_body,
        out_shape=[
            jax.ShapeDtypeStruct(positions.shape, jnp.int32),
            jax.ShapeDtypeStruct(grid, F32),
            jax.ShapeDtypeStruct(object_slices.shape, F32),
        ],
        in_specs=[HBM] * 3,
        out_specs=[VMEM] * 3,
        scratch_shapes=[pltpu.SemaphoreType.DMA((10,))],
        compiler_params=pltpu.CompilerParams(vmem_limit_bytes=LIMIT),
        cost_estimate=pl.CostEstimate(flops=0, bytes_accessed=40 * unit, transcendentals=0),
    )(*given)
    planes = []
    for by in range(1, states):
        planes.append(shifted(plane, "state", by))
    picked = call(send_body, [(2,) + grid] * 2, [VMEM, VMEM], moved=16 * unit)(before, held)
    halo_zero = shifted(picked[0], "frame", -1)
    halo_one = shifted(picked[1], "frame", -1)
    kr, ki, amp, first, tab = pl.pallas_call(
        prepare_body,
        out_shape=[jax.ShapeDtypeStruct(grid, F32)] * 3
        + [jax.ShapeDtypeStruct(x.shape, x.dtype) for x in (probe, tab)],
        in_specs=[HBM] * 5,
        out_specs=[VMEM] * 5,
        scratch_shapes=[
            pltpu.SMEM(positions.shape, jnp.int32),
            pltpu.VMEM(probe.shape, F32),
            pltpu.VMEM(grid, F32),
            pltpu.VMEM(amplitude.shape, F32),
            pltpu.SemaphoreType.DMA((5,)),
        ],
        compiler_params=pltpu.CompilerParams(vmem_limit_bytes=LIMIT),
        cost_estimate=pl.CostEstimate(flops=2 * size**3, bytes_accessed=60 * unit, transcendentals=0),
    )(*given[:2], *(in_hbm(x) for x in (propagator, amplitude, tab)))
    frames = lax.axis_size("frame")
    own = call(turn_body, [grid] * len(planes), [VMEM] * (1 + len(planes)), moved=16 * unit)(pos, *planes)
    pairs = []
    for came, kept in zip(planes, own):
        pairs += [kept, lax.ppermute(came, "frame", [(i, i ^ 1) for i in range(frames)])]
    waves, probes = call(
        inner_body,
        [(states, 2) + grid] * 2,
        [VMEM] * (7 + len(pairs)),
        [pltpu.VMEM((2,) + grid, F32)],
        flops=2 * flops * states,
        moved=24 * unit * states,
    )(pos, held, halo_zero, first, kr, ki, tab, *pairs)
    term_one, chi = call(
        functools.partial(middle_body, rows),
        [(2, rows, size), (states, 2) + grid],
        [VMEM] * 6,
        [pltpu.VMEM((2,) + grid, F32), pltpu.VMEM((states, 2) + grid, F32), pltpu.VMEM(grid, F32)],
        flops=2 * flops * states,
        moved=32 * unit * states,
    )(pos, held, halo_one, waves, amp, tab)
    came_one = shifted(term_one, "frame", 1)
    (term_zero,) = call(
        functools.partial(last_body, rows),
        [(2, rows, size)],
        [VMEM] * 5,
        [pltpu.VMEM((states, 2) + grid, F32)],
        flops=2 * flops * states,
        moved=16 * unit * states,
    )(chi, probes, kr, ki, tab)
    came_zero = shifted(term_zero, "frame", 1)
    gradient = gather(1, rows, size, pos, before, term_one, came_one)
    return gather(0, rows, size, pos, before, term_zero, came_zero, gradient)


def solution(mesh):
    return jax.shard_map(
        on_device,
        mesh=mesh,
        in_specs=(
            P(None, None, "frame", None),
            P("state", None, None, None),
            P("frame", None, None),
            P("frame", None),
            P(),
        ),
        out_specs=P(None, None, ("frame", "state"), None),
        check_vma=False,
    )
```

```python
import functools
import math

import jax
import jax.numpy as jnp
import numpy as np
from jax import lax
from jax.experimental import pallas as pl
from jax.experimental.pallas import tpu as pltpu
from jax.sharding import PartitionSpec as P


F32 = jnp.float32
BF16 = jnp.bfloat16
VMEM = pl.BlockSpec(memory_space=pltpu.VMEM)
HBM = pl.BlockSpec(memory_space=pltpu.MemorySpace.HBM)
SMEM = pl.BlockSpec(memory_space=pltpu.SMEM)
LIMIT = 24 * 1024 * 1024


def shifted(value, axis, by):
    count = lax.axis_size(axis)
    return lax.ppermute(value, axis, [(i, (i + by) % count) for i in range(count)])


def in_hbm(value):
    return pltpu.with_memory_space_constraint(value, pltpu.MemorySpace.HBM)


def call(body, outs, ins, scratch=(), flops=0, moved=0):
    return pl.pallas_call(
        body,
        out_shape=[jax.ShapeDtypeStruct(shape, F32) for shape in outs],
        in_specs=ins,
        out_specs=[VMEM] * len(outs),
        scratch_shapes=list(scratch),
        compiler_params=pltpu.CompilerParams(vmem_limit_bytes=LIMIT),
        cost_estimate=pl.CostEstimate(flops=flops, bytes_accessed=moved, transcendentals=0),
    )


def tables(length):
    half = length // 2
    n = np.arange(half)[:, None]
    forms = []
    for parity in (0, 1):
        k = 2 * np.arange(half)[None, :] + parity
        angle = -2.0 * math.pi * ((n * k) % length) / length
        re, im = np.cos(angle) / math.sqrt(length), np.sin(angle) / math.sqrt(length)
        right = np.block([[re, im], [-im, re]])
        forms += [right, right.T]
    stack = np.stack(forms).astype(np.float64)
    top = stack.astype(BF16)
    rest = (stack - top.astype(np.float64)).astype(BF16)
    return jnp.asarray(np.stack([top, rest]))


def halves(value):
    top = value.astype(BF16)
    return top, (value - top.astype(F32)).astype(BF16)


def dot(a, b):
    return lax.dot_general(a, b, (((1,), (0,)), ((), ())), preferred_element_type=F32)


def times_table(value, tab, which):
    top, rest = halves(value)
    return dot(top, tab[0, which]) + (dot(rest, tab[0, which]) + dot(top, tab[1, which]))


def table_times(value, tab, which):
    top, rest = halves(value)
    return dot(tab[0, which], top) + (dot(tab[0, which], rest) + dot(tab[1, which], top))


def columns_forward(re, im, tab):
    h = re.shape[1] // 2
    r0, r1, i0, i1 = re[:, :h], re[:, h:], im[:, :h], im[:, h:]
    even = times_table(jnp.concatenate([r0 + r1, i0 + i1], 1), tab, 0)
    odd = times_table(jnp.concatenate([r0 - r1, i0 - i1], 1), tab, 2)
    return (
        jnp.concatenate([even[:, :h], odd[:, :h]], 1),
        jnp.concatenate([even[:, h:], odd[:, h:]], 1),
    )


def columns_inverse(re, im, tab):
    h = re.shape[1] // 2
    even = times_table(jnp.concatenate([re[:, :h], im[:, :h]], 1), tab, 1)
    odd = times_table(jnp.concatenate([re[:, h:], im[:, h:]], 1), tab, 3)
    total, gap = even + odd, even - odd
    return (
        jnp.concatenate([total[:, :h], gap[:, :h]], 1),
        jnp.concatenate([total[:, h:], gap[:, h:]], 1),
    )


def rows_forward(re, im, tab):
    h = re.shape[0] // 2
    r0, r1, i0, i1 = re[:h], re[h:], im[:h], im[h:]
    even = table_times(jnp.concatenate([r0 + r1, i0 + i1], 0), tab, 1)
    odd = table_times(jnp.concatenate([r0 - r1, i0 - i1], 0), tab, 3)
    return (
        jnp.concatenate([even[:h], odd[:h]], 0),
        jnp.concatenate([even[h:], odd[h:]], 0),
    )


def rows_inverse(re, im, tab):
    h = re.shape[0] // 2
    even = table_times(jnp.concatenate([re[:h], im[:h]], 0), tab, 0)
    odd = table_times(jnp.concatenate([re[h:], im[h:]], 0), tab, 2)
    total, gap = even + odd, even - odd
    return (
        jnp.concatenate([total[:h], gap[:h]], 0),
        jnp.concatenate([total[h:], gap[h:]], 0),
    )


def forward(waves, tab):
    waves = [columns_forward(*wave, tab) for wave in waves]
    return [rows_forward(*wave, tab) for wave in waves]


def inverse(waves, tab):
    waves = [rows_inverse(*wave, tab) for wave in waves]
    return [columns_inverse(*wave, tab) for wave in waves]


def times(a, b):
    return a[0] * b[0] - a[1] * b[1], a[0] * b[1] + a[1] * b[0]


def times_conj(a, b):
    return a[0] * b[0] + a[1] * b[1], a[0] * b[1] - a[1] * b[0]


def in_groups(states, body):
    group = 2 if states % 2 == 0 else 1
    if states == group:
        body([m for m in range(group)])
        return

    def step(g, carry):
        body([g * group + m for m in range(group)])
        return carry

    lax.fori_loop(0, states // group, step, 0)


def thirds(value):
    top = value.astype(BF16)
    left = value - top.astype(F32)
    mid = left.astype(BF16)
    return top, mid, (left - mid.astype(F32)).astype(BF16)


def parity_picks(size):
    h = size // 2
    picks = []
    for along in (0, 1):
        place = lax.broadcasted_iota(jnp.int32, (size, size), along)
        source = lax.broadcasted_iota(jnp.int32, (size, size), 1 - along)
        wanted = jnp.where(place < h, 2 * place, 2 * (place - h) + 1)
        picks.append(jnp.where(source == wanted, 1.0, 0.0).astype(BF16))
    return picks


def by_parity(value, picks):
    top, mid, low = thirds(value)
    value = (dot(picks[0], top) + dot(picks[0], mid)) + dot(picks[0], low)
    top, mid, low = thirds(value)
    return (dot(top, picks[1]) + dot(mid, picks[1])) + dot(low, picks[1])


def turned(value, row, col):
    return pltpu.roll(pltpu.roll(value, row, 0), col, 1)


def run_copies(moves, sem):
    copies = [pltpu.make_async_copy(src, dst, sem.at[i]) for i, (src, dst) in enumerate(moves)]
    for copy in copies:
        copy.start()
    return copies


def is_odd():
    return lax.rem(lax.axis_index("frame"), 2) == 1


def spread(ref, frame, which, shape):
    return jnp.broadcast_to(ref[frame : frame + 1, which : which + 1], shape)


def turn_of(at_ref, frame, size):
    row = jnp.sum(at_ref[frame : frame + 1, 0:1])
    return row, lax.rem(jnp.sum(at_ref[frame : frame + 1, 1:2]), size)


def owned(at_ref, frame, shape, start=0):
    gap = lax.broadcasted_iota(jnp.int32, shape, 0) + start - spread(at_ref, frame, 0, shape)
    odd = is_odd()
    low = odd if frame == 0 else jnp.logical_not(odd)
    return jnp.where(low, gap, -1 - gap) < 0


def load_body(pos_hbm, probe_hbm, object_hbm, pos_out, plane_out, object_out, sem):
    which = lax.rem(lax.axis_index("frame"), 2)
    half = object_hbm.shape[2] // 2
    moves = [(probe_hbm.at[0, which], plane_out), (pos_hbm, pos_out)]
    for s in range(2):
        for part in range(2):
            for at in (pl.ds(0, half), pl.ds(half, half)):
                moves.append((object_hbm.at[s, part, at], object_out.at[s, part, at]))
    for copy in run_copies(moves, sem):
        copy.wait()


def send_body(pos_ref, before_ref, object_ref, at_ref, even_ref, zero_ref, one_ref):
    size = object_ref.shape[-2]
    odd = is_odd()
    at_ref[0:1] = jnp.where(odd, before_ref[...], pos_ref[...])
    at_ref[1:2] = jnp.where(odd, pos_ref[...], before_ref[...])
    c = lax.broadcasted_iota(jnp.int32, (size, size), 1)
    even_right, odd_right = c < spread(at_ref, 0, 1, c.shape), c < spread(at_ref, 1, 1, c.shape)
    for s, out in enumerate((zero_ref, one_ref)):
        for part in range(2):
            left, right = object_ref[s, part, :, :size], object_ref[s, part, :, size:]
            even_ref[s, part] = jnp.where(even_right, right, left)
            out[part] = jnp.where(odd_right, right, left)


def prepare_body(
    at_ref, prev_ref, probe_hbm, prop_hbm, amp_hbm, tab_hbm,
    wave_re, wave_im, amp_out, first_out, tab_out,
    probe, prop, amp, sem,
):
    copies = run_copies(((probe_hbm, probe), (prop_hbm, prop), (amp_hbm, amp), (tab_hbm, tab_out)), sem)
    size = prop.shape[0]
    picks = parity_picks(size)
    copies[0].wait()
    for frame in range(2):
        turn = turn_of(at_ref, frame, size)
        for c in range(2):
            first_out[frame, c] = turned(probe[0, c], *turn)
    copies[1].wait()
    phase = by_parity(prop[...], picks)
    wave_re[...] = jnp.cos(phase)
    wave_im[...] = jnp.sin(phase)
    copies[2].wait()
    odd = is_odd()
    amp_out[0] = by_parity(jnp.where(odd, prev_ref[0], amp[0]), picks)
    amp_out[1] = by_parity(jnp.where(odd, amp[0], prev_ref[0]), picks)
    copies[3].wait()


def patch_of(frame, at_ref, own, came):
    mine = owned(at_ref, frame, own[0].shape)
    return [jnp.where(mine, own[part], came[part]) for part in range(2)]


def pair(ref, *at):
    return ref[(*at, 0)], ref[(*at, 1)]


def inner_body(frame, at_ref, own_ref, came_ref, first_ref, kr_ref, ki_ref, tab, *refs):
    out_ref, probe_ref, patch = refs[-3:]
    states = out_ref.shape[0]
    own, came = (own_ref.at[0], came_ref.at[0]) if frame == 0 else (own_ref, came_ref)
    patch[0], patch[1] = patch_of(frame, at_ref, own, came)
    odd = is_odd()
    turn = turn_of(at_ref, frame, patch.shape[-1])
    probe_ref[0] = first_ref[frame]
    for m, (plane, swapped) in enumerate(zip(refs[:-3:2], refs[1:-3:2])):
        probe_ref[1 + m, 0] = turned(jnp.where(odd, swapped[...], plane[...]), *turn)
        probe_ref[1 + m, 1] = turned(jnp.where(odd, plane[...], swapped[...]), *turn)

    def body(group):
        waves = forward([times(pair(probe_ref, m), pair(patch)) for m in group], tab)
        waves = inverse([times((kr_ref[...], ki_ref[...]), wave) for wave in waves], tab)
        for m, wave in zip(group, waves):
            out_ref[m, 0], out_ref[m, 1] = wave

    in_groups(states, body)


def middle_body(frame, rows, at_ref, own_ref, came_ref, inner_ref, amp_ref, tab, term_ref, chi_ref, patch, far, power):
    states = inner_ref.shape[0]
    own, came = (own_ref.at[1], came_ref.at[1]) if frame == 0 else (own_ref, came_ref)
    patch[0], patch[1] = patch_of(frame, at_ref, own, came)
    power[...] = jnp.zeros_like(power)

    def outward(group):
        waves = forward([times(pair(patch), pair(inner_ref, m)) for m in group], tab)
        total = power[...]
        for m, wave in zip(group, waves):
            far[m, 0], far[m, 1] = wave
            total += wave[0] * wave[0] + wave[1] * wave[1]
        power[...] = total

    in_groups(states, outward)
    power[...] = 1.0 - amp_ref[frame] * lax.rsqrt(power[...] + 1.0)
    term_ref[...] = jnp.zeros_like(term_ref)
    take = pl.ds(pl.multiple_of(lax.axis_index("state") * rows, rows), rows)

    def homeward(group):
        waves = inverse([(power[...] * far[m, 0], power[...] * far[m, 1]) for m in group], tab)
        for m, wave in zip(group, waves):
            far[m, 0], far[m, 1] = wave
            chi_ref[m, 0], chi_ref[m, 1] = times_conj(pair(patch), wave)
        for m in group:
            part = times_conj(
                (inner_ref[m, 0, take], inner_ref[m, 1, take]), (far[m, 0, take], far[m, 1, take])
            )
            term_ref[0] += part[0]
            term_ref[1] += part[1]

    in_groups(states, homeward)


def last_body(rows, chi_ref, probe_ref, kr_ref, ki_ref, tab, term_ref, front):
    states = chi_ref.shape[0]
    take = pl.ds(pl.multiple_of(lax.axis_index("state") * rows, rows), rows)
    term_ref[...] = jnp.zeros_like(term_ref)

    def body(group):
        waves = forward([pair(chi_ref, m) for m in group], tab)
        waves = [rows_inverse(*times_conj((kr_ref[...], ki_ref[...]), wave), tab) for wave in waves]
        for m, wave in zip(group, waves):
            front[m, 0], front[m, 1] = wave
        for m in group:
            wave = columns_inverse(front[m, 0, take], front[m, 1, take], tab)
            part = times_conj((probe_ref[m, 0, take], probe_ref[m, 1, take]), wave)
            term_ref[0] += part[0]
            term_ref[1] += part[1]

    in_groups(states, body)


def finish_body(rows, at_ref, one_even, zero_even, one_odd, chi_ref, probe_ref, kr_ref, ki_ref, tab, out_ref, front, term, held, sem):
    size = front.shape[-1]
    start = lax.axis_index("state") * rows
    c = lax.broadcasted_iota(jnp.int32, (rows, size), 1)
    frames = [(owned(at_ref, k, c.shape, start), c < spread(at_ref, k, 1, c.shape)) for k in range(2)]
    chunks = 2 if rows % 16 == 0 else 1
    step = rows // chunks

    def leave(s, terms):
        copies = []
        for chunk in range(chunks):
            at = pl.ds(chunk * step, step)
            cut = slice(chunk * step, chunk * step + step)
            for part in range(2):
                left, right = 0.0, 0.0
                for (mine, over), given in zip(frames, terms):
                    value = jnp.where(mine[cut], given[part, at], 0.0)
                    left += jnp.where(over[cut], 0.0, value)
                    right += jnp.where(over[cut], value, 0.0)
                held[s, part, at, :size] = left
                held[s, part, at, size:] = right
                place = (s * chunks + chunk) * 2 + part
                copies.append(pltpu.make_async_copy(held.at[s, part, at], out_ref.at[s, part, at], sem.at[place]))
                copies[-1].start()
        return copies

    copies = leave(1, (one_even, one_odd))
    last_body(rows, chi_ref, probe_ref, kr_ref, ki_ref, tab, term, front)
    copies += leave(0, (zero_even, term))
    for copy in copies:
        copy.wait()


def on_device(object_slices, probe, amplitude, positions, propagator):
    states = lax.axis_size("state")
    size = amplitude.shape[1]
    rows = object_slices.shape[2] // states
    assert object_slices.shape[2:] == (size, 2 * size) and positions.shape[0] == 1
    assert lax.axis_size("frame") % 2 == 0
    return gradient_of(object_slices, probe, amplitude, positions, propagator, states, size, rows)


def gradient_of(object_slices, probe, amplitude, positions, propagator, states, size, rows):
    grid = (size, size)
    unit = size * size
    flops = 24 * size**3
    frames = lax.axis_size("frame")
    across = [(i, (i + 1) % frames if i % 2 else (i - 1) % frames) for i in range(frames)]
    beside = [(i, i ^ 1) for i in range(frames)]
    tab = tables(size)
    before = shifted(positions, "frame", 1)
    lent = shifted(amplitude, "frame", 1)
    given = [in_hbm(x) for x in (positions, probe, object_slices)]
    pos, plane, held = pl.pallas_call(
        load_body,
        out_shape=[
            jax.ShapeDtypeStruct(positions.shape, jnp.int32),
            jax.ShapeDtypeStruct(grid, F32),
            jax.ShapeDtypeStruct(object_slices.shape, F32),
        ],
        in_specs=[HBM] * 3,
        out_specs=[VMEM] * 3,
        scratch_shapes=[pltpu.SemaphoreType.DMA((10,))],
        compiler_params=pltpu.CompilerParams(vmem_limit_bytes=LIMIT),
        cost_estimate=pl.CostEstimate(flops=0, bytes_accessed=40 * unit, transcendentals=0),
    )(*given)
    planes = []
    for by in range(1, states):
        planes.append(shifted(plane, "state", by))
    at, even, zero, one = pl.pallas_call(
        send_body,
        out_shape=[jax.ShapeDtypeStruct((2, 2), jnp.int32)]
        + [jax.ShapeDtypeStruct(shape, F32) for shape in ((2, 2) + grid, (2,) + grid, (2,) + grid)],
        in_specs=[VMEM] * 3,
        out_specs=[VMEM] * 4,
        compiler_params=pltpu.CompilerParams(vmem_limit_bytes=LIMIT),
        cost_estimate=pl.CostEstimate(flops=0, bytes_accessed=64 * unit, transcendentals=0),
    )(pos, before, held)
    came_zero = lax.ppermute(zero, "frame", across)
    came_one = lax.ppermute(one, "frame", across)
    came_even = lax.ppermute(even, "frame", beside)
    kr, ki, amps, first, tab = pl.pallas_call(
        prepare_body,
        out_shape=[jax.ShapeDtypeStruct(shape, F32) for shape in (grid, grid, (2,) + grid, (2, 2) + grid)]
        + [jax.ShapeDtypeStruct(tab.shape, tab.dtype)],
        in_specs=[VMEM] * 2 + [HBM] * 4,
        out_specs=[VMEM] * 5,
        scratch_shapes=[
            pltpu.VMEM(probe.shape, F32),
            pltpu.VMEM(grid, F32),
            pltpu.VMEM(amplitude.shape, F32),
            pltpu.SemaphoreType.DMA((4,)),
        ],
        compiler_params=pltpu.CompilerParams(vmem_limit_bytes=LIMIT),
        cost_estimate=pl.CostEstimate(flops=2 * size**3, bytes_accessed=60 * unit, transcendentals=0),
    )(at, lent, given[1], *(in_hbm(x) for x in (propagator, amplitude, tab)))
    pairs = []
    for plane in planes:
        pairs += [plane, lax.ppermute(plane, "frame", beside)]

    def inner(frame, own, came):
        return call(
            functools.partial(inner_body, frame),
            [(states, 2) + grid] * 2,
            [VMEM] * (7 + len(pairs)),
            [pltpu.VMEM((2,) + grid, F32)],
            flops=2 * flops * states,
            moved=24 * unit * states,
        )(at, own, came, first, kr, ki, tab, *pairs)

    def middle(frame, own, came, waves):
        return call(
            functools.partial(middle_body, frame, rows),
            [(2, rows, size), (states, 2) + grid],
            [VMEM] * 6,
            [pltpu.VMEM((2,) + grid, F32), pltpu.VMEM((states, 2) + grid, F32), pltpu.VMEM(grid, F32)],
            flops=2 * flops * states,
            moved=32 * unit * states,
        )(at, own, came, waves, amps, tab)

    even_waves, even_probes = inner(0, even, came_even)
    waves, probes = inner(1, zero, came_zero)
    one_even, chi = middle(0, even, came_even, even_waves)
    (zero_even,) = call(
        functools.partial(last_body, rows),
        [(2, rows, size)],
        [VMEM] * 5,
        [pltpu.VMEM((states, 2) + grid, F32)],
        flops=2 * flops * states,
        moved=16 * unit * states,
    )(chi, even_probes, kr, ki, tab)
    one_odd, chi = middle(1, one, came_one, waves)
    return pl.pallas_call(
        functools.partial(finish_body, rows),
        out_shape=jax.ShapeDtypeStruct((2, 2, rows, 2 * size), F32),
        in_specs=[VMEM] * 9,
        out_specs=pl.BlockSpec(memory_space=pl.ANY),
        scratch_shapes=[
            pltpu.VMEM((states, 2) + grid, F32),
            pltpu.VMEM((2, rows, size), F32),
            pltpu.VMEM((2, 2, rows, 2 * size), F32),
            pltpu.SemaphoreType.DMA((8,)),
        ],
        compiler_params=pltpu.CompilerParams(vmem_limit_bytes=LIMIT),
        cost_estimate=pl.CostEstimate(flops=2 * flops * states, bytes_accessed=32 * unit * states, transcendentals=0),
    )(at, one_even, zero_even, one_odd, chi, probes, kr, ki, tab)


def solution(mesh):
    return jax.shard_map(
        on_device,
        mesh=mesh,
        in_specs=(
            P(None, None, "frame", None),
            P("state", None, None, None),
            P("frame", None, None),
            P("frame", None),
            P(),
        ),
        out_specs=P(None, None, ("frame", "state"), None),
        check_vma=False,
    )
```

```python
import functools
import math

import jax
import jax.numpy as jnp
import numpy as np
from jax import lax
from jax.experimental import pallas as pl
from jax.experimental.pallas import tpu as pltpu
from jax.sharding import PartitionSpec as P


F32 = jnp.float32
BF16 = jnp.bfloat16
VMEM = pl.BlockSpec(memory_space=pltpu.VMEM)
HBM = pl.BlockSpec(memory_space=pltpu.MemorySpace.HBM)
SMEM = pl.BlockSpec(memory_space=pltpu.SMEM)
LIMIT = 24 * 1024 * 1024


def shifted(value, axis, by):
    count = lax.axis_size(axis)
    return lax.ppermute(value, axis, [(i, (i + by) % count) for i in range(count)])


def in_hbm(value):
    return pltpu.with_memory_space_constraint(value, pltpu.MemorySpace.HBM)


def call(body, outs, ins, scratch=(), flops=0, moved=0):
    return pl.pallas_call(
        body,
        out_shape=[jax.ShapeDtypeStruct(shape, F32) for shape in outs],
        in_specs=ins,
        out_specs=[VMEM] * len(outs),
        scratch_shapes=list(scratch),
        compiler_params=pltpu.CompilerParams(vmem_limit_bytes=LIMIT),
        cost_estimate=pl.CostEstimate(flops=flops, bytes_accessed=moved, transcendentals=0),
    )


def tables(length):
    half = length // 2
    n = np.arange(half)[:, None]
    forms = []
    for parity in (0, 1):
        k = 2 * np.arange(half)[None, :] + parity
        angle = -2.0 * math.pi * ((n * k) % length) / length
        re, im = np.cos(angle) / math.sqrt(length), np.sin(angle) / math.sqrt(length)
        right = np.block([[re, im], [-im, re]])
        forms += [right, right.T]
    stack = np.stack(forms).astype(np.float64)
    top = stack.astype(BF16)
    rest = (stack - top.astype(np.float64)).astype(BF16)
    return jnp.asarray(np.stack([top, rest]))


def halves(value):
    top = value.astype(BF16)
    return top, (value - top.astype(F32)).astype(BF16)


def dot(a, b):
    return lax.dot_general(a, b, (((1,), (0,)), ((), ())), preferred_element_type=F32)


def times_table(value, tab, which):
    top, rest = halves(value)
    return dot(top, tab[0, which]) + (dot(rest, tab[0, which]) + dot(top, tab[1, which]))


def table_times(value, tab, which):
    top, rest = halves(value)
    return dot(tab[0, which], top) + (dot(tab[0, which], rest) + dot(tab[1, which], top))


def columns_forward(re, im, tab):
    h = re.shape[1] // 2
    r0, r1, i0, i1 = re[:, :h], re[:, h:], im[:, :h], im[:, h:]
    even = times_table(jnp.concatenate([r0 + r1, i0 + i1], 1), tab, 0)
    odd = times_table(jnp.concatenate([r0 - r1, i0 - i1], 1), tab, 2)
    return (
        jnp.concatenate([even[:, :h], odd[:, :h]], 1),
        jnp.concatenate([even[:, h:], odd[:, h:]], 1),
    )


def columns_inverse(re, im, tab):
    h = re.shape[1] // 2
    even = times_table(jnp.concatenate([re[:, :h], im[:, :h]], 1), tab, 1)
    odd = times_table(jnp.concatenate([re[:, h:], im[:, h:]], 1), tab, 3)
    total, gap = even + odd, even - odd
    return (
        jnp.concatenate([total[:, :h], gap[:, :h]], 1),
        jnp.concatenate([total[:, h:], gap[:, h:]], 1),
    )


def rows_forward(re, im, tab):
    h = re.shape[0] // 2
    r0, r1, i0, i1 = re[:h], re[h:], im[:h], im[h:]
    even = table_times(jnp.concatenate([r0 + r1, i0 + i1], 0), tab, 1)
    odd = table_times(jnp.concatenate([r0 - r1, i0 - i1], 0), tab, 3)
    return (
        jnp.concatenate([even[:h], odd[:h]], 0),
        jnp.concatenate([even[h:], odd[h:]], 0),
    )


def rows_inverse(re, im, tab):
    h = re.shape[0] // 2
    even = table_times(jnp.concatenate([re[:h], im[:h]], 0), tab, 0)
    odd = table_times(jnp.concatenate([re[h:], im[h:]], 0), tab, 2)
    total, gap = even + odd, even - odd
    return (
        jnp.concatenate([total[:h], gap[:h]], 0),
        jnp.concatenate([total[h:], gap[h:]], 0),
    )


def forward(waves, tab):
    waves = [columns_forward(*wave, tab) for wave in waves]
    return [rows_forward(*wave, tab) for wave in waves]


def inverse(waves, tab):
    waves = [rows_inverse(*wave, tab) for wave in waves]
    return [columns_inverse(*wave, tab) for wave in waves]


def times(a, b):
    return a[0] * b[0] - a[1] * b[1], a[0] * b[1] + a[1] * b[0]


def times_conj(a, b):
    return a[0] * b[0] + a[1] * b[1], a[0] * b[1] - a[1] * b[0]


def in_groups(states, body):
    group = 2 if states % 2 == 0 else 1
    if states == group:
        body([m for m in range(group)])
        return

    def step(g, carry):
        body([g * group + m for m in range(group)])
        return carry

    lax.fori_loop(0, states // group, step, 0)


def thirds(value):
    top = value.astype(BF16)
    left = value - top.astype(F32)
    mid = left.astype(BF16)
    return top, mid, (left - mid.astype(F32)).astype(BF16)


def by_parity(value):
    size = value.shape[0]
    h = size // 2
    picks = []
    for along in (0, 1):
        place = lax.broadcasted_iota(jnp.int32, (size, size), along)
        source = lax.broadcasted_iota(jnp.int32, (size, size), 1 - along)
        wanted = jnp.where(place < h, 2 * place, 2 * (place - h) + 1)
        picks.append(jnp.where(source == wanted, 1.0, 0.0).astype(BF16))
    top, mid, low = thirds(value)
    value = (dot(picks[0], top) + dot(picks[0], mid)) + dot(picks[0], low)
    top, mid, low = thirds(value)
    return (dot(top, picks[1]) + dot(mid, picks[1])) + dot(low, picks[1])


def turned(value, row, col):
    return pltpu.roll(pltpu.roll(value, row, 0), col, 1)


def run_copies(moves, sem):
    copies = [pltpu.make_async_copy(src, dst, sem.at[i]) for i, (src, dst) in enumerate(moves)]
    for copy in copies:
        copy.start()
    return copies


def load_body(pos_hbm, probe_hbm, object_hbm, pos_out, plane_out, object_out, sem):
    which = lax.rem(lax.axis_index("frame"), 2)
    half = object_hbm.shape[2] // 2
    moves = [(probe_hbm.at[0, which], plane_out), (pos_hbm, pos_out)]
    for s in range(2):
        for part in range(2):
            for at in (pl.ds(0, half), pl.ds(half, half)):
                moves.append((object_hbm.at[s, part, at], object_out.at[s, part, at]))
    for copy in run_copies(moves, sem):
        copy.wait()


def flipped(paired):
    return lax.axis_index("state") == 1 if paired else False


def turn_of(at_ref, size):
    return jnp.sum(at_ref[0:1, 0:1]), lax.rem(jnp.sum(at_ref[0:1, 1:2]), size)


def turn_body(at_ref, *refs):
    half = len(refs) // 2
    turn = turn_of(at_ref, refs[0].shape[1])
    for came, out in zip(refs[:half], refs[half:]):
        out[...] = turned(came[...], *turn)


def prepare_body(
    paired, at_ref, lent_ref, probe_hbm, prop_hbm, amp_hbm, tab_hbm,
    wave_re, wave_im, amp_out, first_out, tab_out,
    probe, prop, amp, sem,
):
    copies = run_copies(((probe_hbm, probe), (prop_hbm, prop), (amp_hbm, amp), (tab_hbm, tab_out)), sem)
    size = prop.shape[0]
    copies[0].wait()
    turn = turn_of(at_ref, size)
    for c in range(2):
        first_out[0, c] = turned(probe[0, c], *turn)
    copies[1].wait()
    phase = by_parity(prop[...])
    wave_re[...] = jnp.cos(phase)
    wave_im[...] = jnp.sin(phase)
    copies[2].wait()
    amp_out[...] = by_parity(jnp.where(flipped(paired), lent_ref[0], amp[0]))
    copies[3].wait()


def spread(ref, frame, which, shape):
    return jnp.broadcast_to(ref[frame : frame + 1, which : which + 1], shape)


def covered(paired, at_ref, frame, shape, start=0):
    gap = lax.broadcasted_iota(jnp.int32, shape, 0) + start - spread(at_ref, frame, 0, shape)
    gap = gap if frame else -1 - gap
    return jnp.where(flipped(paired), -1 - gap, gap) < 0


def wrapped(ref, s, part, at_ref, frame):
    size = ref.shape[-2]
    c = lax.broadcasted_iota(jnp.int32, (size, size), 1)
    return jnp.where(c < spread(at_ref, frame, 1, c.shape), ref[s, part, :, size:], ref[s, part, :, :size])


def send_body(paired, pos_ref, before_ref, object_ref, at_ref, zero_ref, one_ref):
    flip = flipped(paired)
    at_ref[0:1] = jnp.where(flip, before_ref[...], pos_ref[...])
    at_ref[1:2] = jnp.where(flip, pos_ref[...], before_ref[...])
    for s, out in enumerate((zero_ref, one_ref)):
        for part in range(2):
            out[part] = wrapped(object_ref, s, part, at_ref, 1)


def patch_of(paired, s, object_ref, halo_ref, at_ref):
    size = halo_ref.shape[-1]
    mine = covered(paired, at_ref, 0, (size, size))
    return [jnp.where(mine, wrapped(object_ref, s, part, at_ref, 0), halo_ref[part]) for part in range(2)]


def pair(ref, *at):
    return ref[(*at, 0)], ref[(*at, 1)]


def inner_body(paired, at_ref, object_ref, halo_ref, first_ref, kr_ref, ki_ref, tab, *refs):
    out_ref, probe_ref, patch = refs[-3:]
    states = out_ref.shape[0]
    patch[0], patch[1] = patch_of(paired, 0, object_ref, halo_ref, at_ref)
    swap = lax.rem(lax.axis_index("frame"), 2) == 1
    probe_ref[:1] = first_ref[...]
    for m, (came, given) in enumerate(zip(refs[:-3:2], refs[1:-3:2])):
        other = turned(given[...], *turn_of(at_ref, given.shape[1]))
        probe_ref[1 + m, 0] = jnp.where(swap, other, came[...])
        probe_ref[1 + m, 1] = jnp.where(swap, came[...], other)

    def body(group):
        waves = forward([times(pair(probe_ref, m), pair(patch)) for m in group], tab)
        waves = inverse([times((kr_ref[...], ki_ref[...]), wave) for wave in waves], tab)
        for m, wave in zip(group, waves):
            out_ref[m, 0], out_ref[m, 1] = wave

    in_groups(states, body)


def blocks_of(rows, paired):
    starts = [lax.axis_index("state")]
    if paired:
        starts.append(lax.rem(lax.axis_index("frame"), 2))
    return [pl.ds(pl.multiple_of(start * rows, rows), rows) for start in starts]


def middle_body(paired, rows, at_ref, object_ref, halo_ref, inner_ref, amp_ref, tab, *refs):
    chi_ref, patch, far, power = refs[-4:]
    terms = refs[:-4]
    states = inner_ref.shape[0]
    patch[0], patch[1] = patch_of(paired, 1, object_ref, halo_ref, at_ref)
    power[...] = jnp.zeros_like(power)

    def outward(group):
        waves = forward([times(pair(patch), pair(inner_ref, m)) for m in group], tab)
        total = power[...]
        for m, wave in zip(group, waves):
            far[m, 0], far[m, 1] = wave
            total += wave[0] * wave[0] + wave[1] * wave[1]
        power[...] = total

    in_groups(states, outward)
    power[...] = 1.0 - amp_ref[...] * lax.rsqrt(power[...] + 1.0)
    for term_ref in terms:
        term_ref[...] = jnp.zeros_like(term_ref)

    def homeward(group):
        waves = inverse([(power[...] * far[m, 0], power[...] * far[m, 1]) for m in group], tab)
        for m, wave in zip(group, waves):
            far[m, 0], far[m, 1] = wave
            chi_ref[m, 0], chi_ref[m, 1] = times_conj(pair(patch), wave)
        for term_ref, take in zip(terms, blocks_of(rows, paired)):
            for m in group:
                part = times_conj(
                    (inner_ref[m, 0, take], inner_ref[m, 1, take]), (far[m, 0, take], far[m, 1, take])
                )
                term_ref[0] += part[0]
                term_ref[1] += part[1]

    in_groups(states, homeward)


def front_term(m, take, front, probe_ref, tab, term_ref):
    wave = columns_inverse(front[m, 0, take], front[m, 1, take], tab)
    part = times_conj((probe_ref[m, 0, take], probe_ref[m, 1, take]), wave)
    term_ref[0] += part[0]
    term_ref[1] += part[1]


def last_body(paired, rows, chi_ref, probe_ref, kr_ref, ki_ref, tab, term_ref, front):
    states = chi_ref.shape[0]
    take = blocks_of(rows, paired)[-1]
    term_ref[...] = jnp.zeros_like(term_ref)

    def body(group):
        waves = forward([pair(chi_ref, m) for m in group], tab)
        waves = [rows_inverse(*times_conj((kr_ref[...], ki_ref[...]), wave), tab) for wave in waves]
        for m, wave in zip(group, waves):
            front[m, 0], front[m, 1] = wave
        for m in group:
            front_term(m, take, front, probe_ref, tab, term_ref)

    in_groups(states, body)


def keep_body(rows, front_ref, probe_ref, tab, term_ref):
    take = blocks_of(rows, True)[0]
    term_ref[...] = jnp.zeros_like(term_ref)

    def body(group):
        for m in group:
            front_term(m, take, front_ref, probe_ref, tab, term_ref)

    in_groups(front_ref.shape[0], body)


def gather_body(slice_id, paired, rows, at_ref, own_ref, came_ref, *refs):
    out_ref, held, sem = refs[-3:]
    size = own_ref.shape[-1]
    start = lax.axis_index("state") * rows
    c = lax.broadcasted_iota(jnp.int32, (rows, size), 1)
    here, there = (covered(paired, at_ref, frame, c.shape, start) for frame in range(2))
    here_right, there_right = (c < spread(at_ref, frame, 1, c.shape) for frame in range(2))
    chunks = 4 if rows % 32 == 0 else 1
    step = rows // chunks
    copies = []
    for chunk in range(chunks):
        at = pl.ds(chunk * step, step)
        cut = slice(chunk * step, chunk * step + step)
        for part in range(2):
            mine = jnp.where(here[cut], own_ref[part, at], 0.0)
            theirs = jnp.where(there[cut], came_ref[part, at], 0.0)
            left, right = here_right[cut], there_right[cut]
            held[part, at, :size] = jnp.where(left, 0.0, mine) + jnp.where(right, 0.0, theirs)
            held[part, at, size:] = jnp.where(left, mine, 0.0) + jnp.where(right, theirs, 0.0)
            copies.append(
                pltpu.make_async_copy(held.at[part, at], out_ref.at[slice_id, part, at], sem.at[len(copies)])
            )
            copies[-1].start()
    for copy in copies:
        copy.wait()


def gather(slice_id, paired, rows, size, at, own, came, *given):
    return pl.pallas_call(
        functools.partial(gather_body, slice_id, paired, rows),
        out_shape=jax.ShapeDtypeStruct((2, 2, rows, 2 * size), F32),
        in_specs=[VMEM] * 3 + [pl.BlockSpec(memory_space=pl.ANY)] * len(given),
        out_specs=pl.BlockSpec(memory_space=pl.ANY),
        scratch_shapes=[pltpu.VMEM((2, rows, 2 * size), F32), pltpu.SemaphoreType.DMA((8,))],
        input_output_aliases={3: 0} if given else {},
        compiler_params=pltpu.CompilerParams(vmem_limit_bytes=LIMIT),
        cost_estimate=pl.CostEstimate(flops=0, bytes_accessed=32 * rows * size, transcendentals=0),
    )(at, own, came, *given)


def on_device(object_slices, probe, amplitude, positions, propagator):
    states = lax.axis_size("state")
    size = amplitude.shape[1]
    rows = object_slices.shape[2] // states
    assert object_slices.shape[2:] == (size, 2 * size) and positions.shape[0] == 1
    assert lax.axis_size("frame") % 2 == 0
    return gradient_of(object_slices, probe, amplitude, positions, propagator, states, size, rows)


def routes(frames, paired):
    if not paired:
        up = [(i, (i + 1) % frames) for i in range(frames)]
        return "frame", [(j, i) for i, j in up], None, up
    halo, lend, give = [], [], []
    for f in range(frames):
        behind, ahead = (f - 1) % frames, (f + 1) % frames
        halo += [(2 * f, 2 * behind), (2 * f + 1, 2 * ahead + 1)]
        lend += [(2 * f + 1, 2 * ahead + 1)]
        give += [(2 * f, 2 * f + 1), (2 * f + 1, 2 * f - 1)] if f % 2 else [(2 * f, 2 * f + 2), (2 * f + 1, 2 * f)]
    return ("frame", "state"), halo, lend, give


def gradient_of(object_slices, probe, amplitude, positions, propagator, states, size, rows):
    paired = states == 2
    grid = (size, size)
    unit = size * size
    flops = 24 * size**3
    frames = lax.axis_size("frame")
    axes, halo_route, lend_route, give_route = routes(frames, paired)
    tab = tables(size)
    before = shifted(positions, "frame", 1)
    lent = lax.ppermute(amplitude, axes, lend_route) if paired else amplitude
    given = [in_hbm(x) for x in (positions, probe, object_slices)]
    pos, plane, held = pl.pallas_call(
        load_body,
        out_shape=[
            jax.ShapeDtypeStruct(positions.shape, jnp.int32),
            jax.ShapeDtypeStruct(grid, F32),
            jax.ShapeDtypeStruct(object_slices.shape, F32),
        ],
        in_specs=[HBM] * 3,
        out_specs=[VMEM] * 3,
        scratch_shapes=[pltpu.SemaphoreType.DMA((10,))],
        compiler_params=pltpu.CompilerParams(vmem_limit_bytes=LIMIT),
        cost_estimate=pl.CostEstimate(flops=0, bytes_accessed=40 * unit, transcendentals=0),
    )(*given)
    planes = []
    for by in range(1, states):
        planes.append(shifted(plane, "state", by))
    at, zero, one = pl.pallas_call(
        functools.partial(send_body, paired),
        out_shape=[jax.ShapeDtypeStruct((2, 2), jnp.int32)] + [jax.ShapeDtypeStruct((2,) + grid, F32)] * 2,
        in_specs=[VMEM] * 3,
        out_specs=[VMEM] * 3,
        compiler_params=pltpu.CompilerParams(vmem_limit_bytes=LIMIT),
        cost_estimate=pl.CostEstimate(flops=0, bytes_accessed=64 * unit, transcendentals=0),
    )(pos, before, held)
    halo_zero = lax.ppermute(zero, axes, halo_route)
    halo_one = lax.ppermute(one, axes, halo_route)
    kr, ki, amp, first, tab = pl.pallas_call(
        functools.partial(prepare_body, paired),
        out_shape=[jax.ShapeDtypeStruct(grid, F32)] * 3
        + [jax.ShapeDtypeStruct(x.shape, x.dtype) for x in (probe, tab)],
        in_specs=[VMEM] * 2 + [HBM] * 4,
        out_specs=[VMEM] * 5,
        scratch_shapes=[
            pltpu.VMEM(probe.shape, F32),
            pltpu.VMEM(grid, F32),
            pltpu.VMEM(amplitude.shape, F32),
            pltpu.SemaphoreType.DMA((4,)),
        ],
        compiler_params=pltpu.CompilerParams(vmem_limit_bytes=LIMIT),
        cost_estimate=pl.CostEstimate(flops=2 * size**3, bytes_accessed=60 * unit, transcendentals=0),
    )(at, lent, given[1], *(in_hbm(x) for x in (propagator, amplitude, tab)))
    own = call(turn_body, [grid] * len(planes), [VMEM] * (1 + len(planes)), moved=16 * unit)(at, *planes)
    pairs = []
    for came, kept in zip(planes, own):
        pairs += [kept, lax.ppermute(came, "frame", [(i, i ^ 1) for i in range(frames)])]
    waves, probes = call(
        functools.partial(inner_body, paired),
        [(states, 2) + grid] * 2,
        [VMEM] * (7 + len(pairs)),
        [pltpu.VMEM((2,) + grid, F32)],
        flops=2 * flops * states,
        moved=24 * unit * states,
    )(at, held, halo_zero, first, kr, ki, tab, *pairs)
    *terms, chi = call(
        functools.partial(middle_body, paired, rows),
        [(2, rows, size)] * (2 if paired else 1) + [(states, 2) + grid],
        [VMEM] * 6,
        [pltpu.VMEM((2,) + grid, F32), pltpu.VMEM((states, 2) + grid, F32), pltpu.VMEM(grid, F32)],
        flops=2 * flops * states,
        moved=32 * unit * states,
    )(at, held, halo_one, waves, amp, tab)
    came_one = lax.ppermute(terms[-1], axes, give_route)
    term_zero, front = call(
        functools.partial(last_body, paired, rows),
        [(2, rows, size), (states, 2) + grid],
        [VMEM] * 5,
        flops=2 * flops * states,
        moved=16 * unit * states,
    )(chi, probes, kr, ki, tab)
    came_zero = lax.ppermute(term_zero, axes, give_route)
    if paired:
        (term_zero,) = call(
            functools.partial(keep_body, rows),
            [(2, rows, size)],
            [VMEM] * 3,
            flops=flops * states // 8,
            moved=16 * unit,
        )(front, probes, tab)
    gradient = gather(1, paired, rows, size, at, terms[0], came_one)
    return gather(0, paired, rows, size, at, term_zero, came_zero, gradient)


def solution(mesh):
    return jax.shard_map(
        on_device,
        mesh=mesh,
        in_specs=(
            P(None, None, "frame", None),
            P("state", None, None, None),
            P("frame", None, None),
            P("frame", None),
            P(),
        ),
        out_specs=P(None, None, ("frame", "state"), None),
        check_vma=False,
    )
```

```python
import functools
import math

import jax
import jax.numpy as jnp
import numpy as np
from jax import lax
from jax.experimental import pallas as pl
from jax.experimental.pallas import tpu as pltpu
from jax.sharding import PartitionSpec as P


F32 = jnp.float32
BF16 = jnp.bfloat16
VMEM = pl.BlockSpec(memory_space=pltpu.VMEM)
HBM = pl.BlockSpec(memory_space=pltpu.MemorySpace.HBM)
SMEM = pl.BlockSpec(memory_space=pltpu.SMEM)
LIMIT = 24 * 1024 * 1024


def shifted(value, axis, by):
    count = lax.axis_size(axis)
    return lax.ppermute(value, axis, [(i, (i + by) % count) for i in range(count)])


def in_hbm(value):
    return pltpu.with_memory_space_constraint(value, pltpu.MemorySpace.HBM)


def call(body, outs, ins, scratch=(), flops=0, moved=0):
    return pl.pallas_call(
        body,
        out_shape=[jax.ShapeDtypeStruct(shape, F32) for shape in outs],
        in_specs=ins,
        out_specs=[VMEM] * len(outs),
        scratch_shapes=list(scratch),
        compiler_params=pltpu.CompilerParams(vmem_limit_bytes=LIMIT),
        cost_estimate=pl.CostEstimate(flops=flops, bytes_accessed=moved, transcendentals=0),
    )


def tables(length):
    half = length // 2
    n = np.arange(half)[:, None]
    forms = []
    for parity in (0, 1):
        k = 2 * np.arange(half)[None, :] + parity
        angle = -2.0 * math.pi * ((n * k) % length) / length
        re, im = np.cos(angle) / math.sqrt(length), np.sin(angle) / math.sqrt(length)
        right = np.block([[re, im], [-im, re]])
        forms += [right, right.T]
    stack = np.stack(forms).astype(np.float64)
    top = stack.astype(BF16)
    rest = (stack - top.astype(np.float64)).astype(BF16)
    return jnp.asarray(np.stack([top, rest]))


def halves(value):
    top = value.astype(BF16)
    return top, (value - top.astype(F32)).astype(BF16)


def dot(a, b):
    return lax.dot_general(a, b, (((1,), (0,)), ((), ())), preferred_element_type=F32)


def times_table(value, tab, which):
    top, rest = halves(value)
    return dot(top, tab[0, which]) + (dot(rest, tab[0, which]) + dot(top, tab[1, which]))


def table_times(value, tab, which):
    top, rest = halves(value)
    return dot(tab[0, which], top) + (dot(tab[0, which], rest) + dot(tab[1, which], top))


def columns_forward(re, im, tab):
    h = re.shape[1] // 2
    r0, r1, i0, i1 = re[:, :h], re[:, h:], im[:, :h], im[:, h:]
    even = times_table(jnp.concatenate([r0 + r1, i0 + i1], 1), tab, 0)
    odd = times_table(jnp.concatenate([r0 - r1, i0 - i1], 1), tab, 2)
    return (
        jnp.concatenate([even[:, :h], odd[:, :h]], 1),
        jnp.concatenate([even[:, h:], odd[:, h:]], 1),
    )


def columns_inverse(re, im, tab):
    h = re.shape[1] // 2
    even = times_table(jnp.concatenate([re[:, :h], im[:, :h]], 1), tab, 1)
    odd = times_table(jnp.concatenate([re[:, h:], im[:, h:]], 1), tab, 3)
    total, gap = even + odd, even - odd
    return (
        jnp.concatenate([total[:, :h], gap[:, :h]], 1),
        jnp.concatenate([total[:, h:], gap[:, h:]], 1),
    )


def rows_forward(re, im, tab):
    h = re.shape[0] // 2
    r0, r1, i0, i1 = re[:h], re[h:], im[:h], im[h:]
    even = table_times(jnp.concatenate([r0 + r1, i0 + i1], 0), tab, 1)
    odd = table_times(jnp.concatenate([r0 - r1, i0 - i1], 0), tab, 3)
    return (
        jnp.concatenate([even[:h], odd[:h]], 0),
        jnp.concatenate([even[h:], odd[h:]], 0),
    )


def rows_inverse(re, im, tab):
    h = re.shape[0] // 2
    even = table_times(jnp.concatenate([re[:h], im[:h]], 0), tab, 0)
    odd = table_times(jnp.concatenate([re[h:], im[h:]], 0), tab, 2)
    total, gap = even + odd, even - odd
    return (
        jnp.concatenate([total[:h], gap[:h]], 0),
        jnp.concatenate([total[h:], gap[h:]], 0),
    )


def forward(waves, tab):
    waves = [columns_forward(*wave, tab) for wave in waves]
    return [rows_forward(*wave, tab) for wave in waves]


def inverse(waves, tab):
    waves = [rows_inverse(*wave, tab) for wave in waves]
    return [columns_inverse(*wave, tab) for wave in waves]


def times(a, b):
    return a[0] * b[0] - a[1] * b[1], a[0] * b[1] + a[1] * b[0]


def times_conj(a, b):
    return a[0] * b[0] + a[1] * b[1], a[0] * b[1] - a[1] * b[0]


def in_groups(states, body):
    group = 2 if states % 2 == 0 else 1
    if states == group:
        body([m for m in range(group)])
        return

    def step(g, carry):
        body([g * group + m for m in range(group)])
        return carry

    lax.fori_loop(0, states // group, step, 0)


def thirds(value):
    top = value.astype(BF16)
    left = value - top.astype(F32)
    mid = left.astype(BF16)
    return top, mid, (left - mid.astype(F32)).astype(BF16)


def by_parity(value):
    size = value.shape[0]
    h = size // 2
    picks = []
    for along in (0, 1):
        place = lax.broadcasted_iota(jnp.int32, (size, size), along)
        source = lax.broadcasted_iota(jnp.int32, (size, size), 1 - along)
        wanted = jnp.where(place < h, 2 * place, 2 * (place - h) + 1)
        picks.append(jnp.where(source == wanted, 1.0, 0.0).astype(BF16))
    top, mid, low = thirds(value)
    value = (dot(picks[0], top) + dot(picks[0], mid)) + dot(picks[0], low)
    top, mid, low = thirds(value)
    return (dot(top, picks[1]) + dot(mid, picks[1])) + dot(low, picks[1])


def turned(value, row, col):
    return pltpu.roll(pltpu.roll(value, row, 0), col, 1)


def run_copies(moves, sem):
    copies = [pltpu.make_async_copy(src, dst, sem.at[i]) for i, (src, dst) in enumerate(moves)]
    for copy in copies:
        copy.start()
    return copies


def load_body(pos_hbm, probe_hbm, object_hbm, pos_out, plane_out, object_out, sem):
    which = lax.rem(lax.axis_index("frame"), 2)
    half = object_hbm.shape[2] // 2
    moves = [(probe_hbm.at[0, which], plane_out), (pos_hbm, pos_out)]
    for s in range(2):
        for part in range(2):
            for at in (pl.ds(0, half), pl.ds(half, half)):
                moves.append((object_hbm.at[s, part, at], object_out.at[s, part, at]))
    for copy in run_copies(moves, sem):
        copy.wait()


def flipped(paired):
    return lax.axis_index("state") == 1 if paired else False


def turn_of(at_ref, size):
    return jnp.sum(at_ref[0:1, 0:1]), lax.rem(jnp.sum(at_ref[0:1, 1:2]), size)


def turn_body(at_ref, *refs):
    half = len(refs) // 2
    turn = turn_of(at_ref, refs[0].shape[1])
    for came, out in zip(refs[:half], refs[half:]):
        out[...] = turned(came[...], *turn)


def prepare_body(
    paired, pos_ref, before_ref, over_ref, probe_hbm, prop_hbm, tab_hbm,
    at_ref, wave_re, wave_im, first_out, tab_out,
    probe, prop, sem,
):
    copies = run_copies(((probe_hbm, probe), (prop_hbm, prop), (tab_hbm, tab_out)), sem)
    flip = flipped(paired)
    at_ref[0:1] = jnp.where(flip, over_ref[...], pos_ref[...])
    at_ref[1:2] = jnp.where(flip, pos_ref[...], before_ref[...])
    size = prop.shape[0]
    copies[0].wait()
    turn = turn_of(at_ref, size)
    for c in range(2):
        first_out[0, c] = turned(probe[0, c], *turn)
    copies[1].wait()
    phase = by_parity(prop[...])
    wave_re[...] = jnp.cos(phase)
    wave_im[...] = jnp.sin(phase)
    copies[2].wait()


def measure_body(paired, amp_ref, lent_ref, out_ref):
    out_ref[...] = by_parity(jnp.where(flipped(paired), lent_ref[0], amp_ref[0]))


def spread(ref, frame, which, shape):
    return jnp.broadcast_to(ref[frame : frame + 1, which : which + 1], shape)


def covered(paired, at_ref, frame, shape, start=0):
    gap = lax.broadcasted_iota(jnp.int32, shape, 0) + start - spread(at_ref, frame, 0, shape)
    gap = gap if frame else -1 - gap
    return jnp.where(flipped(paired), -1 - gap, gap) < 0


def wrapped(ref, s, part, at_ref, frame):
    size = ref.shape[-2]
    c = lax.broadcasted_iota(jnp.int32, (size, size), 1)
    return jnp.where(c < spread(at_ref, frame, 1, c.shape), ref[s, part, :, size:], ref[s, part, :, :size])


def send_body(paired, pos_ref, before_ref, object_ref, zero_ref, one_ref, to_ref):
    to_ref[...] = jnp.where(flipped(paired), pos_ref[...], before_ref[...])
    for s, out in enumerate((zero_ref, one_ref)):
        for part in range(2):
            out[part] = wrapped(object_ref, s, part, to_ref, 0)


def patch_of(paired, s, object_ref, halo_ref, at_ref):
    size = halo_ref.shape[-1]
    mine = covered(paired, at_ref, 0, (size, size))
    return [jnp.where(mine, wrapped(object_ref, s, part, at_ref, 0), halo_ref[part]) for part in range(2)]


def pair(ref, *at):
    return ref[(*at, 0)], ref[(*at, 1)]


def inner_body(paired, at_ref, object_ref, halo_ref, first_ref, kr_ref, ki_ref, tab, *refs):
    out_ref, probe_ref, patch = refs[-3:]
    states = out_ref.shape[0]
    patch[0], patch[1] = patch_of(paired, 0, object_ref, halo_ref, at_ref)
    swap = lax.rem(lax.axis_index("frame"), 2) == 1
    probe_ref[:1] = first_ref[...]
    for m, (came, given) in enumerate(zip(refs[:-3:2], refs[1:-3:2])):
        other = turned(given[...], *turn_of(at_ref, given.shape[1]))
        probe_ref[1 + m, 0] = jnp.where(swap, other, came[...])
        probe_ref[1 + m, 1] = jnp.where(swap, came[...], other)

    def body(group):
        waves = forward([times(pair(probe_ref, m), pair(patch)) for m in group], tab)
        waves = inverse([times((kr_ref[...], ki_ref[...]), wave) for wave in waves], tab)
        for m, wave in zip(group, waves):
            out_ref[m, 0], out_ref[m, 1] = wave

    in_groups(states, body)


def blocks_of(rows, paired):
    starts = [lax.axis_index("state")]
    if paired:
        starts.append(lax.rem(lax.axis_index("frame"), 2))
    return [pl.ds(pl.multiple_of(start * rows, rows), rows) for start in starts]


def middle_body(paired, rows, at_ref, object_ref, halo_ref, inner_ref, amp_ref, tab, *refs):
    chi_ref, patch, far, power = refs[-4:]
    terms = refs[:-4]
    states = inner_ref.shape[0]
    patch[0], patch[1] = patch_of(paired, 1, object_ref, halo_ref, at_ref)
    power[...] = jnp.zeros_like(power)

    def outward(group):
        waves = forward([times(pair(patch), pair(inner_ref, m)) for m in group], tab)
        total = power[...]
        for m, wave in zip(group, waves):
            far[m, 0], far[m, 1] = wave
            total += wave[0] * wave[0] + wave[1] * wave[1]
        power[...] = total

    in_groups(states, outward)
    power[...] = 1.0 - amp_ref[...] * lax.rsqrt(power[...] + 1.0)
    for term_ref in terms:
        term_ref[...] = jnp.zeros_like(term_ref)

    def homeward(group):
        waves = inverse([(power[...] * far[m, 0], power[...] * far[m, 1]) for m in group], tab)
        for m, wave in zip(group, waves):
            far[m, 0], far[m, 1] = wave
            chi_ref[m, 0], chi_ref[m, 1] = times_conj(pair(patch), wave)
        for term_ref, take in zip(terms, blocks_of(rows, paired)):
            for m in group:
                part = times_conj(
                    (inner_ref[m, 0, take], inner_ref[m, 1, take]), (far[m, 0, take], far[m, 1, take])
                )
                term_ref[0] += part[0]
                term_ref[1] += part[1]

    in_groups(states, homeward)


def front_term(m, take, front, probe_ref, tab, term_ref):
    wave = columns_inverse(front[m, 0, take], front[m, 1, take], tab)
    part = times_conj((probe_ref[m, 0, take], probe_ref[m, 1, take]), wave)
    term_ref[0] += part[0]
    term_ref[1] += part[1]


def last_body(paired, rows, chi_ref, probe_ref, kr_ref, ki_ref, tab, term_ref, front):
    states = chi_ref.shape[0]
    take = blocks_of(rows, paired)[-1]
    term_ref[...] = jnp.zeros_like(term_ref)

    def body(group):
        waves = forward([pair(chi_ref, m) for m in group], tab)
        waves = [rows_inverse(*times_conj((kr_ref[...], ki_ref[...]), wave), tab) for wave in waves]
        for m, wave in zip(group, waves):
            front[m, 0], front[m, 1] = wave
        for m in group:
            front_term(m, take, front, probe_ref, tab, term_ref)

    in_groups(states, body)


def keep_body(rows, front_ref, probe_ref, tab, term_ref):
    take = blocks_of(rows, True)[0]
    term_ref[...] = jnp.zeros_like(term_ref)

    def body(group):
        for m in group:
            front_term(m, take, front_ref, probe_ref, tab, term_ref)

    in_groups(front_ref.shape[0], body)


def gather_body(slice_id, paired, rows, at_ref, own_ref, came_ref, *refs):
    out_ref, held, sem = refs[-3:]
    size = own_ref.shape[-1]
    start = lax.axis_index("state") * rows
    c = lax.broadcasted_iota(jnp.int32, (rows, size), 1)
    here, there = (covered(paired, at_ref, frame, c.shape, start) for frame in range(2))
    here_right, there_right = (c < spread(at_ref, frame, 1, c.shape) for frame in range(2))
    chunks = 4 if rows % 32 == 0 else 1
    step = rows // chunks
    copies = []
    for chunk in range(chunks):
        at = pl.ds(chunk * step, step)
        cut = slice(chunk * step, chunk * step + step)
        for part in range(2):
            mine = jnp.where(here[cut], own_ref[part, at], 0.0)
            theirs = jnp.where(there[cut], came_ref[part, at], 0.0)
            left, right = here_right[cut], there_right[cut]
            held[part, at, :size] = jnp.where(left, 0.0, mine) + jnp.where(right, 0.0, theirs)
            held[part, at, size:] = jnp.where(left, mine, 0.0) + jnp.where(right, theirs, 0.0)
            copies.append(
                pltpu.make_async_copy(held.at[part, at], out_ref.at[slice_id, part, at], sem.at[len(copies)])
            )
            copies[-1].start()
    for copy in copies:
        copy.wait()


def gather(slice_id, paired, rows, size, at, own, came, *given):
    return pl.pallas_call(
        functools.partial(gather_body, slice_id, paired, rows),
        out_shape=jax.ShapeDtypeStruct((2, 2, rows, 2 * size), F32),
        in_specs=[VMEM] * 3 + [pl.BlockSpec(memory_space=pl.ANY)] * len(given),
        out_specs=pl.BlockSpec(memory_space=pl.ANY),
        scratch_shapes=[pltpu.VMEM((2, rows, 2 * size), F32), pltpu.SemaphoreType.DMA((8,))],
        input_output_aliases={3: 0} if given else {},
        compiler_params=pltpu.CompilerParams(vmem_limit_bytes=LIMIT),
        cost_estimate=pl.CostEstimate(flops=0, bytes_accessed=32 * rows * size, transcendentals=0),
    )(at, own, came, *given)


def on_device(object_slices, probe, amplitude, positions, propagator):
    states = lax.axis_size("state")
    size = amplitude.shape[1]
    rows = object_slices.shape[2] // states
    assert object_slices.shape[2:] == (size, 2 * size) and positions.shape[0] == 1
    assert lax.axis_size("frame") % 2 == 0
    return gradient_of(object_slices, probe, amplitude, positions, propagator, states, size, rows)


def routes(frames, paired):
    if not paired:
        up = [(i, (i + 1) % frames) for i in range(frames)]
        return "frame", [(j, i) for i, j in up], None, up
    halo, lend, give = [], [], []
    for f in range(frames):
        behind, ahead = (f - 1) % frames, (f + 1) % frames
        halo += [(2 * f, 2 * behind), (2 * f + 1, 2 * ahead + 1)]
        lend += [(2 * f, 2 * ahead + 1)]
        give += [(2 * f, 2 * f + 1), (2 * f + 1, 2 * f - 1)] if f % 2 else [(2 * f, 2 * f + 2), (2 * f + 1, 2 * f)]
    return ("frame", "state"), halo, lend, give


def gradient_of(object_slices, probe, amplitude, positions, propagator, states, size, rows):
    paired = states == 2
    grid = (size, size)
    unit = size * size
    flops = 24 * size**3
    frames = lax.axis_size("frame")
    axes, halo_route, lend_route, give_route = routes(frames, paired)
    tab = tables(size)
    up = [(i, (i + 1) % frames) for i in range(frames)]
    before = lax.ppermute(positions, axes, [(2 * i, 2 * j) for i, j in up] if paired else up)
    over = lax.ppermute(positions, axes, [(2 * i + 1, 2 * j + 1) for i, j in up]) if paired else before
    given = [in_hbm(x) for x in (positions, probe, object_slices)]
    pos, plane, held = pl.pallas_call(
        load_body,
        out_shape=[
            jax.ShapeDtypeStruct(positions.shape, jnp.int32),
            jax.ShapeDtypeStruct(grid, F32),
            jax.ShapeDtypeStruct(object_slices.shape, F32),
        ],
        in_specs=[HBM] * 3,
        out_specs=[VMEM] * 3,
        scratch_shapes=[pltpu.SemaphoreType.DMA((10,))],
        compiler_params=pltpu.CompilerParams(vmem_limit_bytes=LIMIT),
        cost_estimate=pl.CostEstimate(flops=0, bytes_accessed=40 * unit, transcendentals=0),
    )(*given)
    planes = []
    for by in range(1, states):
        planes.append(shifted(plane, "state", by))
    zero, one = call(
        functools.partial(send_body, paired),
        [(2,) + grid] * 2,
        [VMEM] * 3,
        [pltpu.VMEM(positions.shape, jnp.int32)],
        moved=64 * unit,
    )(pos, before, held)
    halo_zero = lax.ppermute(zero, axes, halo_route)
    halo_one = lax.ppermute(one, axes, halo_route)
    lent = lax.ppermute(amplitude, axes, lend_route) if paired else amplitude
    at, kr, ki, first, tab = pl.pallas_call(
        functools.partial(prepare_body, paired),
        out_shape=[jax.ShapeDtypeStruct((2, 2), jnp.int32)]
        + [jax.ShapeDtypeStruct(grid, F32)] * 2
        + [jax.ShapeDtypeStruct(x.shape, x.dtype) for x in (probe, tab)],
        in_specs=[VMEM] * 3 + [HBM] * 3,
        out_specs=[VMEM] * 5,
        scratch_shapes=[pltpu.VMEM(probe.shape, F32), pltpu.VMEM(grid, F32), pltpu.SemaphoreType.DMA((3,))],
        compiler_params=pltpu.CompilerParams(vmem_limit_bytes=LIMIT),
        cost_estimate=pl.CostEstimate(flops=2 * size**3, bytes_accessed=60 * unit, transcendentals=0),
    )(pos, before, over, given[1], in_hbm(propagator), in_hbm(tab))
    own = call(turn_body, [grid] * len(planes), [VMEM] * (1 + len(planes)), moved=16 * unit)(at, *planes)
    pairs = []
    for came, kept in zip(planes, own):
        pairs += [kept, lax.ppermute(came, "frame", [(i, i ^ 1) for i in range(frames)])]
    (amp,) = call(functools.partial(measure_body, paired), [grid], [VMEM] * 2, flops=size**3, moved=12 * unit)(
        amplitude, lent
    )
    waves, probes = call(
        functools.partial(inner_body, paired),
        [(states, 2) + grid] * 2,
        [VMEM] * (7 + len(pairs)),
        [pltpu.VMEM((2,) + grid, F32)],
        flops=2 * flops * states,
        moved=24 * unit * states,
    )(at, held, halo_zero, first, kr, ki, tab, *pairs)
    *terms, chi = call(
        functools.partial(middle_body, paired, rows),
        [(2, rows, size)] * (2 if paired else 1) + [(states, 2) + grid],
        [VMEM] * 6,
        [pltpu.VMEM((2,) + grid, F32), pltpu.VMEM((states, 2) + grid, F32), pltpu.VMEM(grid, F32)],
        flops=2 * flops * states,
        moved=32 * unit * states,
    )(at, held, halo_one, waves, amp, tab)
    came_one = lax.ppermute(terms[-1], axes, give_route)
    term_zero, front = call(
        functools.partial(last_body, paired, rows),
        [(2, rows, size), (states, 2) + grid],
        [VMEM] * 5,
        flops=2 * flops * states,
        moved=16 * unit * states,
    )(chi, probes, kr, ki, tab)
    came_zero = lax.ppermute(term_zero, axes, give_route)
    if paired:
        (term_zero,) = call(
            functools.partial(keep_body, rows),
            [(2, rows, size)],
            [VMEM] * 3,
            flops=flops * states // 8,
            moved=16 * unit,
        )(front, probes, tab)
    gradient = gather(1, paired, rows, size, at, terms[0], came_one)
    return gather(0, paired, rows, size, at, term_zero, came_zero, gradient)


def solution(mesh):
    return jax.shard_map(
        on_device,
        mesh=mesh,
        in_specs=(
            P(None, None, "frame", None),
            P("state", None, None, None),
            P("frame", None, None),
            P("frame", None),
            P(),
        ),
        out_specs=P(None, None, ("frame", "state"), None),
        check_vma=False,
    )
```

```python
import functools
import math

import jax
import jax.numpy as jnp
import numpy as np
from jax import lax
from jax.experimental import pallas as pl
from jax.experimental.pallas import tpu as pltpu
from jax.sharding import PartitionSpec as P


F32 = jnp.float32
BF16 = jnp.bfloat16
VMEM = pl.BlockSpec(memory_space=pltpu.VMEM)
HBM = pl.BlockSpec(memory_space=pltpu.MemorySpace.HBM)
SMEM = pl.BlockSpec(memory_space=pltpu.SMEM)
LIMIT = 24 * 1024 * 1024


def shifted(value, axis, by):
    count = lax.axis_size(axis)
    return lax.ppermute(value, axis, [(i, (i + by) % count) for i in range(count)])


def in_hbm(value):
    return pltpu.with_memory_space_constraint(value, pltpu.MemorySpace.HBM)


def call(body, outs, ins, scratch=(), flops=0, moved=0):
    return pl.pallas_call(
        body,
        out_shape=[jax.ShapeDtypeStruct(shape, F32) for shape in outs],
        in_specs=ins,
        out_specs=[VMEM] * len(outs),
        scratch_shapes=list(scratch),
        compiler_params=pltpu.CompilerParams(vmem_limit_bytes=LIMIT),
        cost_estimate=pl.CostEstimate(flops=flops, bytes_accessed=moved, transcendentals=0),
    )


def tables(length):
    half = length // 2
    n = np.arange(half)[:, None]
    forms = []
    for parity in (0, 1):
        k = 2 * np.arange(half)[None, :] + parity
        angle = -2.0 * math.pi * ((n * k) % length) / length
        re, im = np.cos(angle) / math.sqrt(length), np.sin(angle) / math.sqrt(length)
        right = np.block([[re, im], [-im, re]])
        forms += [right, right.T]
    stack = np.stack(forms).astype(np.float64)
    top = stack.astype(BF16)
    rest = (stack - top.astype(np.float64)).astype(BF16)
    return jnp.asarray(np.stack([top, rest]))


def halves(value):
    top = value.astype(BF16)
    return top, (value - top.astype(F32)).astype(BF16)


def dot(a, b):
    return lax.dot_general(a, b, (((1,), (0,)), ((), ())), preferred_element_type=F32)


def times_table(value, tab, which):
    top, rest = halves(value)
    return dot(top, tab[0, which]) + (dot(rest, tab[0, which]) + dot(top, tab[1, which]))


def table_times(value, tab, which):
    top, rest = halves(value)
    return dot(tab[0, which], top) + (dot(tab[0, which], rest) + dot(tab[1, which], top))


def columns_forward(re, im, tab):
    h = re.shape[1] // 2
    r0, r1, i0, i1 = re[:, :h], re[:, h:], im[:, :h], im[:, h:]
    even = times_table(jnp.concatenate([r0 + r1, i0 + i1], 1), tab, 0)
    odd = times_table(jnp.concatenate([r0 - r1, i0 - i1], 1), tab, 2)
    return (
        jnp.concatenate([even[:, :h], odd[:, :h]], 1),
        jnp.concatenate([even[:, h:], odd[:, h:]], 1),
    )


def columns_inverse(re, im, tab):
    h = re.shape[1] // 2
    even = times_table(jnp.concatenate([re[:, :h], im[:, :h]], 1), tab, 1)
    odd = times_table(jnp.concatenate([re[:, h:], im[:, h:]], 1), tab, 3)
    total, gap = even + odd, even - odd
    return (
        jnp.concatenate([total[:, :h], gap[:, :h]], 1),
        jnp.concatenate([total[:, h:], gap[:, h:]], 1),
    )


def rows_forward(re, im, tab):
    h = re.shape[0] // 2
    r0, r1, i0, i1 = re[:h], re[h:], im[:h], im[h:]
    even = table_times(jnp.concatenate([r0 + r1, i0 + i1], 0), tab, 1)
    odd = table_times(jnp.concatenate([r0 - r1, i0 - i1], 0), tab, 3)
    return (
        jnp.concatenate([even[:h], odd[:h]], 0),
        jnp.concatenate([even[h:], odd[h:]], 0),
    )


def rows_inverse(re, im, tab):
    h = re.shape[0] // 2
    even = table_times(jnp.concatenate([re[:h], im[:h]], 0), tab, 0)
    odd = table_times(jnp.concatenate([re[h:], im[h:]], 0), tab, 2)
    total, gap = even + odd, even - odd
    return (
        jnp.concatenate([total[:h], gap[:h]], 0),
        jnp.concatenate([total[h:], gap[h:]], 0),
    )


def forward(waves, tab):
    waves = [columns_forward(*wave, tab) for wave in waves]
    return [rows_forward(*wave, tab) for wave in waves]


def inverse(waves, tab):
    waves = [rows_inverse(*wave, tab) for wave in waves]
    return [columns_inverse(*wave, tab) for wave in waves]


def times(a, b):
    return a[0] * b[0] - a[1] * b[1], a[0] * b[1] + a[1] * b[0]


def times_conj(a, b):
    return a[0] * b[0] + a[1] * b[1], a[0] * b[1] - a[1] * b[0]


def in_groups(states, body):
    group = 2 if states % 2 == 0 else 1
    if states == group:
        body([m for m in range(group)])
        return

    def step(g, carry):
        body([g * group + m for m in range(group)])
        return carry

    lax.fori_loop(0, states // group, step, 0)


def thirds(value):
    top = value.astype(BF16)
    left = value - top.astype(F32)
    mid = left.astype(BF16)
    return top, mid, (left - mid.astype(F32)).astype(BF16)


def by_parity(value):
    size = value.shape[0]
    h = size // 2
    picks = []
    for along in (0, 1):
        place = lax.broadcasted_iota(jnp.int32, (size, size), along)
        source = lax.broadcasted_iota(jnp.int32, (size, size), 1 - along)
        wanted = jnp.where(place < h, 2 * place, 2 * (place - h) + 1)
        picks.append(jnp.where(source == wanted, 1.0, 0.0).astype(BF16))
    top, mid, low = thirds(value)
    value = (dot(picks[0], top) + dot(picks[0], mid)) + dot(picks[0], low)
    top, mid, low = thirds(value)
    return (dot(top, picks[1]) + dot(mid, picks[1])) + dot(low, picks[1])


def turned(value, row, col):
    return pltpu.roll(pltpu.roll(value, row, 0), col, 1)


def run_copies(moves, sem):
    copies = [pltpu.make_async_copy(src, dst, sem.at[i]) for i, (src, dst) in enumerate(moves)]
    for copy in copies:
        copy.start()
    return copies


def quarters(object_hbm, s, out):
    half = object_hbm.shape[2] // 2
    return [
        (object_hbm.at[s, part, at], out.at[part, at])
        for part in range(2)
        for at in (pl.ds(0, half), pl.ds(half, half))
    ]


def load_body(pos_hbm, probe_hbm, object_hbm, pos_out, plane_out, object_out, sem):
    which = lax.rem(lax.axis_index("frame"), 2)
    moves = [(probe_hbm.at[0, which], plane_out), (pos_hbm, pos_out)] + quarters(object_hbm, 0, object_out)
    for copy in run_copies(moves, sem):
        copy.wait()


def turn_of(pos_ref, size):
    return jnp.sum(pos_ref[0:1, 0:1]), lax.rem(jnp.sum(pos_ref[0:1, 1:2]), size)


def turn_body(pos_ref, *refs):
    half = len(refs) // 2
    turn = turn_of(pos_ref, refs[0].shape[1])
    for came, out in zip(refs[:half], refs[half:]):
        out[...] = turned(came[...], *turn)


def prepare_body(
    pos_hbm, probe_hbm, prop_hbm, amp_hbm, tab_hbm,
    wave_re, wave_im, amp_out, first_out, tab_out,
    pos, probe, prop, amp, sem,
):
    copies = run_copies(
        ((pos_hbm, pos), (probe_hbm, probe), (prop_hbm, prop), (amp_hbm, amp), (tab_hbm, tab_out)), sem
    )
    copies[0].wait()
    copies[1].wait()
    size = prop.shape[0]
    row, col = pos[0, 0], lax.rem(pos[0, 1], size)
    for c in range(2):
        first_out[0, c] = turned(probe[0, c], row, col)
    copies[2].wait()
    phase = by_parity(prop[...])
    wave_re[...] = jnp.cos(phase)
    wave_im[...] = jnp.sin(phase)
    copies[3].wait()
    amp_out[...] = by_parity(amp[0])
    copies[4].wait()


def spread(ref, which, shape):
    return jnp.broadcast_to(ref[0:1, which : which + 1], shape)


def wrapped(ref, part, col_ref):
    size = ref.shape[-2]
    c = lax.broadcasted_iota(jnp.int32, (size, size), 1)
    return jnp.where(c < spread(col_ref, 1, c.shape), ref[part, :, size:], ref[part, :, :size])


def send_body(before_ref, object_ref, out_ref):
    for part in range(2):
        out_ref[part] = wrapped(object_ref, part, before_ref)


def load_send_body(before_ref, object_hbm, object_out, out_ref, sem):
    copies = run_copies(quarters(object_hbm, 1, object_out), sem)
    for copy in copies:
        copy.wait()
    send_body(before_ref, object_out, out_ref)


def patch_of(object_ref, halo_ref, pos_ref):
    size = halo_ref.shape[-1]
    r = lax.broadcasted_iota(jnp.int32, (size, size), 0)
    return [
        jnp.where(r < spread(pos_ref, 0, r.shape), halo_ref[part], wrapped(object_ref, part, pos_ref))
        for part in range(2)
    ]


def pair(ref, *at):
    return ref[(*at, 0)], ref[(*at, 1)]


def inner_body(pos_ref, object_ref, halo_ref, first_ref, kr_ref, ki_ref, tab, *refs):
    out_ref, probe_ref, patch = refs[-3:]
    states = out_ref.shape[0]
    patch[0], patch[1] = patch_of(object_ref, halo_ref, pos_ref)
    swap = lax.rem(lax.axis_index("frame"), 2) == 1
    probe_ref[:1] = first_ref[...]
    for m, (came, given) in enumerate(zip(refs[:-3:2], refs[1:-3:2])):
        other = turned(given[...], *turn_of(pos_ref, given.shape[1]))
        probe_ref[1 + m, 0] = jnp.where(swap, other, came[...])
        probe_ref[1 + m, 1] = jnp.where(swap, came[...], other)

    def body(group):
        waves = forward([times(pair(probe_ref, m), pair(patch)) for m in group], tab)
        waves = inverse([times((kr_ref[...], ki_ref[...]), wave) for wave in waves], tab)
        for m, wave in zip(group, waves):
            out_ref[m, 0], out_ref[m, 1] = wave

    in_groups(states, body)


def middle_body(rows, pos_ref, object_ref, halo_ref, inner_ref, amp_ref, tab, term_ref, half_ref, patch, far, power):
    states = inner_ref.shape[0]
    patch[0], patch[1] = patch_of(object_ref, halo_ref, pos_ref)
    power[...] = jnp.zeros_like(power)

    def outward(group):
        waves = forward([times(pair(patch), pair(inner_ref, m)) for m in group], tab)
        total = power[...]
        for m, wave in zip(group, waves):
            far[m, 0], far[m, 1] = wave
            total += wave[0] * wave[0] + wave[1] * wave[1]
        power[...] = total

    in_groups(states, outward)
    power[...] = 1.0 - amp_ref[...] * lax.rsqrt(power[...] + 1.0)
    term_ref[...] = jnp.zeros_like(term_ref)
    take = pl.ds(pl.multiple_of(lax.axis_index("state") * rows, rows), rows)

    def homeward(group):
        waves = [rows_inverse(power[...] * far[m, 0], power[...] * far[m, 1], tab) for m in group]
        for m, wave in zip(group, waves):
            half_ref[m, 0], half_ref[m, 1] = wave
        for m in group:
            wave = columns_inverse(half_ref[m, 0, take], half_ref[m, 1, take], tab)
            part = times_conj((inner_ref[m, 0, take], inner_ref[m, 1, take]), wave)
            term_ref[0] += part[0]
            term_ref[1] += part[1]

    in_groups(states, homeward)


def last_body(rows, half_ref, patch, probe_ref, kr_ref, ki_ref, tab, term_ref, front):
    states = half_ref.shape[0]
    take = pl.ds(pl.multiple_of(lax.axis_index("state") * rows, rows), rows)
    term_ref[...] = jnp.zeros_like(term_ref)

    def body(group):
        waves = [columns_inverse(*pair(half_ref, m), tab) for m in group]
        waves = forward([times_conj(pair(patch), wave) for wave in waves], tab)
        waves = [rows_inverse(*times_conj((kr_ref[...], ki_ref[...]), wave), tab) for wave in waves]
        for m, wave in zip(group, waves):
            front[m, 0], front[m, 1] = wave
        for m in group:
            wave = columns_inverse(front[m, 0, take], front[m, 1, take], tab)
            part = times_conj((probe_ref[m, 0, take], probe_ref[m, 1, take]), wave)
            term_ref[0] += part[0]
            term_ref[1] += part[1]

    in_groups(states, body)


def gather_body(slice_id, rows, pos_ref, before_ref, own_ref, came_ref, *refs):
    out_ref, held, sem = refs[-3:]
    size = own_ref.shape[-1]
    start = lax.axis_index("state") * rows
    r = lax.broadcasted_iota(jnp.int32, (rows, size), 0) + start
    c = lax.broadcasted_iota(jnp.int32, (rows, size), 1)
    here, there = r >= spread(pos_ref, 0, r.shape), r < spread(before_ref, 0, r.shape)
    here_right, there_right = c < spread(pos_ref, 1, c.shape), c < spread(before_ref, 1, c.shape)
    chunks = 4 if rows % 32 == 0 else 1
    step = rows // chunks
    copies = []
    for chunk in range(chunks):
        at = pl.ds(chunk * step, step)
        cut = slice(chunk * step, chunk * step + step)
        for part in range(2):
            mine = jnp.where(here[cut], own_ref[part, at], 0.0)
            theirs = jnp.where(there[cut], came_ref[part, at], 0.0)
            left, right = here_right[cut], there_right[cut]
            held[part, at, :size] = jnp.where(left, 0.0, mine) + jnp.where(right, 0.0, theirs)
            held[part, at, size:] = jnp.where(left, mine, 0.0) + jnp.where(right, theirs, 0.0)
            copies.append(
                pltpu.make_async_copy(held.at[part, at], out_ref.at[slice_id, part, at], sem.at[len(copies)])
            )
            copies[-1].start()
    for copy in copies:
        copy.wait()


def gather(slice_id, rows, size, pos, before, own, came, *given):
    return pl.pallas_call(
        functools.partial(gather_body, slice_id, rows),
        out_shape=jax.ShapeDtypeStruct((2, 2, rows, 2 * size), F32),
        in_specs=[VMEM] * 4 + [pl.BlockSpec(memory_space=pl.ANY)] * len(given),
        out_specs=pl.BlockSpec(memory_space=pl.ANY),
        scratch_shapes=[pltpu.VMEM((2, rows, 2 * size), F32), pltpu.SemaphoreType.DMA((8,))],
        input_output_aliases={4: 0} if given else {},
        compiler_params=pltpu.CompilerParams(vmem_limit_bytes=LIMIT),
        cost_estimate=pl.CostEstimate(flops=0, bytes_accessed=32 * rows * size, transcendentals=0),
    )(pos, before, own, came, *given)


def on_device(object_slices, probe, amplitude, positions, propagator):
    states = lax.axis_size("state")
    size = amplitude.shape[1]
    rows = object_slices.shape[2] // states
    assert object_slices.shape[2:] == (size, 2 * size) and positions.shape[0] == 1
    assert lax.axis_size("frame") % 2 == 0
    return gradient_of(object_slices, probe, amplitude, positions, propagator, states, size, rows)


def gradient_of(object_slices, probe, amplitude, positions, propagator, states, size, rows):
    grid = (size, size)
    unit = size * size
    flops = 24 * size**3
    tab = tables(size)
    before = shifted(positions, "frame", 1)
    given = [in_hbm(x) for x in (positions, probe, object_slices)]
    pos, plane, held_zero = pl.pallas_call(
        load_body,
        out_shape=[
            jax.ShapeDtypeStruct(positions.shape, jnp.int32),
            jax.ShapeDtypeStruct(grid, F32),
            jax.ShapeDtypeStruct(object_slices.shape[1:], F32),
        ],
        in_specs=[HBM] * 3,
        out_specs=[VMEM] * 3,
        scratch_shapes=[pltpu.SemaphoreType.DMA((6,))],
        compiler_params=pltpu.CompilerParams(vmem_limit_bytes=LIMIT),
        cost_estimate=pl.CostEstimate(flops=0, bytes_accessed=24 * unit, transcendentals=0),
    )(*given)
    planes = []
    for by in range(1, states):
        planes.append(shifted(plane, "state", by))
    (picked,) = call(send_body, [(2,) + grid], [VMEM, VMEM], moved=24 * unit)(before, held_zero)
    halo_zero = shifted(picked, "frame", -1)
    held_one, picked = call(
        load_send_body,
        [object_slices.shape[1:], (2,) + grid],
        [VMEM, HBM],
        [pltpu.SemaphoreType.DMA((4,))],
        moved=40 * unit,
    )(before, given[2])
    halo_one = shifted(picked, "frame", -1)
    kr, ki, amp, first, tab = pl.pallas_call(
        prepare_body,
        out_shape=[jax.ShapeDtypeStruct(grid, F32)] * 3
        + [jax.ShapeDtypeStruct(x.shape, x.dtype) for x in (probe, tab)],
        in_specs=[HBM] * 5,
        out_specs=[VMEM] * 5,
        scratch_shapes=[
            pltpu.SMEM(positions.shape, jnp.int32),
            pltpu.VMEM(probe.shape, F32),
            pltpu.VMEM(grid, F32),
            pltpu.VMEM(amplitude.shape, F32),
            pltpu.SemaphoreType.DMA((5,)),
        ],
        compiler_params=pltpu.CompilerParams(vmem_limit_bytes=LIMIT),
        cost_estimate=pl.CostEstimate(flops=2 * size**3, bytes_accessed=60 * unit, transcendentals=0),
    )(*given[:2], *(in_hbm(x) for x in (propagator, amplitude, tab)))
    frames = lax.axis_size("frame")
    own = call(turn_body, [grid] * len(planes), [VMEM] * (1 + len(planes)), moved=16 * unit)(pos, *planes)
    pairs = []
    for came, kept in zip(planes, own):
        pairs += [kept, lax.ppermute(came, "frame", [(i, i ^ 1) for i in range(frames)])]
    waves, probes = call(
        inner_body,
        [(states, 2) + grid] * 2,
        [VMEM] * (7 + len(pairs)),
        [pltpu.VMEM((2,) + grid, F32)],
        flops=2 * flops * states,
        moved=24 * unit * states,
    )(pos, held_zero, halo_zero, first, kr, ki, tab, *pairs)
    term_one, half, patch = call(
        functools.partial(middle_body, rows),
        [(2, rows, size), (states, 2) + grid, (2,) + grid],
        [VMEM] * 6,
        [pltpu.VMEM((states, 2) + grid, F32), pltpu.VMEM(grid, F32)],
        flops=2 * flops * states,
        moved=32 * unit * states,
    )(pos, held_one, halo_one, waves, amp, tab)
    came_one = shifted(term_one, "frame", 1)
    (term_zero,) = call(
        functools.partial(last_body, rows),
        [(2, rows, size)],
        [VMEM] * 6,
        [pltpu.VMEM((states, 2) + grid, F32)],
        flops=2 * flops * states,
        moved=16 * unit * states,
    )(half, patch, probes, kr, ki, tab)
    came_zero = shifted(term_zero, "frame", 1)
    gradient = gather(1, rows, size, pos, before, term_one, came_one)
    return gather(0, rows, size, pos, before, term_zero, came_zero, gradient)


def solution(mesh):
    return jax.shard_map(
        on_device,
        mesh=mesh,
        in_specs=(
            P(None, None, "frame", None),
            P("state", None, None, None),
            P("frame", None, None),
            P("frame", None),
            P(),
        ),
        out_specs=P(None, None, ("frame", "state"), None),
        check_vma=False,
    )
```

```python
import functools
import math

import jax
import jax.numpy as jnp
import numpy as np
from jax import lax
from jax.experimental import pallas as pl
from jax.experimental.pallas import tpu as pltpu
from jax.sharding import PartitionSpec as P


F32 = jnp.float32
BF16 = jnp.bfloat16
VMEM = pl.BlockSpec(memory_space=pltpu.VMEM)
HBM = pl.BlockSpec(memory_space=pltpu.MemorySpace.HBM)
SMEM = pl.BlockSpec(memory_space=pltpu.SMEM)
LIMIT = 24 * 1024 * 1024


def shifted(value, axis, by):
    count = lax.axis_size(axis)
    return lax.ppermute(value, axis, [(i, (i + by) % count) for i in range(count)])


def in_hbm(value):
    return pltpu.with_memory_space_constraint(value, pltpu.MemorySpace.HBM)


def call(body, outs, ins, scratch=(), flops=0, moved=0):
    return pl.pallas_call(
        body,
        out_shape=[jax.ShapeDtypeStruct(shape, F32) for shape in outs],
        in_specs=ins,
        out_specs=[VMEM] * len(outs),
        scratch_shapes=list(scratch),
        compiler_params=pltpu.CompilerParams(vmem_limit_bytes=LIMIT),
        cost_estimate=pl.CostEstimate(flops=flops, bytes_accessed=moved, transcendentals=0),
    )


def tables(length):
    half = length // 2
    n = np.arange(half)[:, None]
    forms = []
    for parity in (0, 1):
        k = 2 * np.arange(half)[None, :] + parity
        angle = -2.0 * math.pi * ((n * k) % length) / length
        re, im = np.cos(angle) / math.sqrt(length), np.sin(angle) / math.sqrt(length)
        right = np.block([[re, im], [-im, re]])
        forms += [right, right.T]
    stack = np.stack(forms).astype(np.float64)
    top = stack.astype(BF16)
    rest = (stack - top.astype(np.float64)).astype(BF16)
    return jnp.asarray(np.stack([top, rest]))


def halves(value):
    top = value.astype(BF16)
    return top, (value - top.astype(F32)).astype(BF16)


def dot(a, b):
    return lax.dot_general(a, b, (((1,), (0,)), ((), ())), preferred_element_type=F32)


def times_table(value, tab, which):
    top, rest = halves(value)
    return dot(top, tab[0, which]) + (dot(rest, tab[0, which]) + dot(top, tab[1, which]))


def table_times(value, tab, which):
    top, rest = halves(value)
    return dot(tab[0, which], top) + (dot(tab[0, which], rest) + dot(tab[1, which], top))


def columns_forward(re, im, tab):
    h = re.shape[1] // 2
    r0, r1, i0, i1 = re[:, :h], re[:, h:], im[:, :h], im[:, h:]
    even = times_table(jnp.concatenate([r0 + r1, i0 + i1], 1), tab, 0)
    odd = times_table(jnp.concatenate([r0 - r1, i0 - i1], 1), tab, 2)
    return (
        jnp.concatenate([even[:, :h], odd[:, :h]], 1),
        jnp.concatenate([even[:, h:], odd[:, h:]], 1),
    )


def columns_inverse(re, im, tab):
    h = re.shape[1] // 2
    even = times_table(jnp.concatenate([re[:, :h], im[:, :h]], 1), tab, 1)
    odd = times_table(jnp.concatenate([re[:, h:], im[:, h:]], 1), tab, 3)
    total, gap = even + odd, even - odd
    return (
        jnp.concatenate([total[:, :h], gap[:, :h]], 1),
        jnp.concatenate([total[:, h:], gap[:, h:]], 1),
    )


def rows_forward(re, im, tab):
    h = re.shape[0] // 2
    r0, r1, i0, i1 = re[:h], re[h:], im[:h], im[h:]
    even = table_times(jnp.concatenate([r0 + r1, i0 + i1], 0), tab, 1)
    odd = table_times(jnp.concatenate([r0 - r1, i0 - i1], 0), tab, 3)
    return (
        jnp.concatenate([even[:h], odd[:h]], 0),
        jnp.concatenate([even[h:], odd[h:]], 0),
    )


def rows_inverse(re, im, tab):
    h = re.shape[0] // 2
    even = table_times(jnp.concatenate([re[:h], im[:h]], 0), tab, 0)
    odd = table_times(jnp.concatenate([re[h:], im[h:]], 0), tab, 2)
    total, gap = even + odd, even - odd
    return (
        jnp.concatenate([total[:h], gap[:h]], 0),
        jnp.concatenate([total[h:], gap[h:]], 0),
    )


def forward(waves, tab):
    waves = [columns_forward(*wave, tab) for wave in waves]
    return [rows_forward(*wave, tab) for wave in waves]


def inverse(waves, tab):
    waves = [rows_inverse(*wave, tab) for wave in waves]
    return [columns_inverse(*wave, tab) for wave in waves]


def times(a, b):
    return a[0] * b[0] - a[1] * b[1], a[0] * b[1] + a[1] * b[0]


def times_conj(a, b):
    return a[0] * b[0] + a[1] * b[1], a[0] * b[1] - a[1] * b[0]


def in_groups(states, body):
    group = 2 if states % 2 == 0 else 1
    if states == group:
        body([m for m in range(group)])
        return

    def step(g, carry):
        body([g * group + m for m in range(group)])
        return carry

    lax.fori_loop(0, states // group, step, 0)


def thirds(value):
    top = value.astype(BF16)
    left = value - top.astype(F32)
    mid = left.astype(BF16)
    return top, mid, (left - mid.astype(F32)).astype(BF16)


def by_parity(value):
    size = value.shape[0]
    h = size // 2
    picks = []
    for along in (0, 1):
        place = lax.broadcasted_iota(jnp.int32, (size, size), along)
        source = lax.broadcasted_iota(jnp.int32, (size, size), 1 - along)
        wanted = jnp.where(place < h, 2 * place, 2 * (place - h) + 1)
        picks.append(jnp.where(source == wanted, 1.0, 0.0).astype(BF16))
    top, mid, low = thirds(value)
    value = (dot(picks[0], top) + dot(picks[0], mid)) + dot(picks[0], low)
    top, mid, low = thirds(value)
    return (dot(top, picks[1]) + dot(mid, picks[1])) + dot(low, picks[1])


def turned(value, row, col):
    return pltpu.roll(pltpu.roll(value, row, 0), col, 1)


def run_copies(moves, sem):
    copies = [pltpu.make_async_copy(src, dst, sem.at[i]) for i, (src, dst) in enumerate(moves)]
    for copy in copies:
        copy.start()
    return copies


def quarters(object_hbm, s, out):
    half = object_hbm.shape[2] // 2
    return [
        (object_hbm.at[s, part, at], out.at[part, at])
        for part in range(2)
        for at in (pl.ds(0, half), pl.ds(half, half))
    ]


def load_body(pos_hbm, probe_hbm, object_hbm, pos_out, plane_out, object_out, sem):
    which = lax.rem(lax.axis_index("frame"), 2)
    moves = [(probe_hbm.at[0, which], plane_out), (pos_hbm, pos_out)] + quarters(object_hbm, 0, object_out)
    for copy in run_copies(moves, sem):
        copy.wait()


def turn_of(pos_ref, size):
    return jnp.sum(pos_ref[0:1, 0:1]), lax.rem(jnp.sum(pos_ref[0:1, 1:2]), size)


def turn_body(pos_ref, *refs):
    half = len(refs) // 2
    turn = turn_of(pos_ref, refs[0].shape[1])
    for came, out in zip(refs[:half], refs[half:]):
        out[...] = turned(came[...], *turn)


def prepare_body(
    pos_hbm, probe_hbm, prop_hbm, amp_hbm, tab_hbm,
    wave_re, wave_im, amp_out, first_out, tab_out,
    pos, probe, prop, amp, sem,
):
    copies = run_copies(
        ((pos_hbm, pos), (probe_hbm, probe), (prop_hbm, prop), (amp_hbm, amp), (tab_hbm, tab_out)), sem
    )
    copies[0].wait()
    copies[1].wait()
    size = prop.shape[0]
    row, col = pos[0, 0], lax.rem(pos[0, 1], size)
    for c in range(2):
        first_out[0, c] = turned(probe[0, c], row, col)
    copies[2].wait()
    phase = by_parity(prop[...])
    wave_re[...] = jnp.cos(phase)
    wave_im[...] = jnp.sin(phase)
    copies[3].wait()
    amp_out[...] = by_parity(amp[0])
    copies[4].wait()


def spread(ref, which, shape):
    return jnp.broadcast_to(ref[0:1, which : which + 1], shape)


def wrapped(ref, part, col_ref):
    size = ref.shape[-2]
    c = lax.broadcasted_iota(jnp.int32, (size, size), 1)
    return jnp.where(c < spread(col_ref, 1, c.shape), ref[part, :, size:], ref[part, :, :size])


def send_body(before_ref, object_ref, out_ref):
    for part in range(2):
        out_ref[part] = wrapped(object_ref, part, before_ref)


def load_send_body(before_ref, object_hbm, object_out, out_ref, sem):
    copies = run_copies(quarters(object_hbm, 1, object_out), sem)
    for copy in copies:
        copy.wait()
    send_body(before_ref, object_out, out_ref)


def patch_of(object_ref, halo_ref, pos_ref):
    size = halo_ref.shape[-1]
    r = lax.broadcasted_iota(jnp.int32, (size, size), 0)
    return [
        jnp.where(r < spread(pos_ref, 0, r.shape), halo_ref[part], wrapped(object_ref, part, pos_ref))
        for part in range(2)
    ]


def pair(ref, *at):
    return ref[(*at, 0)], ref[(*at, 1)]


def propagate(probes, patch, kr_ref, ki_ref, tab):
    waves = forward([times(probe, pair(patch)) for probe in probes], tab)
    return inverse([times((kr_ref[...], ki_ref[...]), wave) for wave in waves], tab)


def own_body(pos_ref, object_ref, halo_ref, first_ref, kr_ref, ki_ref, tab, out_ref, patch):
    patch[0], patch[1] = patch_of(object_ref, halo_ref, pos_ref)
    (out_ref[0, 0], out_ref[0, 1]), = propagate([pair(first_ref, 0)], patch, kr_ref, ki_ref, tab)


def inner_body(pos_ref, patch, mine_ref, first_ref, kr_ref, ki_ref, tab, *refs):
    out_ref, probe_ref = refs[-2:]
    swap = lax.rem(lax.axis_index("frame"), 2) == 1
    for m, (came, given) in enumerate(zip(refs[:-2:2], refs[1:-2:2])):
        other = turned(given[...], *turn_of(pos_ref, given.shape[1]))
        probe_ref[1 + m, 0] = jnp.where(swap, other, came[...])
        probe_ref[1 + m, 1] = jnp.where(swap, came[...], other)
    probe_ref[:1] = first_ref[...]
    out_ref[:1] = mine_ref[...]

    def body(group):
        waves = propagate([pair(probe_ref, 1 + m) for m in group], patch, kr_ref, ki_ref, tab)
        for m, wave in zip(group, waves):
            out_ref[1 + m, 0], out_ref[1 + m, 1] = wave

    in_groups(out_ref.shape[0] - 1, body)


def middle_body(rows, pos_ref, object_ref, halo_ref, inner_ref, amp_ref, tab, term_ref, half_ref, patch, far, power):
    states = inner_ref.shape[0]
    patch[0], patch[1] = patch_of(object_ref, halo_ref, pos_ref)
    power[...] = jnp.zeros_like(power)

    def outward(group):
        waves = forward([times(pair(patch), pair(inner_ref, m)) for m in group], tab)
        total = power[...]
        for m, wave in zip(group, waves):
            far[m, 0], far[m, 1] = wave
            total += wave[0] * wave[0] + wave[1] * wave[1]
        power[...] = total

    in_groups(states, outward)
    power[...] = 1.0 - amp_ref[...] * lax.rsqrt(power[...] + 1.0)
    term_ref[...] = jnp.zeros_like(term_ref)
    take = pl.ds(pl.multiple_of(lax.axis_index("state") * rows, rows), rows)

    def homeward(group):
        waves = [rows_inverse(power[...] * far[m, 0], power[...] * far[m, 1], tab) for m in group]
        for m, wave in zip(group, waves):
            half_ref[m, 0], half_ref[m, 1] = wave
        for m in group:
            wave = columns_inverse(half_ref[m, 0, take], half_ref[m, 1, take], tab)
            part = times_conj((inner_ref[m, 0, take], inner_ref[m, 1, take]), wave)
            term_ref[0] += part[0]
            term_ref[1] += part[1]

    in_groups(states, homeward)


def last_body(rows, half_ref, patch, probe_ref, kr_ref, ki_ref, tab, term_ref, front):
    states = half_ref.shape[0]
    take = pl.ds(pl.multiple_of(lax.axis_index("state") * rows, rows), rows)
    term_ref[...] = jnp.zeros_like(term_ref)

    def body(group):
        waves = [columns_inverse(*pair(half_ref, m), tab) for m in group]
        waves = forward([times_conj(pair(patch), wave) for wave in waves], tab)
        waves = [rows_inverse(*times_conj((kr_ref[...], ki_ref[...]), wave), tab) for wave in waves]
        for m, wave in zip(group, waves):
            front[m, 0], front[m, 1] = wave
        for m in group:
            wave = columns_inverse(front[m, 0, take], front[m, 1, take], tab)
            part = times_conj((probe_ref[m, 0, take], probe_ref[m, 1, take]), wave)
            term_ref[0] += part[0]
            term_ref[1] += part[1]

    in_groups(states, body)


def gather_body(slice_id, rows, pos_ref, before_ref, own_ref, came_ref, *refs):
    out_ref, held, sem = refs[-3:]
    size = own_ref.shape[-1]
    start = lax.axis_index("state") * rows
    r = lax.broadcasted_iota(jnp.int32, (rows, size), 0) + start
    c = lax.broadcasted_iota(jnp.int32, (rows, size), 1)
    here, there = r >= spread(pos_ref, 0, r.shape), r < spread(before_ref, 0, r.shape)
    here_right, there_right = c < spread(pos_ref, 1, c.shape), c < spread(before_ref, 1, c.shape)
    chunks = 4 if rows % 32 == 0 else 1
    step = rows // chunks
    copies = []
    for chunk in range(chunks):
        at = pl.ds(chunk * step, step)
        cut = slice(chunk * step, chunk * step + step)
        for part in range(2):
            mine = jnp.where(here[cut], own_ref[part, at], 0.0)
            theirs = jnp.where(there[cut], came_ref[part, at], 0.0)
            left, right = here_right[cut], there_right[cut]
            held[part, at, :size] = jnp.where(left, 0.0, mine) + jnp.where(right, 0.0, theirs)
            held[part, at, size:] = jnp.where(left, mine, 0.0) + jnp.where(right, theirs, 0.0)
            copies.append(
                pltpu.make_async_copy(held.at[part, at], out_ref.at[slice_id, part, at], sem.at[len(copies)])
            )
            copies[-1].start()
    for copy in copies:
        copy.wait()


def gather(slice_id, rows, size, pos, before, own, came, *given):
    return pl.pallas_call(
        functools.partial(gather_body, slice_id, rows),
        out_shape=jax.ShapeDtypeStruct((2, 2, rows, 2 * size), F32),
        in_specs=[VMEM] * 4 + [pl.BlockSpec(memory_space=pl.ANY)] * len(given),
        out_specs=pl.BlockSpec(memory_space=pl.ANY),
        scratch_shapes=[pltpu.VMEM((2, rows, 2 * size), F32), pltpu.SemaphoreType.DMA((8,))],
        input_output_aliases={4: 0} if given else {},
        compiler_params=pltpu.CompilerParams(vmem_limit_bytes=LIMIT),
        cost_estimate=pl.CostEstimate(flops=0, bytes_accessed=32 * rows * size, transcendentals=0),
    )(pos, before, own, came, *given)


def on_device(object_slices, probe, amplitude, positions, propagator):
    states = lax.axis_size("state")
    size = amplitude.shape[1]
    rows = object_slices.shape[2] // states
    assert object_slices.shape[2:] == (size, 2 * size) and positions.shape[0] == 1
    assert lax.axis_size("frame") % 2 == 0
    return gradient_of(object_slices, probe, amplitude, positions, propagator, states, size, rows)


def gradient_of(object_slices, probe, amplitude, positions, propagator, states, size, rows):
    grid = (size, size)
    unit = size * size
    flops = 24 * size**3
    tab = tables(size)
    before = shifted(positions, "frame", 1)
    given = [in_hbm(x) for x in (positions, probe, object_slices)]
    pos, plane, held_zero = pl.pallas_call(
        load_body,
        out_shape=[
            jax.ShapeDtypeStruct(positions.shape, jnp.int32),
            jax.ShapeDtypeStruct(grid, F32),
            jax.ShapeDtypeStruct(object_slices.shape[1:], F32),
        ],
        in_specs=[HBM] * 3,
        out_specs=[VMEM] * 3,
        scratch_shapes=[pltpu.SemaphoreType.DMA((6,))],
        compiler_params=pltpu.CompilerParams(vmem_limit_bytes=LIMIT),
        cost_estimate=pl.CostEstimate(flops=0, bytes_accessed=24 * unit, transcendentals=0),
    )(*given)
    planes = []
    for by in range(1, states):
        planes.append(shifted(plane, "state", by))
    (picked,) = call(send_body, [(2,) + grid], [VMEM, VMEM], moved=24 * unit)(before, held_zero)
    halo_zero = shifted(picked, "frame", -1)
    held_one, picked = call(
        load_send_body,
        [object_slices.shape[1:], (2,) + grid],
        [VMEM, HBM],
        [pltpu.SemaphoreType.DMA((4,))],
        moved=40 * unit,
    )(before, given[2])
    halo_one = shifted(picked, "frame", -1)
    kr, ki, amp, first, tab = pl.pallas_call(
        prepare_body,
        out_shape=[jax.ShapeDtypeStruct(grid, F32)] * 3
        + [jax.ShapeDtypeStruct(x.shape, x.dtype) for x in (probe, tab)],
        in_specs=[HBM] * 5,
        out_specs=[VMEM] * 5,
        scratch_shapes=[
            pltpu.SMEM(positions.shape, jnp.int32),
            pltpu.VMEM(probe.shape, F32),
            pltpu.VMEM(grid, F32),
            pltpu.VMEM(amplitude.shape, F32),
            pltpu.SemaphoreType.DMA((5,)),
        ],
        compiler_params=pltpu.CompilerParams(vmem_limit_bytes=LIMIT),
        cost_estimate=pl.CostEstimate(flops=2 * size**3, bytes_accessed=60 * unit, transcendentals=0),
    )(*given[:2], *(in_hbm(x) for x in (propagator, amplitude, tab)))
    frames = lax.axis_size("frame")
    own = call(turn_body, [grid] * len(planes), [VMEM] * (1 + len(planes)), moved=16 * unit)(pos, *planes)
    pairs = []
    for came, kept in zip(planes, own):
        pairs += [kept, lax.ppermute(came, "frame", [(i, i ^ 1) for i in range(frames)])]
    mine, first_patch = call(
        own_body,
        [(1, 2) + grid, (2,) + grid],
        [VMEM] * 7,
        flops=2 * flops,
        moved=24 * unit,
    )(pos, held_zero, halo_zero, first, kr, ki, tab)
    waves, probes = call(
        inner_body,
        [(states, 2) + grid] * 2,
        [VMEM] * (7 + len(pairs)),
        flops=2 * flops * (states - 1),
        moved=24 * unit * states,
    )(pos, first_patch, mine, first, kr, ki, tab, *pairs)
    term_one, half, patch = call(
        functools.partial(middle_body, rows),
        [(2, rows, size), (states, 2) + grid, (2,) + grid],
        [VMEM] * 6,
        [pltpu.VMEM((states, 2) + grid, F32), pltpu.VMEM(grid, F32)],
        flops=2 * flops * states,
        moved=32 * unit * states,
    )(pos, held_one, halo_one, waves, amp, tab)
    came_one = shifted(term_one, "frame", 1)
    (term_zero,) = call(
        functools.partial(last_body, rows),
        [(2, rows, size)],
        [VMEM] * 6,
        [pltpu.VMEM((states, 2) + grid, F32)],
        flops=2 * flops * states,
        moved=16 * unit * states,
    )(half, patch, probes, kr, ki, tab)
    came_zero = shifted(term_zero, "frame", 1)
    gradient = gather(1, rows, size, pos, before, term_one, came_one)
    return gather(0, rows, size, pos, before, term_zero, came_zero, gradient)


def solution(mesh):
    return jax.shard_map(
        on_device,
        mesh=mesh,
        in_specs=(
            P(None, None, "frame", None),
            P("state", None, None, None),
            P("frame", None, None),
            P("frame", None),
            P(),
        ),
        out_specs=P(None, None, ("frame", "state"), None),
        check_vma=False,
    )
```

```python
import functools
import math

import jax
import jax.numpy as jnp
import numpy as np
from jax import lax
from jax.experimental import pallas as pl
from jax.experimental.pallas import tpu as pltpu
from jax.sharding import PartitionSpec as P


F32 = jnp.float32
BF16 = jnp.bfloat16
VMEM = pl.BlockSpec(memory_space=pltpu.VMEM)
HBM = pl.BlockSpec(memory_space=pltpu.MemorySpace.HBM)
SMEM = pl.BlockSpec(memory_space=pltpu.SMEM)
LIMIT = 24 * 1024 * 1024


def shifted(value, axis, by):
    count = lax.axis_size(axis)
    return lax.ppermute(value, axis, [(i, (i + by) % count) for i in range(count)])


def in_hbm(value):
    return pltpu.with_memory_space_constraint(value, pltpu.MemorySpace.HBM)


def call(body, outs, ins, scratch=(), flops=0, moved=0):
    return pl.pallas_call(
        body,
        out_shape=[jax.ShapeDtypeStruct(shape, F32) for shape in outs],
        in_specs=ins,
        out_specs=[VMEM] * len(outs),
        scratch_shapes=list(scratch),
        compiler_params=pltpu.CompilerParams(vmem_limit_bytes=LIMIT),
        cost_estimate=pl.CostEstimate(flops=flops, bytes_accessed=moved, transcendentals=0),
    )


def tables(length):
    half = length // 2
    n = np.arange(half)[:, None]
    forms = []
    for parity in (0, 1):
        k = 2 * np.arange(half)[None, :] + parity
        angle = -2.0 * math.pi * ((n * k) % length) / length
        re, im = np.cos(angle) / math.sqrt(length), np.sin(angle) / math.sqrt(length)
        right = np.block([[re, im], [-im, re]])
        forms += [right, right.T]
    stack = np.stack(forms).astype(np.float64)
    top = stack.astype(BF16)
    rest = (stack - top.astype(np.float64)).astype(BF16)
    return jnp.asarray(np.stack([top, rest]))


def halves(value):
    top = value.astype(BF16)
    return top, (value - top.astype(F32)).astype(BF16)


def dot(a, b):
    return lax.dot_general(a, b, (((1,), (0,)), ((), ())), preferred_element_type=F32)


def times_table(value, tab, which):
    top, rest = halves(value)
    return dot(top, tab[0, which]) + (dot(rest, tab[0, which]) + dot(top, tab[1, which]))


def table_times(value, tab, which):
    top, rest = halves(value)
    return dot(tab[0, which], top) + (dot(tab[0, which], rest) + dot(tab[1, which], top))


def columns_forward(re, im, tab):
    h = re.shape[1] // 2
    r0, r1, i0, i1 = re[:, :h], re[:, h:], im[:, :h], im[:, h:]
    even = times_table(jnp.concatenate([r0 + r1, i0 + i1], 1), tab, 0)
    odd = times_table(jnp.concatenate([r0 - r1, i0 - i1], 1), tab, 2)
    return (
        jnp.concatenate([even[:, :h], odd[:, :h]], 1),
        jnp.concatenate([even[:, h:], odd[:, h:]], 1),
    )


def columns_inverse(re, im, tab):
    h = re.shape[1] // 2
    even = times_table(jnp.concatenate([re[:, :h], im[:, :h]], 1), tab, 1)
    odd = times_table(jnp.concatenate([re[:, h:], im[:, h:]], 1), tab, 3)
    total, gap = even + odd, even - odd
    return (
        jnp.concatenate([total[:, :h], gap[:, :h]], 1),
        jnp.concatenate([total[:, h:], gap[:, h:]], 1),
    )


def rows_forward(re, im, tab):
    h = re.shape[0] // 2
    r0, r1, i0, i1 = re[:h], re[h:], im[:h], im[h:]
    even = table_times(jnp.concatenate([r0 + r1, i0 + i1], 0), tab, 1)
    odd = table_times(jnp.concatenate([r0 - r1, i0 - i1], 0), tab, 3)
    return (
        jnp.concatenate([even[:h], odd[:h]], 0),
        jnp.concatenate([even[h:], odd[h:]], 0),
    )


def rows_inverse(re, im, tab):
    h = re.shape[0] // 2
    even = table_times(jnp.concatenate([re[:h], im[:h]], 0), tab, 0)
    odd = table_times(jnp.concatenate([re[h:], im[h:]], 0), tab, 2)
    total, gap = even + odd, even - odd
    return (
        jnp.concatenate([total[:h], gap[:h]], 0),
        jnp.concatenate([total[h:], gap[h:]], 0),
    )


def forward(waves, tab):
    waves = [columns_forward(*wave, tab) for wave in waves]
    return [rows_forward(*wave, tab) for wave in waves]


def inverse(waves, tab):
    waves = [rows_inverse(*wave, tab) for wave in waves]
    return [columns_inverse(*wave, tab) for wave in waves]


def times(a, b):
    return a[0] * b[0] - a[1] * b[1], a[0] * b[1] + a[1] * b[0]


def times_conj(a, b):
    return a[0] * b[0] + a[1] * b[1], a[0] * b[1] - a[1] * b[0]


def in_groups(states, body):
    group = 2 if states % 2 == 0 else 1
    if states == group:
        body([m for m in range(group)])
        return

    def step(g, carry):
        body([g * group + m for m in range(group)])
        return carry

    lax.fori_loop(0, states // group, step, 0)


def thirds(value):
    top = value.astype(BF16)
    left = value - top.astype(F32)
    mid = left.astype(BF16)
    return top, mid, (left - mid.astype(F32)).astype(BF16)


def by_parity(value):
    size = value.shape[0]
    h = size // 2
    picks = []
    for along in (0, 1):
        place = lax.broadcasted_iota(jnp.int32, (size, size), along)
        source = lax.broadcasted_iota(jnp.int32, (size, size), 1 - along)
        wanted = jnp.where(place < h, 2 * place, 2 * (place - h) + 1)
        picks.append(jnp.where(source == wanted, 1.0, 0.0).astype(BF16))
    top, mid, low = thirds(value)
    value = (dot(picks[0], top) + dot(picks[0], mid)) + dot(picks[0], low)
    top, mid, low = thirds(value)
    return (dot(top, picks[1]) + dot(mid, picks[1])) + dot(low, picks[1])


def turned(value, row, col):
    return pltpu.roll(pltpu.roll(value, row, 0), col, 1)


def run_copies(moves, sem):
    copies = [pltpu.make_async_copy(src, dst, sem.at[i]) for i, (src, dst) in enumerate(moves)]
    for copy in copies:
        copy.start()
    return copies


def quarters(object_hbm, s, out):
    half = object_hbm.shape[2] // 2
    return [
        (object_hbm.at[s, part, at], out.at[part, at])
        for part in range(2)
        for at in (pl.ds(0, half), pl.ds(half, half))
    ]


def load_body(pos_hbm, probe_hbm, object_hbm, pos_out, plane_out, object_out, sem):
    which = lax.rem(lax.axis_index("frame"), 2)
    moves = [(probe_hbm.at[0, which], plane_out), (pos_hbm, pos_out)] + quarters(object_hbm, 0, object_out)
    for copy in run_copies(moves, sem):
        copy.wait()


def turn_of(pos_ref, size):
    return jnp.sum(pos_ref[0:1, 0:1]), lax.rem(jnp.sum(pos_ref[0:1, 1:2]), size)


def turn_body(before_ref, *refs):
    half = len(refs) // 2
    turn = turn_of(before_ref, refs[0].shape[1])
    for came, out in zip(refs[:half], refs[half:]):
        out[...] = turned(came[...], *turn)


def prepare_body(
    before_ref, lent_ref, probe_hbm, prop_hbm, tab_hbm,
    wave_re, wave_im, amp_out, first_out, tab_out,
    probe, prop, sem,
):
    copies = run_copies(((probe_hbm, probe), (prop_hbm, prop), (tab_hbm, tab_out)), sem)
    size = prop.shape[0]
    amp_out[...] = by_parity(lent_ref[0])
    copies[0].wait()
    turn = turn_of(before_ref, size)
    for c in range(2):
        first_out[0, c] = turned(probe[0, c], *turn)
    copies[1].wait()
    phase = by_parity(prop[...])
    wave_re[...] = jnp.cos(phase)
    wave_im[...] = jnp.sin(phase)
    copies[2].wait()


def spread(ref, which, shape):
    return jnp.broadcast_to(ref[0:1, which : which + 1], shape)


def wrapped(ref, part, col_ref):
    size = ref.shape[-2]
    c = lax.broadcasted_iota(jnp.int32, (size, size), 1)
    return jnp.where(c < spread(col_ref, 1, c.shape), ref[part, :, size:], ref[part, :, :size])


def send_body(pos_ref, object_ref, out_ref):
    for part in range(2):
        out_ref[part] = wrapped(object_ref, part, pos_ref)


def load_send_body(pos_ref, object_hbm, object_out, out_ref, sem):
    copies = run_copies(quarters(object_hbm, 1, object_out), sem)
    for copy in copies:
        copy.wait()
    send_body(pos_ref, object_out, out_ref)


def patch_of(object_ref, halo_ref, before_ref):
    size = halo_ref.shape[-1]
    r = lax.broadcasted_iota(jnp.int32, (size, size), 0)
    return [
        jnp.where(r < spread(before_ref, 0, r.shape), wrapped(object_ref, part, before_ref), halo_ref[part])
        for part in range(2)
    ]


def pair(ref, *at):
    return ref[(*at, 0)], ref[(*at, 1)]


def propagate(probes, patch, kr_ref, ki_ref, tab):
    waves = forward([times(probe, pair(patch)) for probe in probes], tab)
    return inverse([times((kr_ref[...], ki_ref[...]), wave) for wave in waves], tab)


def own_body(before_ref, object_ref, halo_ref, first_ref, kr_ref, ki_ref, tab, out_ref, patch):
    patch[0], patch[1] = patch_of(object_ref, halo_ref, before_ref)
    (out_ref[0, 0], out_ref[0, 1]), = propagate([pair(first_ref, 0)], patch, kr_ref, ki_ref, tab)


def inner_body(before_ref, patch, mine_ref, first_ref, kr_ref, ki_ref, tab, *refs):
    out_ref, probe_ref = refs[-2:]
    swap = lax.rem(lax.axis_index("frame"), 2) == 1
    for m, (came, given) in enumerate(zip(refs[:-2:2], refs[1:-2:2])):
        other = turned(given[...], *turn_of(before_ref, given.shape[1]))
        probe_ref[1 + m, 0] = jnp.where(swap, other, came[...])
        probe_ref[1 + m, 1] = jnp.where(swap, came[...], other)
    probe_ref[:1] = first_ref[...]
    out_ref[:1] = mine_ref[...]

    def body(group):
        waves = propagate([pair(probe_ref, 1 + m) for m in group], patch, kr_ref, ki_ref, tab)
        for m, wave in zip(group, waves):
            out_ref[1 + m, 0], out_ref[1 + m, 1] = wave

    in_groups(out_ref.shape[0] - 1, body)


def middle_body(rows, before_ref, object_ref, halo_ref, inner_ref, amp_ref, tab, term_ref, half_ref, patch, far, power):
    states = inner_ref.shape[0]
    patch[0], patch[1] = patch_of(object_ref, halo_ref, before_ref)
    power[...] = jnp.zeros_like(power)

    def outward(group):
        waves = forward([times(pair(patch), pair(inner_ref, m)) for m in group], tab)
        total = power[...]
        for m, wave in zip(group, waves):
            far[m, 0], far[m, 1] = wave
            total += wave[0] * wave[0] + wave[1] * wave[1]
        power[...] = total

    in_groups(states, outward)
    power[...] = 1.0 - amp_ref[...] * lax.rsqrt(power[...] + 1.0)
    term_ref[...] = jnp.zeros_like(term_ref)
    take = pl.ds(pl.multiple_of(lax.axis_index("state") * rows, rows), rows)

    def homeward(group):
        waves = [rows_inverse(power[...] * far[m, 0], power[...] * far[m, 1], tab) for m in group]
        for m, wave in zip(group, waves):
            half_ref[m, 0], half_ref[m, 1] = wave
        for m in group:
            wave = columns_inverse(half_ref[m, 0, take], half_ref[m, 1, take], tab)
            part = times_conj((inner_ref[m, 0, take], inner_ref[m, 1, take]), wave)
            term_ref[0] += part[0]
            term_ref[1] += part[1]

    in_groups(states, homeward)


def last_body(rows, half_ref, patch, probe_ref, kr_ref, ki_ref, tab, term_ref, front):
    states = half_ref.shape[0]
    take = pl.ds(pl.multiple_of(lax.axis_index("state") * rows, rows), rows)
    term_ref[...] = jnp.zeros_like(term_ref)

    def body(group):
        waves = [columns_inverse(*pair(half_ref, m), tab) for m in group]
        waves = forward([times_conj(pair(patch), wave) for wave in waves], tab)
        waves = [rows_inverse(*times_conj((kr_ref[...], ki_ref[...]), wave), tab) for wave in waves]
        for m, wave in zip(group, waves):
            front[m, 0], front[m, 1] = wave
        for m in group:
            wave = columns_inverse(front[m, 0, take], front[m, 1, take], tab)
            part = times_conj((probe_ref[m, 0, take], probe_ref[m, 1, take]), wave)
            term_ref[0] += part[0]
            term_ref[1] += part[1]

    in_groups(states, body)


def gather_body(slice_id, rows, pos_ref, before_ref, own_ref, came_ref, *refs):
    out_ref, held, sem = refs[-3:]
    size = own_ref.shape[-1]
    start = lax.axis_index("state") * rows
    r = lax.broadcasted_iota(jnp.int32, (rows, size), 0) + start
    c = lax.broadcasted_iota(jnp.int32, (rows, size), 1)
    here, there = r < spread(before_ref, 0, r.shape), r >= spread(pos_ref, 0, r.shape)
    here_right, there_right = c < spread(before_ref, 1, c.shape), c < spread(pos_ref, 1, c.shape)
    chunks = 4 if rows % 32 == 0 else 1
    step = rows // chunks
    copies = []
    for chunk in range(chunks):
        at = pl.ds(chunk * step, step)
        cut = slice(chunk * step, chunk * step + step)
        for part in range(2):
            mine = jnp.where(here[cut], own_ref[part, at], 0.0)
            theirs = jnp.where(there[cut], came_ref[part, at], 0.0)
            left, right = here_right[cut], there_right[cut]
            held[part, at, :size] = jnp.where(left, 0.0, mine) + jnp.where(right, 0.0, theirs)
            held[part, at, size:] = jnp.where(left, mine, 0.0) + jnp.where(right, theirs, 0.0)
            copies.append(
                pltpu.make_async_copy(held.at[part, at], out_ref.at[slice_id, part, at], sem.at[len(copies)])
            )
            copies[-1].start()
    for copy in copies:
        copy.wait()


def gather(slice_id, rows, size, pos, before, own, came, *given):
    return pl.pallas_call(
        functools.partial(gather_body, slice_id, rows),
        out_shape=jax.ShapeDtypeStruct((2, 2, rows, 2 * size), F32),
        in_specs=[VMEM] * 4 + [pl.BlockSpec(memory_space=pl.ANY)] * len(given),
        out_specs=pl.BlockSpec(memory_space=pl.ANY),
        scratch_shapes=[pltpu.VMEM((2, rows, 2 * size), F32), pltpu.SemaphoreType.DMA((8,))],
        input_output_aliases={4: 0} if given else {},
        compiler_params=pltpu.CompilerParams(vmem_limit_bytes=LIMIT),
        cost_estimate=pl.CostEstimate(flops=0, bytes_accessed=32 * rows * size, transcendentals=0),
    )(pos, before, own, came, *given)


def on_device(object_slices, probe, amplitude, positions, propagator):
    states = lax.axis_size("state")
    size = amplitude.shape[1]
    rows = object_slices.shape[2] // states
    assert object_slices.shape[2:] == (size, 2 * size) and positions.shape[0] == 1
    assert lax.axis_size("frame") % 2 == 0
    return gradient_of(object_slices, probe, amplitude, positions, propagator, states, size, rows)


def gradient_of(object_slices, probe, amplitude, positions, propagator, states, size, rows):
    grid = (size, size)
    unit = size * size
    flops = 24 * size**3
    tab = tables(size)
    before = shifted(positions, "frame", 1)
    lent = shifted(amplitude, "frame", 1)
    given = [in_hbm(x) for x in (positions, probe, object_slices)]
    pos, plane, held_zero = pl.pallas_call(
        load_body,
        out_shape=[
            jax.ShapeDtypeStruct(positions.shape, jnp.int32),
            jax.ShapeDtypeStruct(grid, F32),
            jax.ShapeDtypeStruct(object_slices.shape[1:], F32),
        ],
        in_specs=[HBM] * 3,
        out_specs=[VMEM] * 3,
        scratch_shapes=[pltpu.SemaphoreType.DMA((6,))],
        compiler_params=pltpu.CompilerParams(vmem_limit_bytes=LIMIT),
        cost_estimate=pl.CostEstimate(flops=0, bytes_accessed=24 * unit, transcendentals=0),
    )(*given)
    planes = []
    for by in range(1, states):
        planes.append(shifted(plane, "state", by))
    (picked,) = call(send_body, [(2,) + grid], [VMEM, VMEM], moved=24 * unit)(pos, held_zero)
    halo_zero = shifted(picked, "frame", 1)
    held_one, picked = call(
        load_send_body,
        [object_slices.shape[1:], (2,) + grid],
        [VMEM, HBM],
        [pltpu.SemaphoreType.DMA((4,))],
        moved=40 * unit,
    )(pos, given[2])
    halo_one = shifted(picked, "frame", 1)
    kr, ki, amp, first, tab = pl.pallas_call(
        prepare_body,
        out_shape=[jax.ShapeDtypeStruct(grid, F32)] * 3
        + [jax.ShapeDtypeStruct(x.shape, x.dtype) for x in (probe, tab)],
        in_specs=[VMEM] * 2 + [HBM] * 3,
        out_specs=[VMEM] * 5,
        scratch_shapes=[pltpu.VMEM(probe.shape, F32), pltpu.VMEM(grid, F32), pltpu.SemaphoreType.DMA((3,))],
        compiler_params=pltpu.CompilerParams(vmem_limit_bytes=LIMIT),
        cost_estimate=pl.CostEstimate(flops=2 * size**3, bytes_accessed=60 * unit, transcendentals=0),
    )(before, lent, given[1], *(in_hbm(x) for x in (propagator, tab)))
    frames = lax.axis_size("frame")
    own = call(turn_body, [grid] * len(planes), [VMEM] * (1 + len(planes)), moved=16 * unit)(before, *planes)
    pairs = []
    for came, kept in zip(planes, own):
        pairs += [kept, lax.ppermute(came, "frame", [(i, i ^ 1) for i in range(frames)])]
    mine, first_patch = call(
        own_body,
        [(1, 2) + grid, (2,) + grid],
        [VMEM] * 7,
        flops=2 * flops,
        moved=24 * unit,
    )(before, held_zero, halo_zero, first, kr, ki, tab)
    waves, probes = call(
        inner_body,
        [(states, 2) + grid] * 2,
        [VMEM] * (7 + len(pairs)),
        flops=2 * flops * (states - 1),
        moved=24 * unit * states,
    )(before, first_patch, mine, first, kr, ki, tab, *pairs)
    term_one, half, patch = call(
        functools.partial(middle_body, rows),
        [(2, rows, size), (states, 2) + grid, (2,) + grid],
        [VMEM] * 6,
        [pltpu.VMEM((states, 2) + grid, F32), pltpu.VMEM(grid, F32)],
        flops=2 * flops * states,
        moved=32 * unit * states,
    )(before, held_one, halo_one, waves, amp, tab)
    came_one = shifted(term_one, "frame", -1)
    (term_zero,) = call(
        functools.partial(last_body, rows),
        [(2, rows, size)],
        [VMEM] * 6,
        [pltpu.VMEM((states, 2) + grid, F32)],
        flops=2 * flops * states,
        moved=16 * unit * states,
    )(half, patch, probes, kr, ki, tab)
    came_zero = shifted(term_zero, "frame", -1)
    gradient = gather(1, rows, size, pos, before, term_one, came_one)
    return gather(0, rows, size, pos, before, term_zero, came_zero, gradient)


def solution(mesh):
    return jax.shard_map(
        on_device,
        mesh=mesh,
        in_specs=(
            P(None, None, "frame", None),
            P("state", None, None, None),
            P("frame", None, None),
            P("frame", None),
            P(),
        ),
        out_specs=P(None, None, ("frame", "state"), None),
        check_vma=False,
    )
```

```python
import functools
import math

import jax
import jax.numpy as jnp
import numpy as np
from jax import lax
from jax.experimental import pallas as pl
from jax.experimental.pallas import tpu as pltpu
from jax.sharding import PartitionSpec as P


F32 = jnp.float32
BF16 = jnp.bfloat16
VMEM = pl.BlockSpec(memory_space=pltpu.VMEM)
HBM = pl.BlockSpec(memory_space=pltpu.MemorySpace.HBM)
SMEM = pl.BlockSpec(memory_space=pltpu.SMEM)
LIMIT = 24 * 1024 * 1024


def shifted(value, axis, by):
    count = lax.axis_size(axis)
    return lax.ppermute(value, axis, [(i, (i + by) % count) for i in range(count)])


def in_hbm(value):
    return pltpu.with_memory_space_constraint(value, pltpu.MemorySpace.HBM)


def call(body, outs, ins, scratch=(), flops=0, moved=0):
    return pl.pallas_call(
        body,
        out_shape=[jax.ShapeDtypeStruct(shape, F32) for shape in outs],
        in_specs=ins,
        out_specs=[VMEM] * len(outs),
        scratch_shapes=list(scratch),
        compiler_params=pltpu.CompilerParams(vmem_limit_bytes=LIMIT),
        cost_estimate=pl.CostEstimate(flops=flops, bytes_accessed=moved, transcendentals=0),
    )


def tables(length):
    half = length // 2
    n = np.arange(half)[:, None]
    forms = []
    for parity in (0, 1):
        k = 2 * np.arange(half)[None, :] + parity
        angle = -2.0 * math.pi * ((n * k) % length) / length
        re, im = np.cos(angle) / math.sqrt(length), np.sin(angle) / math.sqrt(length)
        right = np.block([[re, im], [-im, re]])
        forms += [right, right.T]
    stack = np.stack(forms).astype(np.float64)
    top = stack.astype(BF16)
    rest = (stack - top.astype(np.float64)).astype(BF16)
    return jnp.asarray(np.stack([top, rest]))


def halves(value):
    top = value.astype(BF16)
    return top, (value - top.astype(F32)).astype(BF16)


def dot(a, b):
    return lax.dot_general(a, b, (((1,), (0,)), ((), ())), preferred_element_type=F32)


def times_table(value, tab, which):
    top, rest = halves(value)
    return dot(top, tab[0, which]) + (dot(rest, tab[0, which]) + dot(top, tab[1, which]))


def table_times(value, tab, which):
    top, rest = halves(value)
    return dot(tab[0, which], top) + (dot(tab[0, which], rest) + dot(tab[1, which], top))


def columns_forward(re, im, tab):
    h = re.shape[1] // 2
    r0, r1, i0, i1 = re[:, :h], re[:, h:], im[:, :h], im[:, h:]
    even = times_table(jnp.concatenate([r0 + r1, i0 + i1], 1), tab, 0)
    odd = times_table(jnp.concatenate([r0 - r1, i0 - i1], 1), tab, 2)
    return (
        jnp.concatenate([even[:, :h], odd[:, :h]], 1),
        jnp.concatenate([even[:, h:], odd[:, h:]], 1),
    )


def columns_inverse(re, im, tab):
    h = re.shape[1] // 2
    even = times_table(jnp.concatenate([re[:, :h], im[:, :h]], 1), tab, 1)
    odd = times_table(jnp.concatenate([re[:, h:], im[:, h:]], 1), tab, 3)
    total, gap = even + odd, even - odd
    return (
        jnp.concatenate([total[:, :h], gap[:, :h]], 1),
        jnp.concatenate([total[:, h:], gap[:, h:]], 1),
    )


def rows_forward(re, im, tab):
    h = re.shape[0] // 2
    r0, r1, i0, i1 = re[:h], re[h:], im[:h], im[h:]
    even = table_times(jnp.concatenate([r0 + r1, i0 + i1], 0), tab, 1)
    odd = table_times(jnp.concatenate([r0 - r1, i0 - i1], 0), tab, 3)
    return (
        jnp.concatenate([even[:h], odd[:h]], 0),
        jnp.concatenate([even[h:], odd[h:]], 0),
    )


def rows_inverse(re, im, tab):
    h = re.shape[0] // 2
    even = table_times(jnp.concatenate([re[:h], im[:h]], 0), tab, 0)
    odd = table_times(jnp.concatenate([re[h:], im[h:]], 0), tab, 2)
    total, gap = even + odd, even - odd
    return (
        jnp.concatenate([total[:h], gap[:h]], 0),
        jnp.concatenate([total[h:], gap[h:]], 0),
    )


def forward(waves, tab):
    waves = [columns_forward(*wave, tab) for wave in waves]
    return [rows_forward(*wave, tab) for wave in waves]


def inverse(waves, tab):
    waves = [rows_inverse(*wave, tab) for wave in waves]
    return [columns_inverse(*wave, tab) for wave in waves]


def times(a, b):
    return a[0] * b[0] - a[1] * b[1], a[0] * b[1] + a[1] * b[0]


def times_conj(a, b):
    return a[0] * b[0] + a[1] * b[1], a[0] * b[1] - a[1] * b[0]


def in_groups(states, body):
    group = 2 if states % 2 == 0 else 1
    if states == group:
        body([m for m in range(group)])
        return

    def step(g, carry):
        body([g * group + m for m in range(group)])
        return carry

    lax.fori_loop(0, states // group, step, 0)


def thirds(value):
    top = value.astype(BF16)
    left = value - top.astype(F32)
    mid = left.astype(BF16)
    return top, mid, (left - mid.astype(F32)).astype(BF16)


def by_parity(value):
    size = value.shape[0]
    h = size // 2
    picks = []
    for along in (0, 1):
        place = lax.broadcasted_iota(jnp.int32, (size, size), along)
        source = lax.broadcasted_iota(jnp.int32, (size, size), 1 - along)
        wanted = jnp.where(place < h, 2 * place, 2 * (place - h) + 1)
        picks.append(jnp.where(source == wanted, 1.0, 0.0).astype(BF16))
    top, mid, low = thirds(value)
    value = (dot(picks[0], top) + dot(picks[0], mid)) + dot(picks[0], low)
    top, mid, low = thirds(value)
    return (dot(top, picks[1]) + dot(mid, picks[1])) + dot(low, picks[1])


def turned(value, row, col):
    return pltpu.roll(pltpu.roll(value, row, 0), col, 1)


def run_copies(moves, sem):
    copies = [pltpu.make_async_copy(src, dst, sem.at[i]) for i, (src, dst) in enumerate(moves)]
    for copy in copies:
        copy.start()
    return copies


def quarters(object_hbm, s, out):
    half = object_hbm.shape[2] // 2
    return [
        (object_hbm.at[s, part, at], out.at[part, at])
        for part in range(2)
        for at in (pl.ds(0, half), pl.ds(half, half))
    ]


def load_body(pos_hbm, probe_hbm, object_hbm, pos_out, plane_out, object_out, sem):
    which = lax.rem(lax.axis_index("frame"), 2)
    moves = [(probe_hbm.at[0, which], plane_out), (pos_hbm, pos_out)] + quarters(object_hbm, 0, object_out)
    for copy in run_copies(moves, sem):
        copy.wait()


def turn_of(pos_ref, size):
    return jnp.sum(pos_ref[0:1, 0:1]), lax.rem(jnp.sum(pos_ref[0:1, 1:2]), size)


def turn_body(before_ref, *refs):
    half = len(refs) // 2
    turn = turn_of(before_ref, refs[0].shape[1])
    for came, out in zip(refs[:half], refs[half:]):
        out[...] = turned(came[...], *turn)


def prepare_body(
    before_ref, lent_ref, probe_hbm, prop_hbm, tab_hbm,
    wave_re, wave_im, amp_out, first_out, tab_out,
    probe, prop, sem,
):
    copies = run_copies(((probe_hbm, probe), (prop_hbm, prop), (tab_hbm, tab_out)), sem)
    size = prop.shape[0]
    amp_out[...] = by_parity(lent_ref[0])
    copies[0].wait()
    turn = turn_of(before_ref, size)
    for c in range(2):
        first_out[0, c] = turned(probe[0, c], *turn)
    copies[1].wait()
    phase = by_parity(prop[...])
    wave_re[...] = jnp.cos(phase)
    wave_im[...] = jnp.sin(phase)
    copies[2].wait()


def spread(ref, which, shape):
    return jnp.broadcast_to(ref[0:1, which : which + 1], shape)


def wrapped(ref, part, col_ref):
    size = ref.shape[-2]
    c = lax.broadcasted_iota(jnp.int32, (size, size), 1)
    return jnp.where(c < spread(col_ref, 1, c.shape), ref[part, :, size:], ref[part, :, :size])


def send_body(pos_ref, object_ref, out_ref):
    for part in range(2):
        out_ref[part] = wrapped(object_ref, part, pos_ref)


def load_send_body(pos_ref, object_hbm, object_out, out_ref, sem):
    copies = run_copies(quarters(object_hbm, 1, object_out), sem)
    for copy in copies:
        copy.wait()
    send_body(pos_ref, object_out, out_ref)


def patch_of(object_ref, halo_ref, before_ref):
    size = halo_ref.shape[-1]
    r = lax.broadcasted_iota(jnp.int32, (size, size), 0)
    return [
        jnp.where(r < spread(before_ref, 0, r.shape), wrapped(object_ref, part, before_ref), halo_ref[part])
        for part in range(2)
    ]


def pair(ref, *at):
    return ref[(*at, 0)], ref[(*at, 1)]


def propagate(probes, patch, kr_ref, ki_ref, tab):
    waves = forward([times(probe, pair(patch)) for probe in probes], tab)
    return inverse([times((kr_ref[...], ki_ref[...]), wave) for wave in waves], tab)


def own_body(before_ref, object_ref, halo_ref, first_ref, kr_ref, ki_ref, tab, out_ref, patch):
    patch[0], patch[1] = patch_of(object_ref, halo_ref, before_ref)
    (out_ref[0, 0], out_ref[0, 1]), = propagate([pair(first_ref, 0)], patch, kr_ref, ki_ref, tab)


def inner_body(before_ref, patch, mine_ref, first_ref, kr_ref, ki_ref, tab, *refs):
    out_ref, probe_ref = refs[-2:]
    swap = lax.rem(lax.axis_index("frame"), 2) == 1
    for m, (came, given) in enumerate(zip(refs[:-2:2], refs[1:-2:2])):
        other = turned(given[...], *turn_of(before_ref, given.shape[1]))
        probe_ref[1 + m, 0] = jnp.where(swap, other, came[...])
        probe_ref[1 + m, 1] = jnp.where(swap, came[...], other)
    probe_ref[:1] = first_ref[...]
    out_ref[:1] = mine_ref[...]

    def body(group):
        waves = propagate([pair(probe_ref, 1 + m) for m in group], patch, kr_ref, ki_ref, tab)
        for m, wave in zip(group, waves):
            out_ref[1 + m, 0], out_ref[1 + m, 1] = wave

    in_groups(out_ref.shape[0] - 1, body)


def middle_body(rows, before_ref, object_ref, halo_ref, inner_ref, amp_ref, tab, term_ref, half_ref, patch, far, power):
    states = inner_ref.shape[0]
    patch[0], patch[1] = patch_of(object_ref, halo_ref, before_ref)
    power[...] = jnp.zeros_like(power)

    def outward(group):
        waves = forward([times(pair(patch), pair(inner_ref, m)) for m in group], tab)
        total = power[...]
        for m, wave in zip(group, waves):
            far[m, 0], far[m, 1] = wave
            total += wave[0] * wave[0] + wave[1] * wave[1]
        power[...] = total

    in_groups(states, outward)
    power[...] = 1.0 - amp_ref[...] * lax.rsqrt(power[...] + 1.0)
    term_ref[...] = jnp.zeros_like(term_ref)
    take = pl.ds(pl.multiple_of(lax.axis_index("state") * rows, rows), rows)

    def homeward(group):
        waves = [rows_inverse(power[...] * far[m, 0], power[...] * far[m, 1], tab) for m in group]
        for m, wave in zip(group, waves):
            half_ref[m, 0], half_ref[m, 1] = wave
        for m in group:
            wave = columns_inverse(half_ref[m, 0, take], half_ref[m, 1, take], tab)
            part = times_conj((inner_ref[m, 0, take], inner_ref[m, 1, take]), wave)
            term_ref[0] += part[0]
            term_ref[1] += part[1]

    in_groups(states, homeward)


def last_body(rows, half_ref, patch, probe_ref, kr_ref, ki_ref, tab, term_ref, front):
    states = half_ref.shape[0]
    take = pl.ds(pl.multiple_of(lax.axis_index("state") * rows, rows), rows)
    term_ref[...] = jnp.zeros_like(term_ref)

    def body(group):
        waves = [columns_inverse(*pair(half_ref, m), tab) for m in group]
        waves = forward([times_conj(pair(patch), wave) for wave in waves], tab)
        waves = [rows_inverse(*times_conj((kr_ref[...], ki_ref[...]), wave), tab) for wave in waves]
        for m, wave in zip(group, waves):
            front[m, 0], front[m, 1] = wave
        for m in group:
            wave = columns_inverse(front[m, 0, take], front[m, 1, take], tab)
            part = times_conj((probe_ref[m, 0, take], probe_ref[m, 1, take]), wave)
            term_ref[0] += part[0]
            term_ref[1] += part[1]

    in_groups(states, body)


def gather_body(slice_id, rows, pos_ref, before_ref, own_ref, came_ref, other_ref, *refs):
    out_ref, held, sem = refs[-3:]
    odd = lax.rem(lax.axis_index("frame"), 2) == 1
    size = own_ref.shape[-1]
    start = lax.axis_index("state") * rows
    r = lax.broadcasted_iota(jnp.int32, (rows, size), 0) + start
    c = lax.broadcasted_iota(jnp.int32, (rows, size), 1)
    here, there = r < spread(before_ref, 0, r.shape), r >= spread(pos_ref, 0, r.shape)
    here_right, there_right = c < spread(before_ref, 1, c.shape), c < spread(pos_ref, 1, c.shape)
    chunks = 4 if rows % 32 == 0 else 1
    step = rows // chunks
    copies = []
    for chunk in range(chunks):
        at = pl.ds(chunk * step, step)
        cut = slice(chunk * step, chunk * step + step)
        for part in range(2):
            mine = jnp.where(here[cut], own_ref[part, at], 0.0)
            came = came_ref[part, at]
            if slice_id:
                came = jnp.where(odd, came, other_ref[part, at])
            theirs = jnp.where(there[cut], came, 0.0)
            left, right = here_right[cut], there_right[cut]
            held[part, at, :size] = jnp.where(left, 0.0, mine) + jnp.where(right, 0.0, theirs)
            held[part, at, size:] = jnp.where(left, mine, 0.0) + jnp.where(right, theirs, 0.0)
            copies.append(
                pltpu.make_async_copy(held.at[part, at], out_ref.at[slice_id, part, at], sem.at[len(copies)])
            )
            copies[-1].start()
    for copy in copies:
        copy.wait()


def gather(slice_id, rows, size, pos, before, own, came, other, *given):
    return pl.pallas_call(
        functools.partial(gather_body, slice_id, rows),
        out_shape=jax.ShapeDtypeStruct((2, 2, rows, 2 * size), F32),
        in_specs=[VMEM] * 5 + [pl.BlockSpec(memory_space=pl.ANY)] * len(given),
        out_specs=pl.BlockSpec(memory_space=pl.ANY),
        scratch_shapes=[pltpu.VMEM((2, rows, 2 * size), F32), pltpu.SemaphoreType.DMA((8,))],
        input_output_aliases={5: 0} if given else {},
        compiler_params=pltpu.CompilerParams(vmem_limit_bytes=LIMIT),
        cost_estimate=pl.CostEstimate(flops=0, bytes_accessed=32 * rows * size, transcendentals=0),
    )(pos, before, own, came, other, *given)


def on_device(object_slices, probe, amplitude, positions, propagator):
    states = lax.axis_size("state")
    size = amplitude.shape[1]
    rows = object_slices.shape[2] // states
    assert object_slices.shape[2:] == (size, 2 * size) and positions.shape[0] == 1
    assert lax.axis_size("frame") % 2 == 0
    return gradient_of(object_slices, probe, amplitude, positions, propagator, states, size, rows)


def gradient_of(object_slices, probe, amplitude, positions, propagator, states, size, rows):
    grid = (size, size)
    unit = size * size
    flops = 24 * size**3
    tab = tables(size)
    before = shifted(positions, "frame", 1)
    lent = shifted(amplitude, "frame", 1)
    given = [in_hbm(x) for x in (positions, probe, object_slices)]
    pos, plane, held_zero = pl.pallas_call(
        load_body,
        out_shape=[
            jax.ShapeDtypeStruct(positions.shape, jnp.int32),
            jax.ShapeDtypeStruct(grid, F32),
            jax.ShapeDtypeStruct(object_slices.shape[1:], F32),
        ],
        in_specs=[HBM] * 3,
        out_specs=[VMEM] * 3,
        scratch_shapes=[pltpu.SemaphoreType.DMA((6,))],
        compiler_params=pltpu.CompilerParams(vmem_limit_bytes=LIMIT),
        cost_estimate=pl.CostEstimate(flops=0, bytes_accessed=24 * unit, transcendentals=0),
    )(*given)
    planes = []
    for by in range(1, states):
        planes.append(shifted(plane, "state", by))
    (picked,) = call(send_body, [(2,) + grid], [VMEM, VMEM], moved=24 * unit)(pos, held_zero)
    halo_zero = shifted(picked, "frame", 1)
    held_one, picked = call(
        load_send_body,
        [object_slices.shape[1:], (2,) + grid],
        [VMEM, HBM],
        [pltpu.SemaphoreType.DMA((4,))],
        moved=40 * unit,
    )(pos, given[2])
    halo_one = shifted(picked, "frame", 1)
    kr, ki, amp, first, tab = pl.pallas_call(
        prepare_body,
        out_shape=[jax.ShapeDtypeStruct(grid, F32)] * 3
        + [jax.ShapeDtypeStruct(x.shape, x.dtype) for x in (probe, tab)],
        in_specs=[VMEM] * 2 + [HBM] * 3,
        out_specs=[VMEM] * 5,
        scratch_shapes=[pltpu.VMEM(probe.shape, F32), pltpu.VMEM(grid, F32), pltpu.SemaphoreType.DMA((3,))],
        compiler_params=pltpu.CompilerParams(vmem_limit_bytes=LIMIT),
        cost_estimate=pl.CostEstimate(flops=2 * size**3, bytes_accessed=60 * unit, transcendentals=0),
    )(before, lent, given[1], *(in_hbm(x) for x in (propagator, tab)))
    frames = lax.axis_size("frame")
    own = call(turn_body, [grid] * len(planes), [VMEM] * (1 + len(planes)), moved=16 * unit)(before, *planes)
    pairs = []
    for came, kept in zip(planes, own):
        pairs += [kept, lax.ppermute(came, "frame", [(i, i ^ 1) for i in range(frames)])]
    mine, first_patch = call(
        own_body,
        [(1, 2) + grid, (2,) + grid],
        [VMEM] * 7,
        flops=2 * flops,
        moved=24 * unit,
    )(before, held_zero, halo_zero, first, kr, ki, tab)
    waves, probes = call(
        inner_body,
        [(states, 2) + grid] * 2,
        [VMEM] * (7 + len(pairs)),
        flops=2 * flops * (states - 1),
        moved=24 * unit * states,
    )(before, first_patch, mine, first, kr, ki, tab, *pairs)
    term_one, half, patch = call(
        functools.partial(middle_body, rows),
        [(2, rows, size), (states, 2) + grid, (2,) + grid],
        [VMEM] * 6,
        [pltpu.VMEM((states, 2) + grid, F32), pltpu.VMEM(grid, F32)],
        flops=2 * flops * states,
        moved=32 * unit * states,
    )(before, held_one, halo_one, waves, amp, tab)
    came_one = lax.ppermute(term_one, "frame", [(i, (i - 1) % frames) for i in range(0, frames, 2)])
    (term_zero,) = call(
        functools.partial(last_body, rows),
        [(2, rows, size)],
        [VMEM] * 6,
        [pltpu.VMEM((states, 2) + grid, F32)],
        flops=2 * flops * states,
        moved=16 * unit * states,
    )(half, patch, probes, kr, ki, tab)
    came_zero = shifted(term_zero, "frame", -1)
    came_beside = lax.ppermute(term_one, "frame", [(i, i - 1) for i in range(1, frames, 2)])
    gradient = gather(1, rows, size, pos, before, term_one, came_one, came_beside)
    return gather(0, rows, size, pos, before, term_zero, came_zero, pos, gradient)


def solution(mesh):
    return jax.shard_map(
        on_device,
        mesh=mesh,
        in_specs=(
            P(None, None, "frame", None),
            P("state", None, None, None),
            P("frame", None, None),
            P("frame", None),
            P(),
        ),
        out_specs=P(None, None, ("frame", "state"), None),
        check_vma=False,
    )
```

```python
import functools
import math

import jax
import jax.numpy as jnp
import numpy as np
from jax import lax
from jax.experimental import pallas as pl
from jax.experimental.pallas import tpu as pltpu
from jax.sharding import PartitionSpec as P


F32 = jnp.float32
BF16 = jnp.bfloat16
VMEM = pl.BlockSpec(memory_space=pltpu.VMEM)
HBM = pl.BlockSpec(memory_space=pltpu.MemorySpace.HBM)
SMEM = pl.BlockSpec(memory_space=pltpu.SMEM)
LIMIT = 24 * 1024 * 1024


def shifted(value, axis, by):
    count = lax.axis_size(axis)
    return lax.ppermute(value, axis, [(i, (i + by) % count) for i in range(count)])


def in_hbm(value):
    return pltpu.with_memory_space_constraint(value, pltpu.MemorySpace.HBM)


def call(body, outs, ins, scratch=(), flops=0, moved=0):
    return pl.pallas_call(
        body,
        out_shape=[jax.ShapeDtypeStruct(shape, F32) for shape in outs],
        in_specs=ins,
        out_specs=[VMEM] * len(outs),
        scratch_shapes=list(scratch),
        compiler_params=pltpu.CompilerParams(vmem_limit_bytes=LIMIT),
        cost_estimate=pl.CostEstimate(flops=flops, bytes_accessed=moved, transcendentals=0),
    )


def tables(length):
    half = length // 2
    n = np.arange(half)[:, None]
    forms = []
    for parity in (0, 1):
        k = 2 * np.arange(half)[None, :] + parity
        angle = -2.0 * math.pi * ((n * k) % length) / length
        re, im = np.cos(angle) / math.sqrt(length), np.sin(angle) / math.sqrt(length)
        right = np.block([[re, im], [-im, re]])
        forms += [right, right.T]
    stack = np.stack(forms).astype(np.float64)
    top = stack.astype(BF16)
    rest = (stack - top.astype(np.float64)).astype(BF16)
    return jnp.asarray(np.stack([top, rest]))


def halves(value):
    top = value.astype(BF16)
    return top, (value - top.astype(F32)).astype(BF16)


def dot(a, b):
    return lax.dot_general(a, b, (((1,), (0,)), ((), ())), preferred_element_type=F32)


def times_table(value, tab, which):
    top, rest = halves(value)
    return dot(top, tab[0, which]) + (dot(rest, tab[0, which]) + dot(top, tab[1, which]))


def table_times(value, tab, which):
    top, rest = halves(value)
    return dot(tab[0, which], top) + (dot(tab[0, which], rest) + dot(tab[1, which], top))


def columns_forward(re, im, tab):
    h = re.shape[1] // 2
    r0, r1, i0, i1 = re[:, :h], re[:, h:], im[:, :h], im[:, h:]
    even = times_table(jnp.concatenate([r0 + r1, i0 + i1], 1), tab, 0)
    odd = times_table(jnp.concatenate([r0 - r1, i0 - i1], 1), tab, 2)
    return (
        jnp.concatenate([even[:, :h], odd[:, :h]], 1),
        jnp.concatenate([even[:, h:], odd[:, h:]], 1),
    )


def columns_inverse(re, im, tab):
    h = re.shape[1] // 2
    even = times_table(jnp.concatenate([re[:, :h], im[:, :h]], 1), tab, 1)
    odd = times_table(jnp.concatenate([re[:, h:], im[:, h:]], 1), tab, 3)
    total, gap = even + odd, even - odd
    return (
        jnp.concatenate([total[:, :h], gap[:, :h]], 1),
        jnp.concatenate([total[:, h:], gap[:, h:]], 1),
    )


def rows_forward(re, im, tab):
    h = re.shape[0] // 2
    r0, r1, i0, i1 = re[:h], re[h:], im[:h], im[h:]
    even = table_times(jnp.concatenate([r0 + r1, i0 + i1], 0), tab, 1)
    odd = table_times(jnp.concatenate([r0 - r1, i0 - i1], 0), tab, 3)
    return (
        jnp.concatenate([even[:h], odd[:h]], 0),
        jnp.concatenate([even[h:], odd[h:]], 0),
    )


def rows_inverse(re, im, tab):
    h = re.shape[0] // 2
    even = table_times(jnp.concatenate([re[:h], im[:h]], 0), tab, 0)
    odd = table_times(jnp.concatenate([re[h:], im[h:]], 0), tab, 2)
    total, gap = even + odd, even - odd
    return (
        jnp.concatenate([total[:h], gap[:h]], 0),
        jnp.concatenate([total[h:], gap[h:]], 0),
    )


def forward(waves, tab):
    waves = [columns_forward(*wave, tab) for wave in waves]
    return [rows_forward(*wave, tab) for wave in waves]


def inverse(waves, tab):
    waves = [rows_inverse(*wave, tab) for wave in waves]
    return [columns_inverse(*wave, tab) for wave in waves]


def times(a, b):
    return a[0] * b[0] - a[1] * b[1], a[0] * b[1] + a[1] * b[0]


def times_conj(a, b):
    return a[0] * b[0] + a[1] * b[1], a[0] * b[1] - a[1] * b[0]


def in_groups(states, body):
    group = 2 if states % 2 == 0 else 1
    if states == group:
        body([m for m in range(group)])
        return

    def step(g, carry):
        body([g * group + m for m in range(group)])
        return carry

    lax.fori_loop(0, states // group, step, 0)


def thirds(value):
    top = value.astype(BF16)
    left = value - top.astype(F32)
    mid = left.astype(BF16)
    return top, mid, (left - mid.astype(F32)).astype(BF16)


def by_parity(value):
    size = value.shape[0]
    h = size // 2
    picks = []
    for along in (0, 1):
        place = lax.broadcasted_iota(jnp.int32, (size, size), along)
        source = lax.broadcasted_iota(jnp.int32, (size, size), 1 - along)
        wanted = jnp.where(place < h, 2 * place, 2 * (place - h) + 1)
        picks.append(jnp.where(source == wanted, 1.0, 0.0).astype(BF16))
    top, mid, low = thirds(value)
    value = (dot(picks[0], top) + dot(picks[0], mid)) + dot(picks[0], low)
    top, mid, low = thirds(value)
    return (dot(top, picks[1]) + dot(mid, picks[1])) + dot(low, picks[1])


def turned(value, row, col):
    return pltpu.roll(pltpu.roll(value, row, 0), col, 1)


def run_copies(moves, sem):
    copies = [pltpu.make_async_copy(src, dst, sem.at[i]) for i, (src, dst) in enumerate(moves)]
    for copy in copies:
        copy.start()
    return copies


def quarters(object_hbm, s, out):
    half = object_hbm.shape[2] // 2
    return [
        (object_hbm.at[s, part, at], out.at[part, at])
        for part in range(2)
        for at in (pl.ds(0, half), pl.ds(half, half))
    ]


def load_body(pos_hbm, probe_hbm, object_hbm, pos_out, plane_out, object_out, sem):
    which = lax.rem(lax.axis_index("frame"), 2)
    moves = [(probe_hbm.at[0, which], plane_out), (pos_hbm, pos_out)] + quarters(object_hbm, 0, object_out)
    for copy in run_copies(moves, sem):
        copy.wait()


def turn_of(pos_ref, size):
    return jnp.sum(pos_ref[0:1, 0:1]), lax.rem(jnp.sum(pos_ref[0:1, 1:2]), size)


def turn_body(before_ref, *refs):
    half = len(refs) // 2
    turn = turn_of(before_ref, refs[0].shape[1])
    for came, out in zip(refs[:half], refs[half:]):
        out[...] = turned(came[...], *turn)


def prepare_body(
    before_ref, probe_hbm, prop_hbm, amp_hbm, tab_hbm,
    wave_re, wave_im, amp_out, first_out, tab_out,
    probe, prop, amp, sem,
):
    copies = run_copies(((amp_hbm, amp), (probe_hbm, probe), (prop_hbm, prop), (tab_hbm, tab_out)), sem)
    size = prop.shape[0]
    copies[0].wait()
    amp_out[...] = by_parity(amp[0])
    copies[1].wait()
    turn = turn_of(before_ref, size)
    for c in range(2):
        first_out[0, c] = turned(probe[0, c], *turn)
    copies[2].wait()
    phase = by_parity(prop[...])
    wave_re[...] = jnp.cos(phase)
    wave_im[...] = jnp.sin(phase)
    copies[3].wait()


def spread(ref, which, shape):
    return jnp.broadcast_to(ref[0:1, which : which + 1], shape)


def wrapped(ref, part, col_ref):
    size = ref.shape[-2]
    c = lax.broadcasted_iota(jnp.int32, (size, size), 1)
    return jnp.where(c < spread(col_ref, 1, c.shape), ref[part, :, size:], ref[part, :, :size])


def send_body(pos_ref, object_ref, out_ref):
    for part in range(2):
        out_ref[part] = wrapped(object_ref, part, pos_ref)


def load_send_body(pos_ref, object_hbm, object_out, out_ref, sem):
    copies = run_copies(quarters(object_hbm, 1, object_out), sem)
    for copy in copies:
        copy.wait()
    send_body(pos_ref, object_out, out_ref)


def patch_of(object_ref, halo_ref, before_ref):
    size = halo_ref.shape[-1]
    r = lax.broadcasted_iota(jnp.int32, (size, size), 0)
    return [
        jnp.where(r < spread(before_ref, 0, r.shape), wrapped(object_ref, part, before_ref), halo_ref[part])
        for part in range(2)
    ]


def pair(ref, *at):
    return ref[(*at, 0)], ref[(*at, 1)]


def propagate(probes, patch, kr_ref, ki_ref, tab):
    waves = forward([times(probe, pair(patch)) for probe in probes], tab)
    return inverse([times((kr_ref[...], ki_ref[...]), wave) for wave in waves], tab)


def own_body(before_ref, object_ref, halo_ref, first_ref, kr_ref, ki_ref, tab, out_ref, patch):
    patch[0], patch[1] = patch_of(object_ref, halo_ref, before_ref)
    (out_ref[0, 0], out_ref[0, 1]), = propagate([pair(first_ref, 0)], patch, kr_ref, ki_ref, tab)


def inner_body(before_ref, patch, mine_ref, first_ref, kr_ref, ki_ref, tab, *refs):
    out_ref, probe_ref = refs[-2:]
    swap = lax.rem(lax.axis_index("frame"), 2) == 1
    for m, (came, given) in enumerate(zip(refs[:-2:2], refs[1:-2:2])):
        other = turned(given[...], *turn_of(before_ref, given.shape[1]))
        probe_ref[1 + m, 0] = jnp.where(swap, other, came[...])
        probe_ref[1 + m, 1] = jnp.where(swap, came[...], other)
    probe_ref[:1] = first_ref[...]
    out_ref[:1] = mine_ref[...]

    def body(group):
        waves = propagate([pair(probe_ref, 1 + m) for m in group], patch, kr_ref, ki_ref, tab)
        for m, wave in zip(group, waves):
            out_ref[1 + m, 0], out_ref[1 + m, 1] = wave

    in_groups(out_ref.shape[0] - 1, body)


def outward_body(before_ref, object_ref, halo_ref, inner_ref, tab, far, power, patch):
    patch[0], patch[1] = patch_of(object_ref, halo_ref, before_ref)
    power[...] = jnp.zeros_like(power)

    def outward(group):
        waves = forward([times(pair(patch), pair(inner_ref, m)) for m in group], tab)
        total = power[...]
        for m, wave in zip(group, waves):
            far[m, 0], far[m, 1] = wave
            total += wave[0] * wave[0] + wave[1] * wave[1]
        power[...] = total

    in_groups(inner_ref.shape[0], outward)


def middle_body(rows, far, power, inner_ref, amp_ref, tab, term_ref, half_ref, factor):
    factor[...] = 1.0 - amp_ref[...] * lax.rsqrt(power[...] + 1.0)
    term_ref[...] = jnp.zeros_like(term_ref)
    take = pl.ds(pl.multiple_of(lax.axis_index("state") * rows, rows), rows)

    def homeward(group):
        waves = [rows_inverse(factor[...] * far[m, 0], factor[...] * far[m, 1], tab) for m in group]
        for m, wave in zip(group, waves):
            half_ref[m, 0], half_ref[m, 1] = wave
        for m in group:
            wave = columns_inverse(half_ref[m, 0, take], half_ref[m, 1, take], tab)
            part = times_conj((inner_ref[m, 0, take], inner_ref[m, 1, take]), wave)
            term_ref[0] += part[0]
            term_ref[1] += part[1]

    in_groups(inner_ref.shape[0], homeward)


def last_body(rows, half_ref, patch, probe_ref, kr_ref, ki_ref, tab, term_ref, front):
    states = half_ref.shape[0]
    take = pl.ds(pl.multiple_of(lax.axis_index("state") * rows, rows), rows)
    term_ref[...] = jnp.zeros_like(term_ref)

    def body(group):
        waves = [columns_inverse(*pair(half_ref, m), tab) for m in group]
        waves = forward([times_conj(pair(patch), wave) for wave in waves], tab)
        waves = [rows_inverse(*times_conj((kr_ref[...], ki_ref[...]), wave), tab) for wave in waves]
        for m, wave in zip(group, waves):
            front[m, 0], front[m, 1] = wave
        for m in group:
            wave = columns_inverse(front[m, 0, take], front[m, 1, take], tab)
            part = times_conj((probe_ref[m, 0, take], probe_ref[m, 1, take]), wave)
            term_ref[0] += part[0]
            term_ref[1] += part[1]

    in_groups(states, body)


def gather_body(slice_id, rows, pos_ref, before_ref, own_ref, came_ref, *refs):
    out_ref, held, sem = refs[-3:]
    size = own_ref.shape[-1]
    start = lax.axis_index("state") * rows
    r = lax.broadcasted_iota(jnp.int32, (rows, size), 0) + start
    c = lax.broadcasted_iota(jnp.int32, (rows, size), 1)
    here, there = r < spread(before_ref, 0, r.shape), r >= spread(pos_ref, 0, r.shape)
    here_right, there_right = c < spread(before_ref, 1, c.shape), c < spread(pos_ref, 1, c.shape)
    chunks = 4 if rows % 32 == 0 else 1
    step = rows // chunks
    copies = []
    for chunk in range(chunks):
        at = pl.ds(chunk * step, step)
        cut = slice(chunk * step, chunk * step + step)
        for part in range(2):
            mine = jnp.where(here[cut], own_ref[part, at], 0.0)
            theirs = jnp.where(there[cut], came_ref[part, at], 0.0)
            left, right = here_right[cut], there_right[cut]
            held[part, at, :size] = jnp.where(left, 0.0, mine) + jnp.where(right, 0.0, theirs)
            held[part, at, size:] = jnp.where(left, mine, 0.0) + jnp.where(right, theirs, 0.0)
            copies.append(
                pltpu.make_async_copy(held.at[part, at], out_ref.at[slice_id, part, at], sem.at[len(copies)])
            )
            copies[-1].start()
    for copy in copies:
        copy.wait()


def gather(slice_id, rows, size, pos, before, own, came, *given):
    return pl.pallas_call(
        functools.partial(gather_body, slice_id, rows),
        out_shape=jax.ShapeDtypeStruct((2, 2, rows, 2 * size), F32),
        in_specs=[VMEM] * 4 + [pl.BlockSpec(memory_space=pl.ANY)] * len(given),
        out_specs=pl.BlockSpec(memory_space=pl.ANY),
        scratch_shapes=[pltpu.VMEM((2, rows, 2 * size), F32), pltpu.SemaphoreType.DMA((8,))],
        input_output_aliases={4: 0} if given else {},
        compiler_params=pltpu.CompilerParams(vmem_limit_bytes=LIMIT),
        cost_estimate=pl.CostEstimate(flops=0, bytes_accessed=32 * rows * size, transcendentals=0),
    )(pos, before, own, came, *given)


def on_device(object_slices, probe, amplitude, positions, propagator):
    states = lax.axis_size("state")
    size = amplitude.shape[1]
    rows = object_slices.shape[2] // states
    assert object_slices.shape[2:] == (size, 2 * size) and positions.shape[0] == 1
    assert lax.axis_size("frame") % 2 == 0
    return gradient_of(object_slices, probe, amplitude, positions, propagator, states, size, rows)


def gradient_of(object_slices, probe, amplitude, positions, propagator, states, size, rows):
    grid = (size, size)
    unit = size * size
    flops = 24 * size**3
    tab = tables(size)
    before = shifted(positions, "frame", 1)
    given = [in_hbm(x) for x in (positions, probe, object_slices)]
    pos, plane, held_zero = pl.pallas_call(
        load_body,
        out_shape=[
            jax.ShapeDtypeStruct(positions.shape, jnp.int32),
            jax.ShapeDtypeStruct(grid, F32),
            jax.ShapeDtypeStruct(object_slices.shape[1:], F32),
        ],
        in_specs=[HBM] * 3,
        out_specs=[VMEM] * 3,
        scratch_shapes=[pltpu.SemaphoreType.DMA((6,))],
        compiler_params=pltpu.CompilerParams(vmem_limit_bytes=LIMIT),
        cost_estimate=pl.CostEstimate(flops=0, bytes_accessed=24 * unit, transcendentals=0),
    )(*given)
    planes = []
    for by in range(1, states):
        planes.append(shifted(plane, "state", by))
    (picked,) = call(send_body, [(2,) + grid], [VMEM, VMEM], moved=24 * unit)(pos, held_zero)
    halo_zero = shifted(picked, "frame", 1)
    held_one, picked = call(
        load_send_body,
        [object_slices.shape[1:], (2,) + grid],
        [VMEM, HBM],
        [pltpu.SemaphoreType.DMA((4,))],
        moved=40 * unit,
    )(pos, given[2])
    halo_one = shifted(picked, "frame", 1)
    kr, ki, amp, first, tab = pl.pallas_call(
        prepare_body,
        out_shape=[jax.ShapeDtypeStruct(grid, F32)] * 3
        + [jax.ShapeDtypeStruct(x.shape, x.dtype) for x in (probe, tab)],
        in_specs=[VMEM] + [HBM] * 4,
        out_specs=[VMEM] * 5,
        scratch_shapes=[
            pltpu.VMEM(probe.shape, F32),
            pltpu.VMEM(grid, F32),
            pltpu.VMEM(amplitude.shape, F32),
            pltpu.SemaphoreType.DMA((4,)),
        ],
        compiler_params=pltpu.CompilerParams(vmem_limit_bytes=LIMIT),
        cost_estimate=pl.CostEstimate(flops=2 * size**3, bytes_accessed=60 * unit, transcendentals=0),
    )(before, given[1], *(in_hbm(x) for x in (propagator, amplitude, tab)))
    amp = shifted(amp, "frame", 1)
    frames = lax.axis_size("frame")
    own = call(turn_body, [grid] * len(planes), [VMEM] * (1 + len(planes)), moved=16 * unit)(before, *planes)
    pairs = []
    for came, kept in zip(planes, own):
        pairs += [kept, lax.ppermute(came, "frame", [(i, i ^ 1) for i in range(frames)])]
    mine, first_patch = call(
        own_body,
        [(1, 2) + grid, (2,) + grid],
        [VMEM] * 7,
        flops=2 * flops,
        moved=24 * unit,
    )(before, held_zero, halo_zero, first, kr, ki, tab)
    waves, probes = call(
        inner_body,
        [(states, 2) + grid] * 2,
        [VMEM] * (7 + len(pairs)),
        flops=2 * flops * (states - 1),
        moved=24 * unit * states,
    )(before, first_patch, mine, first, kr, ki, tab, *pairs)
    far, power, patch = call(
        outward_body,
        [(states, 2) + grid, grid, (2,) + grid],
        [VMEM] * 5,
        flops=flops * states,
        moved=32 * unit * states,
    )(before, held_one, halo_one, waves, tab)
    term_one, half = call(
        functools.partial(middle_body, rows),
        [(2, rows, size), (states, 2) + grid],
        [VMEM] * 5,
        [pltpu.VMEM(grid, F32)],
        flops=flops * states,
        moved=32 * unit * states,
    )(far, power, waves, amp, tab)
    came_one = shifted(term_one, "frame", -1)
    (term_zero,) = call(
        functools.partial(last_body, rows),
        [(2, rows, size)],
        [VMEM] * 6,
        [pltpu.VMEM((states, 2) + grid, F32)],
        flops=2 * flops * states,
        moved=16 * unit * states,
    )(half, patch, probes, kr, ki, tab)
    came_zero = shifted(term_zero, "frame", -1)
    gradient = gather(1, rows, size, pos, before, term_one, came_one)
    return gather(0, rows, size, pos, before, term_zero, came_zero, gradient)


def solution(mesh):
    return jax.shard_map(
        on_device,
        mesh=mesh,
        in_specs=(
            P(None, None, "frame", None),
            P("state", None, None, None),
            P("frame", None, None),
            P("frame", None),
            P(),
        ),
        out_specs=P(None, None, ("frame", "state"), None),
        check_vma=False,
    )
```
